256 devices in a mesh: seq: 32 (over z_hi, y, core), tp: 8 (over z_lo, x).
Axes of the slice: x: 4, y: 4, z: 8 (z_hi: 4, z_lo: 2; z = z_hi * 2 + z_lo), core: 2. Of those that a mesh axis runs over, the one named last changes fastest.
Arguments:
- pixels: bfloat16 [64, 256, 1664], P('seq', 'tp'), may hold values from -6 to 6
- text_rows: bfloat16 [16384, 1664], P(('seq', 'tp')), may hold values from -6 to 6
- patch_counts: int32 [64], replicated, may hold values from 4 to 256, as said below
- picture_starts: int32 [64], replicated, may hold values from 0 to 16320, as said below
- block_lengths: int32 [32], replicated, may hold values from 256 to 512
- vision_gain: float32 [1664], replicated, may hold values from 0.25 to 1.75
- vision_project: bfloat16 [1664, 3, 1664], P(None, None, 'tp')
- vision_output: bfloat16 [1664, 1664], P('tp'), may hold values from -0.15625 to 0.15625
- merge_gain: float32 [1664], replicated, may hold values from 0.25 to 1.75
- merge_weight: bfloat16 [6656, 1664], P('tp'), may hold values from -0.078125 to 0.078125
- text_gain: float32 [1664], replicated, may hold values from 0.25 to 1.75
- text_project: bfloat16 [1664, 3, 1664], P(None, None, 'tp')
- text_output: bfloat16 [1664, 1664], P('tp'), may hold values from -0.15625 to 0.15625
Outputs:
- hidden: bfloat16 [16384, 1664], P(('seq', 'tp'))
- key_cache: bfloat16 [16384, 1664], P('seq', 'tp')
- value_cache: bfloat16 [16384, 1664], P('seq', 'tp')
The draws below stay inside these ranges and needn't reach their ends.
Inputs may be any that keep to these rules, and one draw needn't show every extreme that they name: `patch_counts`: every count is a multiple of 4. Picture p's merged tokens take positions picture_starts[p] to picture_starts[p] + 63 inside one block of 512 positions, and these ranges of different pictures are disjoint; every block holds exactly one picture of each rank k < 2, rank k meaning the pictures s * 2 + k; the pictures of one index of seq lie in different blocks.
All inputs are finite; a program needn't handle non-finite values.
Results may differ from the reference program's by a relative error of at most 0.034.
The reference program's roundings to bfloat16 on the way count: a program that leaves them out, or rounds other values in their place, can miss the bound.
Values may be sent and summed in bfloat16 or wider, within the bound.
A program may use at most 128 MiB of HBM per device.

```python
import math
import jax
import jax.numpy as jnp
from jax import lax

D = 1664
HEADS = 16
HEAD = 104
PATCH = 256
PICS_DEV = 2
TOK_DEV = 512
MERGED = 64
PICS = 64
BLOCKS = 32
TOKENS = 16384
SLOT = 256


def projection_draw(base_key):
    subkeys = jax.random.split(base_key, 1)
    base_scale = (3.0 / D) ** 0.5
    base_draw = jnp.clip(jax.random.normal(subkeys[0], (D, 3, D), jnp.float32), -5.0, 5.0) * base_scale
    return base_draw.astype(jnp.bfloat16)


def draw_vision_project(key, part):
    return projection_draw(jax.random.fold_in(key, 11))


def draw_text_project(key, part):
    return projection_draw(jax.random.fold_in(key, 23))


def draw_patch_counts(key, part):
    subkeys = jax.random.split(jax.random.fold_in(key, 41), 3)
    groups_drawn = jax.random.randint(subkeys[0], (PICS,), 1, PATCH // 4 + 1)
    fullest = jax.random.randint(subkeys[1], (), 0, PICS)
    smallest = (fullest + 1 + jax.random.randint(subkeys[2], (), 0, PICS - 1)) % PICS
    picture_index = jnp.arange(PICS)
    groups_drawn = jnp.where(picture_index == fullest, PATCH // 4, groups_drawn)
    groups_drawn = jnp.where(picture_index == smallest, 1, groups_drawn)
    return (4 * groups_drawn).astype(jnp.int32)


def draw_picture_starts(key, part):
    subkeys = jax.random.split(jax.random.fold_in(key, 37), 5)
    spread = jax.random.permutation(subkeys[0], BLOCKS)
    ordering = jax.random.permutation(subkeys[1], BLOCKS)
    shifts = jax.random.permutation(subkeys[2], BLOCKS)[:PICS_DEV]
    destinations = spread[(ordering[:, None] + shifts[None, :]) % BLOCKS]
    rotations = jax.random.randint(subkeys[3], (BLOCKS,), 0, PICS_DEV)
    slot_index = (jnp.arange(PICS_DEV)[None, :] + rotations[destinations]) % PICS_DEV
    offsets = jax.random.randint(subkeys[4], (BLOCKS, PICS_DEV), 0, SLOT - MERGED + 1)
    offsets = jnp.where((destinations == BLOCKS - 1) & (slot_index == PICS_DEV - 1), SLOT - MERGED, offsets)
    offsets = jnp.where((destinations == 0) & (slot_index == 0), 0, offsets)
    return (destinations * TOK_DEV + slot_index * SLOT + offsets).reshape(PICS).astype(jnp.int32)


def draw_block_lengths(key, part):
    subkeys = jax.random.split(jax.random.fold_in(key, 53), 3)
    lengths = jax.random.randint(subkeys[0], (BLOCKS,), TOK_DEV // 2, TOK_DEV + 1)
    longest = jax.random.randint(subkeys[1], (), 0, BLOCKS)
    shortest = (longest + 1 + jax.random.randint(subkeys[2], (), 0, BLOCKS - 1)) % BLOCKS
    block_index = jnp.arange(BLOCKS)
    lengths = jnp.where(block_index == longest, TOK_DEV, lengths)
    lengths = jnp.where(block_index == shortest, TOK_DEV // 2, lengths)
    return lengths.astype(jnp.int32)


def block_levels(rng, extent, shards, low, high):
    def one(axis_at, blocks):
        steps = jax.random.uniform(jax.random.fold_in(jax.random.fold_in(rng, 6), axis_at), (blocks,), jnp.float32, low / len(shards), high / len(shards))
        return jnp.repeat(jnp.exp(steps), extent[axis_at] // blocks).reshape((-1,) + (1,) * (len(extent) - axis_at - 1))

    gain = one(*shards[0])
    for cut in shards[1:]:
        gain = gain * one(*cut)
    return gain


def noise(stream_key, shape, scale, reach, shards=(), held_as=jnp.bfloat16):
    array = jax.random.normal(stream_key, shape, jnp.float32) * scale
    if len(shards) > 0:
        array = block_levels(stream_key, shape, shards, -0.22, 0.18) * array
    return jnp.clip(array, min=-reach, max=reach).astype(held_as)


def setup_inputs(seed: int = 0) -> dict:
    key_list = jax.random.split(jax.random.key(seed), 14)
    return {
        "pixels": noise(key_list[0], (PICS, PATCH, D), 1.0, 6.0, ((0, 32), (1, 8))),
        "text_rows": noise(key_list[1], (TOKENS, D), 1.0, 6.0, ((0, 256),)),
        "patch_counts": draw_patch_counts(jax.random.fold_in(key_list[13], 71), 0),
        "picture_starts": draw_picture_starts(jax.random.fold_in(key_list[13], 71), 0),
        "block_lengths": draw_block_lengths(jax.random.fold_in(key_list[13], 71), 0),
        "vision_gain": jnp.clip(1.0 + 0.15 * jax.random.normal(key_list[5], (D,), jnp.float32), 0.25, 1.75),
        "vision_project": draw_vision_project(jax.random.fold_in(key_list[13], 71), 0),
        "vision_output": noise(key_list[7], (D, D), D ** -0.5, 0.15625, ((0, 8),)),
        "merge_gain": jnp.clip(1.0 + 0.15 * jax.random.normal(key_list[8], (D,), jnp.float32), 0.25, 1.75),
        "merge_weight": noise(key_list[9], (4 * D, D), (4 * D) ** -0.5, 0.078125, ((0, 8),)),
        "text_gain": jnp.clip(1.0 + 0.15 * jax.random.normal(key_list[10], (D,), jnp.float32), 0.25, 1.75),
        "text_project": draw_text_project(jax.random.fold_in(key_list[13], 71), 0),
        "text_output": noise(key_list[12], (D, D), D ** -0.5, 0.15625, ((0, 8),)),
    }


LN_EPS = 1e-05
RMS_EPS = 1e-06
MASKED_SCORE = -1e+30

def layer_normed(row_values, gain_vector):
    floats = row_values.astype(jnp.float32)
    centre = floats - lax.optimization_barrier(jnp.mean(floats, -1, keepdims=True))
    spread = lax.optimization_barrier(jnp.mean(centre * centre, -1, keepdims=True))
    return centre * lax.rsqrt(spread + LN_EPS) * gain_vector

def rms_normed(row_values, gain_vector):
    floats = row_values.astype(jnp.float32)
    return floats * lax.rsqrt(lax.optimization_barrier(jnp.mean(floats * floats, -1, keepdims=True)) + RMS_EPS) * gain_vector

def rotary(heads_in, positions):
    halfway = heads_in.shape[-1] // 2
    rates = 10000.0 ** (-2.0 * jnp.arange(halfway, dtype=jnp.float32) / heads_in.shape[-1])
    angles = positions.astype(jnp.float32)[:, None] * rates[None, :]
    cosine_table = jnp.cos(angles)[:, None, :]
    sine_table = jnp.sin(angles)[:, None, :]
    leading = heads_in[..., :halfway]
    trailing = heads_in[..., halfway:]
    return jnp.concatenate([leading * cosine_table - trailing * sine_table, trailing * cosine_table + leading * sine_table], -1)

def reference(pixels, text_rows, patch_counts, picture_starts, block_lengths, vision_gain, vision_project, vision_output, merge_gain, merge_weight, text_gain, text_project, text_output):
    score_scale = 1.0 / math.sqrt(HEAD)

    def vision_picture(packed):
        pixels_one, live_count = packed
        normed = layer_normed(pixels_one, vision_gain).astype(jnp.bfloat16)
        projected = jnp.dot(normed, vision_project.reshape(D, 3 * D), preferred_element_type=jnp.float32).astype(jnp.bfloat16)
        projected = lax.optimization_barrier(projected).astype(jnp.float32)
        queries = projected[:, :D].reshape(PATCH, HEADS, HEAD)
        key_heads = projected[:, D:2 * D].reshape(PATCH, HEADS, HEAD)
        value_heads = projected[:, 2 * D:].reshape(PATCH, HEADS, HEAD)
        scores = jnp.einsum('qhd,khd->hqk', queries, key_heads) * score_scale
        allowed = (jnp.arange(PATCH, dtype=jnp.int32) < live_count)[None, None, :]
        scores = jnp.where(allowed, scores, MASKED_SCORE)
        highest = lax.optimization_barrier(jnp.max(scores, -1, keepdims=True))
        weights = jnp.where(allowed, jnp.exp(scores - highest), 0.0)
        rounded = lax.optimization_barrier(weights.astype(jnp.bfloat16)).astype(jnp.float32)
        mixture = jnp.einsum('hqk,khd->qhd', rounded, value_heads)
        mixture = mixture / jnp.transpose(lax.optimization_barrier(jnp.sum(weights, -1)))[:, :, None]
        attended = mixture.reshape(PATCH, D).astype(jnp.bfloat16)
        vision_rows = (pixels_one.astype(jnp.float32) + jnp.dot(attended, vision_output, preferred_element_type=jnp.float32)).astype(jnp.bfloat16)
        merge_input = layer_normed(vision_rows, merge_gain).astype(jnp.bfloat16)
        return jnp.dot(merge_input.reshape(MERGED, 4 * D), merge_weight, preferred_element_type=jnp.float32).astype(jnp.bfloat16)
    visual = lax.map(vision_picture, (pixels, patch_counts))
    slot_index = jnp.arange(MERGED, dtype=jnp.int32)
    target = picture_starts[:, None] + slot_index[None, :]
    target = jnp.where(slot_index[None, :] < (patch_counts // 4)[:, None], target, TOKENS).reshape(-1)
    embedded = text_rows.at[target].set(visual.reshape(PICS * MERGED, D), mode='drop')
    text_normed = rms_normed(embedded, text_gain).astype(jnp.bfloat16)
    projected = jnp.dot(text_normed, text_project.reshape(D, 3 * D), preferred_element_type=jnp.float32)
    positions = jnp.arange(TOKENS, dtype=jnp.int32)
    query_rows = rotary(projected[:, :D].reshape(TOKENS, HEADS, HEAD), positions).astype(jnp.bfloat16)
    key_cache = rotary(projected[:, D:2 * D].reshape(TOKENS, HEADS, HEAD), positions).astype(jnp.bfloat16)
    value_cache = projected[:, 2 * D:].astype(jnp.bfloat16).reshape(TOKENS, HEADS, HEAD)
    query_float = lax.optimization_barrier(query_rows).astype(jnp.float32)
    key_float = lax.optimization_barrier(key_cache).astype(jnp.float32)
    value_float = lax.optimization_barrier(value_cache).astype(jnp.float32)
    key_index = positions % TOK_DEV
    key_usable = key_index < block_lengths[positions // TOK_DEV]

    def attend_block(block_index):
        first_row = block_index * TOK_DEV
        block_query = lax.dynamic_slice_in_dim(query_float, first_row, TOK_DEV, 0)
        row_positions = first_row + jnp.arange(TOK_DEV, dtype=jnp.int32)
        scores = jnp.einsum('qhd,khd->hqk', block_query, key_float) * score_scale
        allowed = ((positions[None, :] <= row_positions[:, None]) & key_usable[None, :])[None]
        scores = jnp.where(allowed, scores, MASKED_SCORE)
        highest = lax.optimization_barrier(jnp.max(scores, -1, keepdims=True))
        weights = jnp.where(allowed, jnp.exp(scores - highest), 0.0)
        rounded = lax.optimization_barrier(weights.astype(jnp.bfloat16)).astype(jnp.float32)
        mixture = jnp.einsum('hqk,khd->qhd', rounded, value_float)
        mixture = mixture / jnp.transpose(lax.optimization_barrier(jnp.sum(weights, -1)))[:, :, None]
        return mixture.reshape(TOK_DEV, D).astype(jnp.bfloat16)
    attended = lax.map(attend_block, jnp.arange(BLOCKS, dtype=jnp.int32)).reshape(TOKENS, D)
    hidden = (embedded.astype(jnp.float32) + jnp.dot(attended, text_output, preferred_element_type=jnp.float32)).astype(jnp.bfloat16)
    return (hidden, key_cache.reshape(TOKENS, D), value_cache.reshape(TOKENS, D))
```

```python
import math

import jax
import jax.numpy as jnp
from jax import lax
from jax.experimental import pallas as pl
from jax.experimental.pallas import tpu as pltpu
from jax.sharding import PartitionSpec as P

HEAD = 104


LN_EPS = 1e-05
RMS_EPS = 1e-06
MASKED_SCORE = -1e30
KEY_SPAN = 512


def layer_normed(row_values, gain_vector):
    floats = row_values.astype(jnp.float32)
    centre = floats - jnp.mean(floats, -1, keepdims=True)
    spread = jnp.mean(centre * centre, -1, keepdims=True)
    return centre * lax.rsqrt(spread + LN_EPS) * gain_vector


def rms_normed(row_values, gain_vector):
    floats = row_values.astype(jnp.float32)
    return floats * lax.rsqrt(jnp.mean(floats * floats, -1, keepdims=True) + RMS_EPS) * gain_vector


def rotary(heads_in, positions):
    halfway = heads_in.shape[-1] // 2
    rates = 10000.0 ** (-2.0 * jnp.arange(halfway, dtype=jnp.float32) / heads_in.shape[-1])
    angles = positions.astype(jnp.float32)[:, None] * rates[None, :]
    cosine_table = jnp.cos(angles)[:, None, :]
    sine_table = jnp.sin(angles)[:, None, :]
    leading = heads_in[..., :halfway]
    trailing = heads_in[..., halfway:]
    return jnp.concatenate(
        [
            leading * cosine_table - trailing * sine_table,
            trailing * cosine_table + leading * sine_table,
        ],
        -1,
    )


def summed_rows(term_task, own_rows):
    return lax.psum_scatter(
        term_task(jnp.int32(0), own_rows * lax.axis_size("tp")),
        "tp",
        scatter_dimension=0,
        tiled=True,
    )


def attention_kernel(meta_ref, lengths_ref, q_ref, k_ref, v_ref, o_ref, m_sc, l_sc, acc_sc):
    step = pl.program_id(0)
    seq = meta_ref[0]
    rows, width = q_ref.shape
    span = k_ref.shape[0]
    heads = width // HEAD
    score_scale = 1.0 / math.sqrt(HEAD)

    @pl.when(step == 0)
    def _():
        m_sc[...] = jnp.full(m_sc.shape, MASKED_SCORE, jnp.float32)
        l_sc[...] = jnp.zeros(l_sc.shape, jnp.float32)
        acc_sc[...] = jnp.zeros(acc_sc.shape, jnp.float32)

    @pl.when(step <= seq)
    def _():
        q = q_ref[...]
        k = k_ref[...]
        v = v_ref[...]
        column = lax.broadcasted_iota(jnp.int32, (rows, width), 1)
        query_pos = seq * rows + lax.broadcasted_iota(jnp.int32, (rows, span), 0)
        key_index = lax.broadcasted_iota(jnp.int32, (rows, span), 1)
        allowed = (step * span + key_index <= query_pos) & (key_index < lengths_ref[step])
        for h in range(heads):
            in_head = (column >= h * HEAD) & (column < (h + 1) * HEAD)
            q_head = jnp.where(in_head, q, jnp.zeros_like(q))
            scores = (
                lax.dot_general(
                    q_head, k, (((1,), (1,)), ((), ())), preferred_element_type=jnp.float32
                )
                * score_scale
            )
            scores = jnp.where(allowed, scores, MASKED_SCORE)
            m_prev = m_sc[h][:, :1]
            m_new = jnp.maximum(m_prev, jnp.max(scores, axis=1, keepdims=True))
            weights = jnp.where(allowed, jnp.exp(scores - m_new), 0.0)
            alpha = jnp.exp(m_prev - m_new)
            l_new = alpha * l_sc[h][:, :1] + jnp.sum(weights, axis=1, keepdims=True)
            mixed = jnp.dot(weights.astype(jnp.bfloat16), v, preferred_element_type=jnp.float32)
            acc_sc[h] = acc_sc[h] * alpha + mixed
            m_sc[h] = jnp.broadcast_to(m_new, m_sc.shape[1:])
            l_sc[h] = jnp.broadcast_to(l_new, l_sc.shape[1:])

    @pl.when(step == pl.num_programs(0) - 1)
    def _():
        column = lax.broadcasted_iota(jnp.int32, (rows, width), 1)
        result = jnp.zeros((rows, width), jnp.float32)
        for h in range(heads):
            in_head = (column >= h * HEAD) & (column < (h + 1) * HEAD)
            result = jnp.where(in_head, acc_sc[h] / l_sc[h][:, :1], result)
        o_ref[...] = result.astype(o_ref.dtype)


def causal_attention(query_flat, key_all, value_all, seq_index, block_lengths, rows_per_block):
    rows, width = query_flat.shape
    span = rows_per_block
    steps = key_all.shape[0] // span
    heads = width // HEAD
    meta = jnp.reshape(seq_index, (1,)).astype(jnp.int32)
    grid_spec = pltpu.PrefetchScalarGridSpec(
        num_scalar_prefetch=2,
        grid=(steps,),
        in_specs=[
            pl.BlockSpec((rows, width), lambda i, m, n: (0, 0)),
            pl.BlockSpec((span, width), lambda i, m, n: (jnp.minimum(i, m[0]), 0)),
            pl.BlockSpec((span, width), lambda i, m, n: (jnp.minimum(i, m[0]), 0)),
        ],
        out_specs=pl.BlockSpec((rows, width), lambda i, m, n: (0, 0)),
        scratch_shapes=[
            pltpu.VMEM((heads, rows, 128), jnp.float32),
            pltpu.VMEM((heads, rows, 128), jnp.float32),
            pltpu.VMEM((heads, rows, width), jnp.float32),
        ],
    )
    flops = 4 * heads * rows * key_all.shape[0] * width
    return pl.pallas_call(
        attention_kernel,
        grid_spec=grid_spec,
        out_shape=jax.ShapeDtypeStruct((rows, width), jnp.bfloat16),
        compiler_params=pltpu.CompilerParams(dimension_semantics=("arbitrary",)),
        cost_estimate=pl.CostEstimate(
            flops=flops,
            transcendentals=heads * rows * key_all.shape[0],
            bytes_accessed=2 * key_all.size * 2 + 2 * query_flat.size * 2,
        ),
    )(meta, block_lengths, query_flat, key_all, value_all)


def shards(
    pixels,
    text_rows,
    patch_counts,
    picture_starts,
    block_lengths,
    vision_gain,
    vision_project,
    vision_output,
    merge_gain,
    merge_weight,
    text_gain,
    text_project,
    text_output,
):
    seq_ways = lax.axis_size("seq")
    tp_ways = lax.axis_size("tp")
    seq_index = lax.axis_index("seq")
    tp_index = lax.axis_index("tp")
    picture_total, local_patches, model_width = pixels.shape
    patch_total = local_patches * tp_ways
    local_width = vision_project.shape[2]
    head_count = local_width // HEAD
    patch_normed = layer_normed(pixels, vision_gain).astype(jnp.bfloat16)
    packed_project = vision_project.reshape(model_width, 3 * local_width)
    projected = jnp.einsum(
        "npd,de->npe",
        lax.all_gather(patch_normed, "tp", axis=1, tiled=True),
        packed_project,
        preferred_element_type=jnp.float32,
    ).astype(jnp.bfloat16)
    queries = projected[..., :local_width].reshape(picture_total, patch_total, head_count, HEAD)
    key_heads = projected[..., local_width : 2 * local_width].reshape(
        picture_total, patch_total, head_count, HEAD
    )
    value_heads = projected[..., 2 * local_width :].reshape(
        picture_total, patch_total, head_count, HEAD
    )
    live_counts = lax.dynamic_slice_in_dim(
        patch_counts, seq_index * picture_total, picture_total, 0
    )
    score_scale = 1.0 / math.sqrt(HEAD)
    scores = (
        jnp.einsum("nqhd,nkhd->nhqk", queries, key_heads, preferred_element_type=jnp.float32)
        * score_scale
    )
    allowed = (jnp.arange(patch_total, dtype=jnp.int32)[None, :] < live_counts[:, None])[
        :, None, None, :
    ]
    scores = jnp.where(allowed, scores, MASKED_SCORE)
    highest = jnp.max(scores, -1, keepdims=True)
    weights = jnp.where(allowed, jnp.exp(scores - highest), 0.0)
    mixture = jnp.einsum(
        "nhqk,nkhd->nqhd",
        weights.astype(jnp.bfloat16),
        value_heads,
        preferred_element_type=jnp.float32,
    )
    mixture = mixture / jnp.transpose(jnp.sum(weights, -1), (0, 2, 1))[..., None]
    attended = mixture.astype(jnp.bfloat16).reshape(picture_total, patch_total, local_width)
    patch_major = jnp.transpose(attended, (1, 0, 2)).reshape(
        patch_total * picture_total, local_width
    )

    def vision_term(offset, row_count):
        return jnp.dot(patch_major, vision_output, preferred_element_type=jnp.float32)

    vision_sum = summed_rows(vision_term, local_patches * picture_total)
    vision_sum = jnp.transpose(
        vision_sum.reshape(local_patches, picture_total, model_width), (1, 0, 2)
    )
    vision_rows = (pixels.astype(jnp.float32) + vision_sum).astype(jnp.bfloat16)
    merge_input = layer_normed(vision_rows, merge_gain).astype(jnp.bfloat16)
    merged_total = patch_total // 4
    input_share = merge_weight.shape[0]
    whole_pictures = lax.all_gather(merge_input, "tp", axis=1, tiled=True)
    merged_rows = whole_pictures.reshape(picture_total * merged_total, 4 * model_width)
    owned_inputs = lax.dynamic_slice_in_dim(merged_rows, tp_index * input_share, input_share, 1)

    def merge_term(offset, row_count):
        return jnp.dot(owned_inputs, merge_weight, preferred_element_type=jnp.float32)

    part_rows = picture_total * merged_total // tp_ways
    visual_part = summed_rows(merge_term, part_rows).astype(jnp.bfloat16)
    rows_per_block = text_rows.shape[0] * tp_ways
    start_table = picture_starts.reshape(seq_ways, picture_total)
    dest_table = start_table // rows_per_block
    picture_rank = tp_index * part_rows // merged_total
    rank_dest = jnp.sum(
        jnp.where(
            jnp.arange(picture_total, dtype=jnp.int32)[None, :] == picture_rank, dest_table, 0
        ),
        1,
    )
    senders = rank_dest == seq_index
    segment = lax.all_gather(visual_part, "seq", axis=0, tiled=True)
    row_count = segment.shape[0]
    sources = jnp.arange(row_count, dtype=jnp.int32) // part_rows
    wanted = jnp.any(
        (sources[:, None] == jnp.arange(seq_ways, dtype=jnp.int32)[None, :]) & senders[None, :], 1
    )
    selector = (
        (jnp.arange(row_count, dtype=jnp.int32) % part_rows)[None, :]
        == jnp.arange(part_rows, dtype=jnp.int32)[:, None]
    ) & wanted[None, :]
    arrived = jnp.dot(
        selector.astype(jnp.bfloat16), segment, preferred_element_type=jnp.float32
    ).astype(jnp.bfloat16)
    text_block, visual_block = (
        lax.all_gather(text_rows, "tp", axis=0, tiled=True),
        lax.all_gather(arrived, "tp", axis=0, tiled=True),
    )
    landed = dest_table == seq_index
    local_starts = jnp.sum(jnp.where(landed, start_table - seq_index * rows_per_block, 0), 0)
    live_groups = jnp.sum(
        jnp.where(landed, patch_counts.reshape(seq_ways, picture_total) // 4, 0), 0
    )
    slot_index = jnp.arange(merged_total, dtype=jnp.int32)
    targets = (local_starts[:, None] + slot_index[None, :]).reshape(-1)
    in_use = (slot_index[None, :] < live_groups[:, None]).reshape(-1)
    placement = (jnp.arange(rows_per_block, dtype=jnp.int32)[:, None] == targets[None, :]) & in_use[
        None, :
    ]
    covered = jnp.any(placement, 1)
    placed = jnp.dot(
        placement.astype(jnp.bfloat16), visual_block, preferred_element_type=jnp.float32
    ).astype(jnp.bfloat16)
    embedded = jnp.where(covered[:, None], placed, text_block)
    text_normed = rms_normed(embedded, text_gain).astype(jnp.bfloat16)
    text_heads = jnp.dot(
        text_normed,
        text_project.reshape(model_width, 3 * local_width),
        preferred_element_type=jnp.float32,
    )
    positions = seq_index * rows_per_block + jnp.arange(rows_per_block, dtype=jnp.int32)
    query_rows = rotary(
        text_heads[:, :local_width].reshape(rows_per_block, head_count, HEAD), positions
    ).astype(jnp.bfloat16)
    key_rows = rotary(
        text_heads[:, local_width : 2 * local_width].reshape(rows_per_block, head_count, HEAD),
        positions,
    ).astype(jnp.bfloat16)
    value_rows = text_heads[:, 2 * local_width :].astype(jnp.bfloat16)
    key_flat = key_rows.reshape(rows_per_block, local_width)
    key_all = lax.all_gather(key_flat, "seq", axis=0, tiled=True)
    value_all = lax.all_gather(value_rows, "seq", axis=0, tiled=True)
    attended_rows = causal_attention(
        query_rows.reshape(rows_per_block, local_width),
        key_all,
        value_all,
        seq_index,
        block_lengths,
        rows_per_block,
    )
    own_rows = text_rows.shape[0]

    def text_term(offset, row_count):
        return jnp.dot(attended_rows, text_output, preferred_element_type=jnp.float32)

    text_sum = summed_rows(text_term, own_rows)
    residual = lax.dynamic_slice_in_dim(embedded, tp_index * own_rows, own_rows, 0)
    hidden = (residual.astype(jnp.float32) + text_sum).astype(jnp.bfloat16)
    return (hidden, key_flat, value_rows)


def solution(mesh):
    placed = (
        P("seq", "tp", None),
        P(("seq", "tp"), None),
        P(),
        P(),
        P(),
        P(),
        P(None, None, "tp"),
        P("tp", None),
        P(),
        P("tp", None),
        P(),
        P(None, None, "tp"),
        P("tp", None),
    )
    return jax.shard_map(
        shards,
        mesh=mesh,
        in_specs=placed,
        out_specs=(P(("seq", "tp"), None), P("seq", "tp"), P("seq", "tp")),
        check_vma=False,
    )
```

```python
import math

import jax
import jax.numpy as jnp
from jax import lax
from jax.experimental import pallas as pl
from jax.experimental.pallas import tpu as pltpu
from jax.sharding import PartitionSpec as P

HEAD = 104


LN_EPS = 1e-05
RMS_EPS = 1e-06
MASKED_SCORE = -1e30
KEY_SPAN = 512


def layer_normed(row_values, gain_vector):
    floats = row_values.astype(jnp.float32)
    centre = floats - jnp.mean(floats, -1, keepdims=True)
    spread = jnp.mean(centre * centre, -1, keepdims=True)
    return centre * lax.rsqrt(spread + LN_EPS) * gain_vector


def rms_normed(row_values, gain_vector):
    floats = row_values.astype(jnp.float32)
    return floats * lax.rsqrt(jnp.mean(floats * floats, -1, keepdims=True) + RMS_EPS) * gain_vector


def rotary(heads_in, positions):
    halfway = heads_in.shape[-1] // 2
    rates = 10000.0 ** (-2.0 * jnp.arange(halfway, dtype=jnp.float32) / heads_in.shape[-1])
    angles = positions.astype(jnp.float32)[:, None] * rates[None, :]
    cosine_table = jnp.cos(angles)[:, None, :]
    sine_table = jnp.sin(angles)[:, None, :]
    leading = heads_in[..., :halfway]
    trailing = heads_in[..., halfway:]
    return jnp.concatenate(
        [
            leading * cosine_table - trailing * sine_table,
            trailing * cosine_table + leading * sine_table,
        ],
        -1,
    )


def summed_rows(term_task, own_rows):
    return lax.psum_scatter(
        term_task(jnp.int32(0), own_rows * lax.axis_size("tp")),
        "tp",
        scatter_dimension=0,
        tiled=True,
    )


def attention_kernel(meta_ref, lengths_ref, q_ref, k_ref, v_ref, o_ref, m_sc, l_sc, acc_sc):
    step = pl.program_id(0)
    seq = meta_ref[0]
    rows, width = q_ref.shape
    span = k_ref.shape[0]
    heads = width // HEAD
    score_scale = 1.0 / math.sqrt(HEAD)

    @pl.when(step == 0)
    def _():
        m_sc[...] = jnp.full(m_sc.shape, MASKED_SCORE, jnp.float32)
        l_sc[...] = jnp.zeros(l_sc.shape, jnp.float32)
        acc_sc[...] = jnp.zeros(acc_sc.shape, jnp.float32)

    def update(diagonal):
        q = q_ref[...]
        k = k_ref[...]
        v = v_ref[...]
        column = lax.broadcasted_iota(jnp.int32, (rows, width), 1)
        key_index = lax.broadcasted_iota(jnp.int32, (1, span), 1)
        bias = jnp.where(key_index < lengths_ref[step], 0.0, MASKED_SCORE).astype(jnp.float32)
        if diagonal:
            causal = lax.broadcasted_iota(jnp.int32, (rows, span), 1) <= lax.broadcasted_iota(
                jnp.int32, (rows, span), 0
            )
        for h in range(heads):
            in_head = (column >= h * HEAD) & (column < (h + 1) * HEAD)
            q_head = jnp.where(in_head, q, jnp.zeros_like(q))
            scores = (
                lax.dot_general(
                    q_head, k, (((1,), (1,)), ((), ())), preferred_element_type=jnp.float32
                )
                * score_scale
                + bias
            )
            if diagonal:
                scores = jnp.where(causal, scores, MASKED_SCORE)
            m_prev = m_sc[h][:, :1]
            m_new = jnp.maximum(m_prev, jnp.max(scores, axis=1, keepdims=True))
            weights = jnp.exp(scores - m_new)
            alpha = jnp.exp(m_prev - m_new)
            l_new = alpha * l_sc[h][:, :1] + jnp.sum(weights, axis=1, keepdims=True)
            mixed = jnp.dot(weights.astype(jnp.bfloat16), v, preferred_element_type=jnp.float32)
            acc_sc[h] = acc_sc[h] * alpha + mixed
            m_sc[h] = jnp.broadcast_to(m_new, m_sc.shape[1:])
            l_sc[h] = jnp.broadcast_to(l_new, l_sc.shape[1:])

    @pl.when(step < seq)
    def _():
        update(False)

    @pl.when(step == seq)
    def _():
        update(True)

    @pl.when(step == pl.num_programs(0) - 1)
    def _():
        column = lax.broadcasted_iota(jnp.int32, (rows, width), 1)
        result = jnp.zeros((rows, width), jnp.float32)
        for h in range(heads):
            in_head = (column >= h * HEAD) & (column < (h + 1) * HEAD)
            result = jnp.where(in_head, acc_sc[h] / l_sc[h][:, :1], result)
        o_ref[...] = result.astype(o_ref.dtype)


def causal_attention(query_flat, key_value_all, seq_index, block_lengths, rows_per_block):
    rows, width = query_flat.shape
    span = rows_per_block
    steps = key_value_all.shape[0] // (2 * span)
    heads = width // HEAD
    meta = jnp.reshape(seq_index, (1,)).astype(jnp.int32)
    grid_spec = pltpu.PrefetchScalarGridSpec(
        num_scalar_prefetch=2,
        grid=(steps,),
        in_specs=[
            pl.BlockSpec((rows, width), lambda i, m, n: (0, 0)),
            pl.BlockSpec((span, width), lambda i, m, n: (2 * jnp.minimum(i, m[0]), 0)),
            pl.BlockSpec((span, width), lambda i, m, n: (2 * jnp.minimum(i, m[0]) + 1, 0)),
        ],
        out_specs=pl.BlockSpec((rows, width), lambda i, m, n: (0, 0)),
        scratch_shapes=[
            pltpu.VMEM((heads, rows, 128), jnp.float32),
            pltpu.VMEM((heads, rows, 128), jnp.float32),
            pltpu.VMEM((heads, rows, width), jnp.float32),
        ],
    )
    keys_total = steps * span
    return pl.pallas_call(
        attention_kernel,
        grid_spec=grid_spec,
        out_shape=jax.ShapeDtypeStruct((rows, width), jnp.bfloat16),
        compiler_params=pltpu.CompilerParams(dimension_semantics=("arbitrary",)),
        cost_estimate=pl.CostEstimate(
            flops=4 * heads * rows * keys_total * width,
            transcendentals=heads * rows * keys_total,
            bytes_accessed=key_value_all.size * 2 + 2 * query_flat.size * 2,
        ),
    )(meta, block_lengths, query_flat, key_value_all, key_value_all)


def shards(
    pixels,
    text_rows,
    patch_counts,
    picture_starts,
    block_lengths,
    vision_gain,
    vision_project,
    vision_output,
    merge_gain,
    merge_weight,
    text_gain,
    text_project,
    text_output,
):
    seq_ways = lax.axis_size("seq")
    tp_ways = lax.axis_size("tp")
    seq_index = lax.axis_index("seq")
    tp_index = lax.axis_index("tp")
    picture_total, local_patches, model_width = pixels.shape
    patch_total = local_patches * tp_ways
    local_width = vision_project.shape[2]
    head_count = local_width // HEAD
    patch_normed = layer_normed(pixels, vision_gain).astype(jnp.bfloat16)
    packed_project = vision_project.reshape(model_width, 3 * local_width)
    projected = jnp.einsum(
        "npd,de->npe",
        lax.all_gather(patch_normed, "tp", axis=1, tiled=True),
        packed_project,
        preferred_element_type=jnp.float32,
    ).astype(jnp.bfloat16)
    queries = projected[..., :local_width].reshape(picture_total, patch_total, head_count, HEAD)
    key_heads = projected[..., local_width : 2 * local_width].reshape(
        picture_total, patch_total, head_count, HEAD
    )
    value_heads = projected[..., 2 * local_width :].reshape(
        picture_total, patch_total, head_count, HEAD
    )
    live_counts = lax.dynamic_slice_in_dim(
        patch_counts, seq_index * picture_total, picture_total, 0
    )
    score_scale = 1.0 / math.sqrt(HEAD)
    scores = (
        jnp.einsum("nqhd,nkhd->nhqk", queries, key_heads, preferred_element_type=jnp.float32)
        * score_scale
    )
    allowed = (jnp.arange(patch_total, dtype=jnp.int32)[None, :] < live_counts[:, None])[
        :, None, None, :
    ]
    scores = jnp.where(allowed, scores, MASKED_SCORE)
    highest = jnp.max(scores, -1, keepdims=True)
    weights = jnp.where(allowed, jnp.exp(scores - highest), 0.0)
    mixture = jnp.einsum(
        "nhqk,nkhd->nqhd",
        weights.astype(jnp.bfloat16),
        value_heads,
        preferred_element_type=jnp.float32,
    )
    mixture = mixture / jnp.transpose(jnp.sum(weights, -1), (0, 2, 1))[..., None]
    attended = mixture.astype(jnp.bfloat16).reshape(picture_total, patch_total, local_width)
    patch_major = jnp.transpose(attended, (1, 0, 2)).reshape(
        patch_total * picture_total, local_width
    )

    def vision_term(offset, row_count):
        return jnp.dot(patch_major, vision_output, preferred_element_type=jnp.float32)

    vision_sum = summed_rows(vision_term, local_patches * picture_total)
    vision_sum = jnp.transpose(
        vision_sum.reshape(local_patches, picture_total, model_width), (1, 0, 2)
    )
    vision_rows = (pixels.astype(jnp.float32) + vision_sum).astype(jnp.bfloat16)
    merge_input = layer_normed(vision_rows, merge_gain).astype(jnp.bfloat16)
    merged_total = patch_total // 4
    input_share = merge_weight.shape[0]
    whole_pictures = lax.all_gather(merge_input, "tp", axis=1, tiled=True)
    merged_rows = whole_pictures.reshape(picture_total * merged_total, 4 * model_width)
    owned_inputs = lax.dynamic_slice_in_dim(merged_rows, tp_index * input_share, input_share, 1)

    def merge_term(offset, row_count):
        return jnp.dot(owned_inputs, merge_weight, preferred_element_type=jnp.float32)

    part_rows = picture_total * merged_total // tp_ways
    visual_part = summed_rows(merge_term, part_rows).astype(jnp.bfloat16)
    rows_per_block = text_rows.shape[0] * tp_ways
    start_table = picture_starts.reshape(seq_ways, picture_total)
    dest_table = start_table // rows_per_block
    picture_rank = tp_index * part_rows // merged_total
    rank_dest = jnp.sum(
        jnp.where(
            jnp.arange(picture_total, dtype=jnp.int32)[None, :] == picture_rank, dest_table, 0
        ),
        1,
    )
    senders = rank_dest == seq_index
    segment = lax.all_gather(visual_part, "seq", axis=0, tiled=True)
    row_count = segment.shape[0]
    sources = jnp.arange(row_count, dtype=jnp.int32) // part_rows
    wanted = jnp.any(
        (sources[:, None] == jnp.arange(seq_ways, dtype=jnp.int32)[None, :]) & senders[None, :], 1
    )
    selector = (
        (jnp.arange(row_count, dtype=jnp.int32) % part_rows)[None, :]
        == jnp.arange(part_rows, dtype=jnp.int32)[:, None]
    ) & wanted[None, :]
    arrived = jnp.dot(
        selector.astype(jnp.bfloat16), segment, preferred_element_type=jnp.float32
    ).astype(jnp.bfloat16)
    text_block, visual_block = (
        lax.all_gather(text_rows, "tp", axis=0, tiled=True),
        lax.all_gather(arrived, "tp", axis=0, tiled=True),
    )
    landed = dest_table == seq_index
    local_starts = jnp.sum(jnp.where(landed, start_table - seq_index * rows_per_block, 0), 0)
    live_groups = jnp.sum(
        jnp.where(landed, patch_counts.reshape(seq_ways, picture_total) // 4, 0), 0
    )
    slot_index = jnp.arange(merged_total, dtype=jnp.int32)
    targets = (local_starts[:, None] + slot_index[None, :]).reshape(-1)
    in_use = (slot_index[None, :] < live_groups[:, None]).reshape(-1)
    placement = (jnp.arange(rows_per_block, dtype=jnp.int32)[:, None] == targets[None, :]) & in_use[
        None, :
    ]
    covered = jnp.any(placement, 1)
    placed = jnp.dot(
        placement.astype(jnp.bfloat16), visual_block, preferred_element_type=jnp.float32
    ).astype(jnp.bfloat16)
    embedded = jnp.where(covered[:, None], placed, text_block)
    text_normed = rms_normed(embedded, text_gain).astype(jnp.bfloat16)
    text_heads = jnp.dot(
        text_normed,
        text_project.reshape(model_width, 3 * local_width),
        preferred_element_type=jnp.float32,
    )
    positions = seq_index * rows_per_block + jnp.arange(rows_per_block, dtype=jnp.int32)
    query_rows = rotary(
        text_heads[:, :local_width].reshape(rows_per_block, head_count, HEAD), positions
    ).astype(jnp.bfloat16)
    key_rows = rotary(
        text_heads[:, local_width : 2 * local_width].reshape(rows_per_block, head_count, HEAD),
        positions,
    ).astype(jnp.bfloat16)
    value_rows = text_heads[:, 2 * local_width :].astype(jnp.bfloat16)
    key_flat = key_rows.reshape(rows_per_block, local_width)
    key_value_all = lax.all_gather(
        jnp.concatenate([key_flat, value_rows], 0), "seq", axis=0, tiled=True
    )
    attended_rows = causal_attention(
        query_rows.reshape(rows_per_block, local_width),
        key_value_all,
        seq_index,
        block_lengths,
        rows_per_block,
    )
    own_rows = text_rows.shape[0]

    def text_term(offset, row_count):
        return jnp.dot(attended_rows, text_output, preferred_element_type=jnp.float32)

    text_sum = summed_rows(text_term, own_rows)
    residual = lax.dynamic_slice_in_dim(embedded, tp_index * own_rows, own_rows, 0)
    hidden = (residual.astype(jnp.float32) + text_sum).astype(jnp.bfloat16)
    return (hidden, key_flat, value_rows)


def solution(mesh):
    placed = (
        P("seq", "tp", None),
        P(("seq", "tp"), None),
        P(),
        P(),
        P(),
        P(),
        P(None, None, "tp"),
        P("tp", None),
        P(),
        P("tp", None),
        P(),
        P(None, None, "tp"),
        P("tp", None),
    )
    return jax.shard_map(
        shards,
        mesh=mesh,
        in_specs=placed,
        out_specs=(P(("seq", "tp"), None), P("seq", "tp"), P("seq", "tp")),
        check_vma=False,
    )
```

```python
import math

import jax
import jax.numpy as jnp
from jax import lax
from jax.experimental import pallas as pl
from jax.experimental.pallas import tpu as pltpu
from jax.sharding import PartitionSpec as P

HEAD = 104


LN_EPS = 1e-05
RMS_EPS = 1e-06
MASKED_SCORE = -1e30
KEY_SPAN = 512


def layer_normed(row_values, gain_vector):
    floats = row_values.astype(jnp.float32)
    centre = floats - jnp.mean(floats, -1, keepdims=True)
    spread = jnp.mean(centre * centre, -1, keepdims=True)
    return centre * lax.rsqrt(spread + LN_EPS) * gain_vector


def rms_normed(row_values, gain_vector):
    floats = row_values.astype(jnp.float32)
    return floats * lax.rsqrt(jnp.mean(floats * floats, -1, keepdims=True) + RMS_EPS) * gain_vector


def rotary(heads_in, positions):
    halfway = heads_in.shape[-1] // 2
    rates = 10000.0 ** (-2.0 * jnp.arange(halfway, dtype=jnp.float32) / heads_in.shape[-1])
    angles = positions.astype(jnp.float32)[:, None] * rates[None, :]
    cosine_table = jnp.cos(angles)[:, None, :]
    sine_table = jnp.sin(angles)[:, None, :]
    leading = heads_in[..., :halfway]
    trailing = heads_in[..., halfway:]
    return jnp.concatenate(
        [
            leading * cosine_table - trailing * sine_table,
            trailing * cosine_table + leading * sine_table,
        ],
        -1,
    )


def summed_rows(term_task, own_rows):
    return lax.psum_scatter(
        term_task(jnp.int32(0), own_rows * lax.axis_size("tp")),
        "tp",
        scatter_dimension=0,
        tiled=True,
    )


def attention_kernel(meta_ref, lengths_ref, qt_ref, k_ref, v_ref, o_ref, m_sc, l_sc, acc_sc):
    step = pl.program_id(0)
    seq = meta_ref[0]
    width, rows = qt_ref.shape
    span = k_ref.shape[0]
    heads = width // HEAD
    score_scale = 1.0 / math.sqrt(HEAD)

    @pl.when(step == 0)
    def _():
        m_sc[...] = jnp.full(m_sc.shape, MASKED_SCORE, jnp.float32)
        l_sc[...] = jnp.zeros(l_sc.shape, jnp.float32)
        acc_sc[...] = jnp.zeros(acc_sc.shape, jnp.float32)

    def update(diagonal):
        qt = qt_ref[...]
        k = k_ref[...]
        v = v_ref[...]
        feature = lax.broadcasted_iota(jnp.int32, (width, rows), 0)
        key_index = lax.broadcasted_iota(jnp.int32, (span, 1), 0)
        bias = jnp.where(key_index < lengths_ref[step], 0.0, MASKED_SCORE).astype(jnp.float32)
        if diagonal:
            causal = lax.broadcasted_iota(jnp.int32, (span, rows), 0) <= lax.broadcasted_iota(
                jnp.int32, (span, rows), 1
            )
        for h in range(heads):
            in_head = (feature >= h * HEAD) & (feature < (h + 1) * HEAD)
            qt_head = jnp.where(in_head, qt, jnp.zeros_like(qt))
            scores = jnp.dot(k, qt_head, preferred_element_type=jnp.float32) * score_scale + bias
            if diagonal:
                scores = jnp.where(causal, scores, MASKED_SCORE)
            m_prev = m_sc[h]
            m_new = jnp.maximum(m_prev, jnp.max(scores, axis=0, keepdims=True))
            weights = jnp.exp(scores - m_new)
            alpha = jnp.exp(m_prev - m_new)
            l_sc[h] = alpha * l_sc[h] + jnp.sum(weights, axis=0, keepdims=True)
            mixed = lax.dot_general(
                v,
                weights.astype(jnp.bfloat16),
                (((0,), (0,)), ((), ())),
                preferred_element_type=jnp.float32,
            )
            acc_sc[h] = acc_sc[h] * alpha + mixed
            m_sc[h] = m_new

    @pl.when(step < seq)
    def _():
        update(False)

    @pl.when(step == seq)
    def _():
        update(True)

    @pl.when(step == pl.num_programs(0) - 1)
    def _():
        feature = lax.broadcasted_iota(jnp.int32, (width, rows), 0)
        result = jnp.zeros((width, rows), jnp.float32)
        for h in range(heads):
            in_head = (feature >= h * HEAD) & (feature < (h + 1) * HEAD)
            result = jnp.where(in_head, acc_sc[h] / l_sc[h], result)
        o_ref[...] = result


def causal_attention(query_flat, key_value_all, seq_index, block_lengths, rows_per_block):
    rows, width = query_flat.shape
    span = rows_per_block
    steps = key_value_all.shape[0] // (2 * span)
    heads = width // HEAD
    meta = jnp.reshape(seq_index, (1,)).astype(jnp.int32)
    grid_spec = pltpu.PrefetchScalarGridSpec(
        num_scalar_prefetch=2,
        grid=(steps,),
        in_specs=[
            pl.BlockSpec((width, rows), lambda i, m, n: (0, 0)),
            pl.BlockSpec((span, width), lambda i, m, n: (2 * jnp.minimum(i, m[0]), 0)),
            pl.BlockSpec((span, width), lambda i, m, n: (2 * jnp.minimum(i, m[0]) + 1, 0)),
        ],
        out_specs=pl.BlockSpec((width, rows), lambda i, m, n: (0, 0)),
        scratch_shapes=[
            pltpu.VMEM((heads, 1, rows), jnp.float32),
            pltpu.VMEM((heads, 1, rows), jnp.float32),
            pltpu.VMEM((heads, width, rows), jnp.float32),
        ],
    )
    keys_total = steps * span
    result = pl.pallas_call(
        attention_kernel,
        grid_spec=grid_spec,
        out_shape=jax.ShapeDtypeStruct((width, rows), jnp.float32),
        compiler_params=pltpu.CompilerParams(dimension_semantics=("arbitrary",)),
        cost_estimate=pl.CostEstimate(
            flops=4 * heads * rows * keys_total * width,
            transcendentals=heads * rows * keys_total,
            bytes_accessed=key_value_all.size * 2 + 3 * query_flat.size * 2,
        ),
    )(meta, block_lengths, jnp.transpose(query_flat), key_value_all, key_value_all)
    return jnp.transpose(result).astype(jnp.bfloat16)


def shards(
    pixels,
    text_rows,
    patch_counts,
    picture_starts,
    block_lengths,
    vision_gain,
    vision_project,
    vision_output,
    merge_gain,
    merge_weight,
    text_gain,
    text_project,
    text_output,
):
    seq_ways = lax.axis_size("seq")
    tp_ways = lax.axis_size("tp")
    seq_index = lax.axis_index("seq")
    tp_index = lax.axis_index("tp")
    picture_total, local_patches, model_width = pixels.shape
    patch_total = local_patches * tp_ways
    local_width = vision_project.shape[2]
    head_count = local_width // HEAD
    patch_normed = layer_normed(pixels, vision_gain).astype(jnp.bfloat16)
    packed_project = vision_project.reshape(model_width, 3 * local_width)
    projected = jnp.einsum(
        "npd,de->npe",
        lax.all_gather(patch_normed, "tp", axis=1, tiled=True),
        packed_project,
        preferred_element_type=jnp.float32,
    ).astype(jnp.bfloat16)
    queries = projected[..., :local_width].reshape(picture_total, patch_total, head_count, HEAD)
    key_heads = projected[..., local_width : 2 * local_width].reshape(
        picture_total, patch_total, head_count, HEAD
    )
    value_heads = projected[..., 2 * local_width :].reshape(
        picture_total, patch_total, head_count, HEAD
    )
    live_counts = lax.dynamic_slice_in_dim(
        patch_counts, seq_index * picture_total, picture_total, 0
    )
    score_scale = 1.0 / math.sqrt(HEAD)
    scores = (
        jnp.einsum("nqhd,nkhd->nhqk", queries, key_heads, preferred_element_type=jnp.float32)
        * score_scale
    )
    allowed = (jnp.arange(patch_total, dtype=jnp.int32)[None, :] < live_counts[:, None])[
        :, None, None, :
    ]
    scores = jnp.where(allowed, scores, MASKED_SCORE)
    highest = jnp.max(scores, -1, keepdims=True)
    weights = jnp.where(allowed, jnp.exp(scores - highest), 0.0)
    mixture = jnp.einsum(
        "nhqk,nkhd->nqhd",
        weights.astype(jnp.bfloat16),
        value_heads,
        preferred_element_type=jnp.float32,
    )
    mixture = mixture / jnp.transpose(jnp.sum(weights, -1), (0, 2, 1))[..., None]
    attended = mixture.astype(jnp.bfloat16).reshape(picture_total, patch_total, local_width)
    patch_major = jnp.transpose(attended, (1, 0, 2)).reshape(
        patch_total * picture_total, local_width
    )

    def vision_term(offset, row_count):
        return jnp.dot(patch_major, vision_output, preferred_element_type=jnp.float32)

    vision_sum = summed_rows(vision_term, local_patches * picture_total)
    vision_sum = jnp.transpose(
        vision_sum.reshape(local_patches, picture_total, model_width), (1, 0, 2)
    )
    vision_rows = (pixels.astype(jnp.float32) + vision_sum).astype(jnp.bfloat16)
    merge_input = layer_normed(vision_rows, merge_gain).astype(jnp.bfloat16)
    merged_total = patch_total // 4
    input_share = merge_weight.shape[0]
    whole_pictures = lax.all_gather(merge_input, "tp", axis=1, tiled=True)
    merged_rows = whole_pictures.reshape(picture_total * merged_total, 4 * model_width)
    owned_inputs = lax.dynamic_slice_in_dim(merged_rows, tp_index * input_share, input_share, 1)

    def merge_term(offset, row_count):
        return jnp.dot(owned_inputs, merge_weight, preferred_element_type=jnp.float32)

    part_rows = picture_total * merged_total // tp_ways
    visual_part = summed_rows(merge_term, part_rows).astype(jnp.bfloat16)
    rows_per_block = text_rows.shape[0] * tp_ways
    start_table = picture_starts.reshape(seq_ways, picture_total)
    dest_table = start_table // rows_per_block
    picture_rank = tp_index * part_rows // merged_total
    rank_dest = jnp.sum(
        jnp.where(
            jnp.arange(picture_total, dtype=jnp.int32)[None, :] == picture_rank, dest_table, 0
        ),
        1,
    )
    senders = rank_dest == seq_index
    segment = lax.all_gather(visual_part, "seq", axis=0, tiled=True)
    row_count = segment.shape[0]
    sources = jnp.arange(row_count, dtype=jnp.int32) // part_rows
    wanted = jnp.any(
        (sources[:, None] == jnp.arange(seq_ways, dtype=jnp.int32)[None, :]) & senders[None, :], 1
    )
    selector = (
        (jnp.arange(row_count, dtype=jnp.int32) % part_rows)[None, :]
        == jnp.arange(part_rows, dtype=jnp.int32)[:, None]
    ) & wanted[None, :]
    arrived = jnp.dot(
        selector.astype(jnp.bfloat16), segment, preferred_element_type=jnp.float32
    ).astype(jnp.bfloat16)
    text_block, visual_block = (
        lax.all_gather(text_rows, "tp", axis=0, tiled=True),
        lax.all_gather(arrived, "tp", axis=0, tiled=True),
    )
    landed = dest_table == seq_index
    local_starts = jnp.sum(jnp.where(landed, start_table - seq_index * rows_per_block, 0), 0)
    live_groups = jnp.sum(
        jnp.where(landed, patch_counts.reshape(seq_ways, picture_total) // 4, 0), 0
    )
    slot_index = jnp.arange(merged_total, dtype=jnp.int32)
    targets = (local_starts[:, None] + slot_index[None, :]).reshape(-1)
    in_use = (slot_index[None, :] < live_groups[:, None]).reshape(-1)
    placement = (jnp.arange(rows_per_block, dtype=jnp.int32)[:, None] == targets[None, :]) & in_use[
        None, :
    ]
    covered = jnp.any(placement, 1)
    placed = jnp.dot(
        placement.astype(jnp.bfloat16), visual_block, preferred_element_type=jnp.float32
    ).astype(jnp.bfloat16)
    embedded = jnp.where(covered[:, None], placed, text_block)
    text_normed = rms_normed(embedded, text_gain).astype(jnp.bfloat16)
    text_heads = jnp.dot(
        text_normed,
        text_project.reshape(model_width, 3 * local_width),
        preferred_element_type=jnp.float32,
    )
    positions = seq_index * rows_per_block + jnp.arange(rows_per_block, dtype=jnp.int32)
    query_rows = rotary(
        text_heads[:, :local_width].reshape(rows_per_block, head_count, HEAD), positions
    ).astype(jnp.bfloat16)
    key_rows = rotary(
        text_heads[:, local_width : 2 * local_width].reshape(rows_per_block, head_count, HEAD),
        positions,
    ).astype(jnp.bfloat16)
    value_rows = text_heads[:, 2 * local_width :].astype(jnp.bfloat16)
    key_flat = key_rows.reshape(rows_per_block, local_width)
    key_value_all = lax.all_gather(
        jnp.concatenate([key_flat, value_rows], 0), "seq", axis=0, tiled=True
    )
    attended_rows = causal_attention(
        query_rows.reshape(rows_per_block, local_width),
        key_value_all,
        seq_index,
        block_lengths,
        rows_per_block,
    )
    own_rows = text_rows.shape[0]

    def text_term(offset, row_count):
        return jnp.dot(attended_rows, text_output, preferred_element_type=jnp.float32)

    text_sum = summed_rows(text_term, own_rows)
    residual = lax.dynamic_slice_in_dim(embedded, tp_index * own_rows, own_rows, 0)
    hidden = (residual.astype(jnp.float32) + text_sum).astype(jnp.bfloat16)
    return (hidden, key_flat, value_rows)


def solution(mesh):
    placed = (
        P("seq", "tp", None),
        P(("seq", "tp"), None),
        P(),
        P(),
        P(),
        P(),
        P(None, None, "tp"),
        P("tp", None),
        P(),
        P("tp", None),
        P(),
        P(None, None, "tp"),
        P("tp", None),
    )
    return jax.shard_map(
        shards,
        mesh=mesh,
        in_specs=placed,
        out_specs=(P(("seq", "tp"), None), P("seq", "tp"), P("seq", "tp")),
        check_vma=False,
    )
```

```python
import functools
import math

import jax
import jax.numpy as jnp
from jax import lax
from jax.experimental import pallas as pl
from jax.experimental.pallas import tpu as pltpu
from jax.sharding import PartitionSpec as P

HEAD = 104


LN_EPS = 1e-05
RMS_EPS = 1e-06
MASKED_SCORE = -1e30
KEY_SPAN = 512


def layer_normed(row_values, gain_vector):
    floats = row_values.astype(jnp.float32)
    centre = floats - jnp.mean(floats, -1, keepdims=True)
    spread = jnp.mean(centre * centre, -1, keepdims=True)
    return centre * lax.rsqrt(spread + LN_EPS) * gain_vector


def rms_normed(row_values, gain_vector):
    floats = row_values.astype(jnp.float32)
    return floats * lax.rsqrt(jnp.mean(floats * floats, -1, keepdims=True) + RMS_EPS) * gain_vector


def rotary(heads_in, positions):
    halfway = heads_in.shape[-1] // 2
    rates = 10000.0 ** (-2.0 * jnp.arange(halfway, dtype=jnp.float32) / heads_in.shape[-1])
    angles = positions.astype(jnp.float32)[:, None] * rates[None, :]
    cosine_table = jnp.cos(angles)[:, None, :]
    sine_table = jnp.sin(angles)[:, None, :]
    leading = heads_in[..., :halfway]
    trailing = heads_in[..., halfway:]
    return jnp.concatenate(
        [
            leading * cosine_table - trailing * sine_table,
            trailing * cosine_table + leading * sine_table,
        ],
        -1,
    )


MESH_IDS = pl.DeviceIdType.MESH


def exchange_kernel(ways, gather, x_ref, y_ref, send_sem, recv_sem, local_sem):
    me = lax.axis_index("tp")
    row = lax.axis_index("seq")
    barrier = pltpu.get_barrier_semaphore()
    for shift in range(1, ways):
        peer = lax.rem(me + shift, ways)
        pl.semaphore_signal(barrier, inc=1, device_id=(row, peer), device_id_type=MESH_IDS)
    pl.semaphore_wait(barrier, ways - 1)
    sends = []
    for shift in range(1, ways):
        peer = lax.rem(me + shift, ways)
        copy = pltpu.make_async_remote_copy(
            src_ref=x_ref if gather else x_ref.at[peer],
            dst_ref=y_ref.at[me],
            send_sem=send_sem.at[shift],
            recv_sem=recv_sem.at[shift],
            device_id=(row, peer),
            device_id_type=MESH_IDS,
        )
        copy.start()
        sends.append(copy)
    local = pltpu.make_async_copy(x_ref if gather else x_ref.at[me], y_ref.at[me], local_sem)
    local.start()
    for copy in sends:
        copy.wait_send()
    for shift in range(1, ways):
        source = lax.rem(me + ways - shift, ways)
        arriving = pltpu.make_async_remote_copy(
            src_ref=x_ref if gather else x_ref.at[source],
            dst_ref=y_ref.at[source],
            send_sem=send_sem.at[shift],
            recv_sem=recv_sem.at[shift],
            device_id=(row, source),
            device_id_type=MESH_IDS,
        )
        arriving.wait_recv()
    local.wait()


def tp_exchange(x, ways, gather, collective_id):
    piece = x.shape if gather else x.shape[1:]
    return pl.pallas_call(
        functools.partial(exchange_kernel, ways, gather),
        out_shape=jax.ShapeDtypeStruct((ways,) + tuple(piece), x.dtype),
        in_specs=[pl.BlockSpec(memory_space=pl.ANY)],
        out_specs=pl.BlockSpec(memory_space=pl.ANY),
        scratch_shapes=[
            pltpu.SemaphoreType.DMA((ways,)),
            pltpu.SemaphoreType.DMA((ways,)),
            pltpu.SemaphoreType.DMA(()),
        ],
        compiler_params=pltpu.CompilerParams(collective_id=collective_id, has_side_effects=True),
    )(x)


def summed_rows(term_task, own_rows, collective_id):
    ways = lax.axis_size("tp")
    partial = term_task(jnp.int32(0), own_rows * ways)
    pieces = partial.reshape((ways, own_rows) + partial.shape[1:])
    return jnp.sum(tp_exchange(pieces, ways, False, collective_id), 0)


def gathered_patches(piece, collective_id):
    ways = lax.axis_size("tp")
    whole = tp_exchange(piece, ways, True, collective_id)
    return jnp.transpose(whole, (1, 0, 2, 3)).reshape(
        (piece.shape[0], ways * piece.shape[1]) + piece.shape[2:]
    )


def attention_kernel(meta_ref, lengths_ref, qt_ref, k_ref, v_ref, o_ref, m_sc, l_sc, acc_sc):
    step = pl.program_id(0)
    seq = meta_ref[0]
    width, rows = qt_ref.shape
    span = k_ref.shape[0]
    heads = width // HEAD
    score_scale = 1.0 / math.sqrt(HEAD)

    @pl.when(step == 0)
    def _():
        m_sc[...] = jnp.full(m_sc.shape, MASKED_SCORE, jnp.float32)
        l_sc[...] = jnp.zeros(l_sc.shape, jnp.float32)
        acc_sc[...] = jnp.zeros(acc_sc.shape, jnp.float32)

    def update(diagonal):
        qt = qt_ref[...]
        k = k_ref[...]
        v = v_ref[...]
        feature = lax.broadcasted_iota(jnp.int32, (width, rows), 0)
        key_index = lax.broadcasted_iota(jnp.int32, (span, 1), 0)
        bias = jnp.where(key_index < lengths_ref[step], 0.0, MASKED_SCORE).astype(jnp.float32)
        if diagonal:
            causal = lax.broadcasted_iota(jnp.int32, (span, rows), 0) <= lax.broadcasted_iota(
                jnp.int32, (span, rows), 1
            )
        for h in range(heads):
            in_head = (feature >= h * HEAD) & (feature < (h + 1) * HEAD)
            qt_head = jnp.where(in_head, qt, jnp.zeros_like(qt))
            scores = jnp.dot(k, qt_head, preferred_element_type=jnp.float32) * score_scale + bias
            if diagonal:
                scores = jnp.where(causal, scores, MASKED_SCORE)
            m_prev = m_sc[h]
            m_new = jnp.maximum(m_prev, jnp.max(scores, axis=0, keepdims=True))
            weights = jnp.exp(scores - m_new)
            alpha = jnp.exp(m_prev - m_new)
            l_sc[h] = alpha * l_sc[h] + jnp.sum(weights, axis=0, keepdims=True)
            mixed = lax.dot_general(
                v,
                weights.astype(jnp.bfloat16),
                (((0,), (0,)), ((), ())),
                preferred_element_type=jnp.float32,
            )
            acc_sc[h] = acc_sc[h] * alpha + mixed
            m_sc[h] = m_new

    @pl.when(step < seq)
    def _():
        update(False)

    @pl.when(step == seq)
    def _():
        update(True)

    @pl.when(step == pl.num_programs(0) - 1)
    def _():
        feature = lax.broadcasted_iota(jnp.int32, (width, rows), 0)
        result = jnp.zeros((width, rows), jnp.float32)
        for h in range(heads):
            in_head = (feature >= h * HEAD) & (feature < (h + 1) * HEAD)
            result = jnp.where(in_head, acc_sc[h] / l_sc[h], result)
        o_ref[...] = result


def causal_attention(query_flat, key_value_all, seq_index, block_lengths, rows_per_block):
    rows, width = query_flat.shape
    span = rows_per_block
    steps = key_value_all.shape[0] // (2 * span)
    heads = width // HEAD
    meta = jnp.reshape(seq_index, (1,)).astype(jnp.int32)
    grid_spec = pltpu.PrefetchScalarGridSpec(
        num_scalar_prefetch=2,
        grid=(steps,),
        in_specs=[
            pl.BlockSpec((width, rows), lambda i, m, n: (0, 0)),
            pl.BlockSpec((span, width), lambda i, m, n: (2 * jnp.minimum(i, m[0]), 0)),
            pl.BlockSpec((span, width), lambda i, m, n: (2 * jnp.minimum(i, m[0]) + 1, 0)),
        ],
        out_specs=pl.BlockSpec((width, rows), lambda i, m, n: (0, 0)),
        scratch_shapes=[
            pltpu.VMEM((heads, 1, rows), jnp.float32),
            pltpu.VMEM((heads, 1, rows), jnp.float32),
            pltpu.VMEM((heads, width, rows), jnp.float32),
        ],
    )
    keys_total = steps * span
    result = pl.pallas_call(
        attention_kernel,
        grid_spec=grid_spec,
        out_shape=jax.ShapeDtypeStruct((width, rows), jnp.float32),
        compiler_params=pltpu.CompilerParams(dimension_semantics=("arbitrary",)),
        cost_estimate=pl.CostEstimate(
            flops=4 * heads * rows * keys_total * width,
            transcendentals=heads * rows * keys_total,
            bytes_accessed=key_value_all.size * 2 + 3 * query_flat.size * 2,
        ),
    )(meta, block_lengths, jnp.transpose(query_flat), key_value_all, key_value_all)
    return jnp.transpose(result).astype(jnp.bfloat16)


def shards(
    pixels,
    text_rows,
    patch_counts,
    picture_starts,
    block_lengths,
    vision_gain,
    vision_project,
    vision_output,
    merge_gain,
    merge_weight,
    text_gain,
    text_project,
    text_output,
):
    seq_ways = lax.axis_size("seq")
    tp_ways = lax.axis_size("tp")
    seq_index = lax.axis_index("seq")
    tp_index = lax.axis_index("tp")
    picture_total, local_patches, model_width = pixels.shape
    patch_total = local_patches * tp_ways
    local_width = vision_project.shape[2]
    head_count = local_width // HEAD
    patch_normed = layer_normed(pixels, vision_gain).astype(jnp.bfloat16)
    packed_project = vision_project.reshape(model_width, 3 * local_width)
    projected = jnp.einsum(
        "npd,de->npe",
        gathered_patches(patch_normed, 0),
        packed_project,
        preferred_element_type=jnp.float32,
    ).astype(jnp.bfloat16)
    queries = projected[..., :local_width].reshape(picture_total, patch_total, head_count, HEAD)
    key_heads = projected[..., local_width : 2 * local_width].reshape(
        picture_total, patch_total, head_count, HEAD
    )
    value_heads = projected[..., 2 * local_width :].reshape(
        picture_total, patch_total, head_count, HEAD
    )
    live_counts = lax.dynamic_slice_in_dim(
        patch_counts, seq_index * picture_total, picture_total, 0
    )
    score_scale = 1.0 / math.sqrt(HEAD)
    scores = (
        jnp.einsum("nqhd,nkhd->nhqk", queries, key_heads, preferred_element_type=jnp.float32)
        * score_scale
    )
    allowed = (jnp.arange(patch_total, dtype=jnp.int32)[None, :] < live_counts[:, None])[
        :, None, None, :
    ]
    scores = jnp.where(allowed, scores, MASKED_SCORE)
    highest = jnp.max(scores, -1, keepdims=True)
    weights = jnp.where(allowed, jnp.exp(scores - highest), 0.0)
    mixture = jnp.einsum(
        "nhqk,nkhd->nqhd",
        weights.astype(jnp.bfloat16),
        value_heads,
        preferred_element_type=jnp.float32,
    )
    mixture = mixture / jnp.transpose(jnp.sum(weights, -1), (0, 2, 1))[..., None]
    attended = mixture.astype(jnp.bfloat16).reshape(picture_total, patch_total, local_width)
    patch_major = jnp.transpose(attended, (1, 0, 2)).reshape(
        patch_total * picture_total, local_width
    )

    def vision_term(offset, row_count):
        return jnp.dot(patch_major, vision_output, preferred_element_type=jnp.float32)

    vision_sum = summed_rows(vision_term, local_patches * picture_total, 2)
    vision_sum = jnp.transpose(
        vision_sum.reshape(local_patches, picture_total, model_width), (1, 0, 2)
    )
    vision_rows = (pixels.astype(jnp.float32) + vision_sum).astype(jnp.bfloat16)
    merge_input = layer_normed(vision_rows, merge_gain).astype(jnp.bfloat16)
    merged_total = patch_total // 4
    input_share = merge_weight.shape[0]
    whole_pictures = gathered_patches(merge_input, 1)
    merged_rows = whole_pictures.reshape(picture_total * merged_total, 4 * model_width)
    owned_inputs = lax.dynamic_slice_in_dim(merged_rows, tp_index * input_share, input_share, 1)

    def merge_term(offset, row_count):
        return jnp.dot(owned_inputs, merge_weight, preferred_element_type=jnp.float32)

    part_rows = picture_total * merged_total // tp_ways
    visual_part = summed_rows(merge_term, part_rows, 3).astype(jnp.bfloat16)
    rows_per_block = text_rows.shape[0] * tp_ways
    start_table = picture_starts.reshape(seq_ways, picture_total)
    dest_table = start_table // rows_per_block
    picture_rank = tp_index * part_rows // merged_total
    rank_dest = jnp.sum(
        jnp.where(
            jnp.arange(picture_total, dtype=jnp.int32)[None, :] == picture_rank, dest_table, 0
        ),
        1,
    )
    senders = rank_dest == seq_index
    segment = lax.all_gather(visual_part, "seq", axis=0, tiled=True)
    row_count = segment.shape[0]
    sources = jnp.arange(row_count, dtype=jnp.int32) // part_rows
    wanted = jnp.any(
        (sources[:, None] == jnp.arange(seq_ways, dtype=jnp.int32)[None, :]) & senders[None, :], 1
    )
    selector = (
        (jnp.arange(row_count, dtype=jnp.int32) % part_rows)[None, :]
        == jnp.arange(part_rows, dtype=jnp.int32)[:, None]
    ) & wanted[None, :]
    arrived = jnp.dot(
        selector.astype(jnp.bfloat16), segment, preferred_element_type=jnp.float32
    ).astype(jnp.bfloat16)
    both_blocks = tp_exchange(jnp.concatenate([text_rows, arrived], 0), tp_ways, True, 5)
    text_block = both_blocks[:, : text_rows.shape[0]].reshape(-1, model_width)
    visual_block = both_blocks[:, text_rows.shape[0] :].reshape(-1, model_width)
    landed = dest_table == seq_index
    local_starts = jnp.sum(jnp.where(landed, start_table - seq_index * rows_per_block, 0), 0)
    live_groups = jnp.sum(
        jnp.where(landed, patch_counts.reshape(seq_ways, picture_total) // 4, 0), 0
    )
    slot_index = jnp.arange(merged_total, dtype=jnp.int32)
    targets = (local_starts[:, None] + slot_index[None, :]).reshape(-1)
    in_use = (slot_index[None, :] < live_groups[:, None]).reshape(-1)
    placement = (jnp.arange(rows_per_block, dtype=jnp.int32)[:, None] == targets[None, :]) & in_use[
        None, :
    ]
    covered = jnp.any(placement, 1)
    placed = jnp.dot(
        placement.astype(jnp.bfloat16), visual_block, preferred_element_type=jnp.float32
    ).astype(jnp.bfloat16)
    embedded = jnp.where(covered[:, None], placed, text_block)
    text_normed = rms_normed(embedded, text_gain).astype(jnp.bfloat16)
    text_heads = jnp.dot(
        text_normed,
        text_project.reshape(model_width, 3 * local_width),
        preferred_element_type=jnp.float32,
    )
    positions = seq_index * rows_per_block + jnp.arange(rows_per_block, dtype=jnp.int32)
    query_rows = rotary(
        text_heads[:, :local_width].reshape(rows_per_block, head_count, HEAD), positions
    ).astype(jnp.bfloat16)
    key_rows = rotary(
        text_heads[:, local_width : 2 * local_width].reshape(rows_per_block, head_count, HEAD),
        positions,
    ).astype(jnp.bfloat16)
    value_rows = text_heads[:, 2 * local_width :].astype(jnp.bfloat16)
    key_flat = key_rows.reshape(rows_per_block, local_width)
    key_value_all = lax.all_gather(
        jnp.concatenate([key_flat, value_rows], 0), "seq", axis=0, tiled=True
    )
    attended_rows = causal_attention(
        query_rows.reshape(rows_per_block, local_width),
        key_value_all,
        seq_index,
        block_lengths,
        rows_per_block,
    )
    own_rows = text_rows.shape[0]

    def text_term(offset, row_count):
        return jnp.dot(attended_rows, text_output, preferred_element_type=jnp.float32)

    text_sum = summed_rows(text_term, own_rows, 4)
    residual = lax.dynamic_slice_in_dim(embedded, tp_index * own_rows, own_rows, 0)
    hidden = (residual.astype(jnp.float32) + text_sum).astype(jnp.bfloat16)
    return (hidden, key_flat, value_rows)


def solution(mesh):
    placed = (
        P("seq", "tp", None),
        P(("seq", "tp"), None),
        P(),
        P(),
        P(),
        P(),
        P(None, None, "tp"),
        P("tp", None),
        P(),
        P("tp", None),
        P(),
        P(None, None, "tp"),
        P("tp", None),
    )
    return jax.shard_map(
        shards,
        mesh=mesh,
        in_specs=placed,
        out_specs=(P(("seq", "tp"), None), P("seq", "tp"), P("seq", "tp")),
        check_vma=False,
    )
```

```python
import functools
import math

import jax
import jax.numpy as jnp
from jax import lax
from jax.experimental import pallas as pl
from jax.experimental.pallas import tpu as pltpu
from jax.sharding import PartitionSpec as P

HEAD = 104


LN_EPS = 1e-05
RMS_EPS = 1e-06
MASKED_SCORE = -1e30
KEY_SPAN = 512


def layer_normed(row_values, gain_vector):
    floats = row_values.astype(jnp.float32)
    centre = floats - jnp.mean(floats, -1, keepdims=True)
    spread = jnp.mean(centre * centre, -1, keepdims=True)
    return centre * lax.rsqrt(spread + LN_EPS) * gain_vector


def rms_normed(row_values, gain_vector):
    floats = row_values.astype(jnp.float32)
    return floats * lax.rsqrt(jnp.mean(floats * floats, -1, keepdims=True) + RMS_EPS) * gain_vector


def rotary(heads_in, positions):
    halfway = heads_in.shape[-1] // 2
    rates = 10000.0 ** (-2.0 * jnp.arange(halfway, dtype=jnp.float32) / heads_in.shape[-1])
    angles = positions.astype(jnp.float32)[:, None] * rates[None, :]
    cosine_table = jnp.cos(angles)[:, None, :]
    sine_table = jnp.sin(angles)[:, None, :]
    leading = heads_in[..., :halfway]
    trailing = heads_in[..., halfway:]
    return jnp.concatenate(
        [
            leading * cosine_table - trailing * sine_table,
            trailing * cosine_table + leading * sine_table,
        ],
        -1,
    )


MESH_IDS = pl.DeviceIdType.MESH


def exchange_kernel(ways, gather, x_ref, y_ref, send_sem, recv_sem, local_sem):
    me = lax.axis_index("tp")
    row = lax.axis_index("seq")
    barrier = pltpu.get_barrier_semaphore()
    for shift in range(1, ways):
        peer = lax.rem(me + shift, ways)
        pl.semaphore_signal(barrier, inc=1, device_id=(row, peer), device_id_type=MESH_IDS)
    pl.semaphore_wait(barrier, ways - 1)
    sends = []
    for shift in range(1, ways):
        peer = lax.rem(me + shift, ways)
        copy = pltpu.make_async_remote_copy(
            src_ref=x_ref if gather else x_ref.at[peer],
            dst_ref=y_ref.at[me],
            send_sem=send_sem.at[shift],
            recv_sem=recv_sem.at[shift],
            device_id=(row, peer),
            device_id_type=MESH_IDS,
        )
        copy.start()
        sends.append(copy)
    local = pltpu.make_async_copy(x_ref if gather else x_ref.at[me], y_ref.at[me], local_sem)
    local.start()
    for copy in sends:
        copy.wait_send()
    for shift in range(1, ways):
        source = lax.rem(me + ways - shift, ways)
        arriving = pltpu.make_async_remote_copy(
            src_ref=x_ref if gather else x_ref.at[source],
            dst_ref=y_ref.at[source],
            send_sem=send_sem.at[shift],
            recv_sem=recv_sem.at[shift],
            device_id=(row, source),
            device_id_type=MESH_IDS,
        )
        arriving.wait_recv()
    local.wait()


def tp_exchange(x, ways, gather, collective_id):
    piece = x.shape if gather else x.shape[1:]
    return pl.pallas_call(
        functools.partial(exchange_kernel, ways, gather),
        out_shape=jax.ShapeDtypeStruct((ways,) + tuple(piece), x.dtype),
        in_specs=[pl.BlockSpec(memory_space=pl.ANY)],
        out_specs=pl.BlockSpec(memory_space=pl.ANY),
        scratch_shapes=[
            pltpu.SemaphoreType.DMA((ways,)),
            pltpu.SemaphoreType.DMA((ways,)),
            pltpu.SemaphoreType.DMA(()),
        ],
        compiler_params=pltpu.CompilerParams(collective_id=collective_id, has_side_effects=True),
    )(x)


def summed_rows(term_task, own_rows, collective_id):
    ways = lax.axis_size("tp")
    partial = term_task(jnp.int32(0), own_rows * ways)
    pieces = partial.reshape((ways, own_rows) + partial.shape[1:]).astype(jnp.bfloat16)
    arrived = tp_exchange(pieces, ways, False, collective_id)
    return jnp.sum(arrived.astype(jnp.float32), 0)


def gathered_patches(piece, collective_id):
    ways = lax.axis_size("tp")
    whole = tp_exchange(piece, ways, True, collective_id)
    return jnp.transpose(whole, (1, 0, 2, 3)).reshape(
        (piece.shape[0], ways * piece.shape[1]) + piece.shape[2:]
    )


def attention_kernel(meta_ref, lengths_ref, qt_ref, k_ref, v_ref, o_ref, m_sc, l_sc, acc_sc):
    step = pl.program_id(0)
    seq = meta_ref[0]
    width, rows = qt_ref.shape
    span = k_ref.shape[0]
    heads = width // HEAD
    score_scale = 1.0 / math.sqrt(HEAD)

    @pl.when(step == 0)
    def _():
        m_sc[...] = jnp.full(m_sc.shape, MASKED_SCORE, jnp.float32)
        l_sc[...] = jnp.zeros(l_sc.shape, jnp.float32)
        acc_sc[...] = jnp.zeros(acc_sc.shape, jnp.float32)

    def update(diagonal):
        qt = qt_ref[...]
        k = k_ref[...]
        v = v_ref[...]
        feature = lax.broadcasted_iota(jnp.int32, (width, rows), 0)
        key_index = lax.broadcasted_iota(jnp.int32, (span, 1), 0)
        bias = jnp.where(key_index < lengths_ref[step], 0.0, MASKED_SCORE).astype(jnp.float32)
        if diagonal:
            causal = lax.broadcasted_iota(jnp.int32, (span, rows), 0) <= lax.broadcasted_iota(
                jnp.int32, (span, rows), 1
            )
        for h in range(heads):
            in_head = (feature >= h * HEAD) & (feature < (h + 1) * HEAD)
            qt_head = jnp.where(in_head, qt, jnp.zeros_like(qt))
            scores = jnp.dot(k, qt_head, preferred_element_type=jnp.float32) * score_scale + bias
            if diagonal:
                scores = jnp.where(causal, scores, MASKED_SCORE)
            m_prev = m_sc[h]
            m_new = jnp.maximum(m_prev, jnp.max(scores, axis=0, keepdims=True))
            weights = jnp.exp(scores - m_new)
            alpha = jnp.exp(m_prev - m_new)
            l_sc[h] = alpha * l_sc[h] + jnp.sum(weights, axis=0, keepdims=True)
            mixed = lax.dot_general(
                v,
                weights.astype(jnp.bfloat16),
                (((0,), (0,)), ((), ())),
                preferred_element_type=jnp.float32,
            )
            acc_sc[h] = acc_sc[h] * alpha + mixed
            m_sc[h] = m_new

    @pl.when(step < seq)
    def _():
        update(False)

    @pl.when(step == seq)
    def _():
        update(True)

    @pl.when(step == pl.num_programs(0) - 1)
    def _():
        feature = lax.broadcasted_iota(jnp.int32, (width, rows), 0)
        result = jnp.zeros((width, rows), jnp.float32)
        for h in range(heads):
            in_head = (feature >= h * HEAD) & (feature < (h + 1) * HEAD)
            result = jnp.where(in_head, acc_sc[h] / l_sc[h], result)
        o_ref[...] = result


def causal_attention(query_flat, key_value_all, seq_index, block_lengths, rows_per_block):
    rows, width = query_flat.shape
    span = rows_per_block
    steps = key_value_all.shape[0] // (2 * span)
    heads = width // HEAD
    meta = jnp.reshape(seq_index, (1,)).astype(jnp.int32)
    grid_spec = pltpu.PrefetchScalarGridSpec(
        num_scalar_prefetch=2,
        grid=(steps,),
        in_specs=[
            pl.BlockSpec((width, rows), lambda i, m, n: (0, 0)),
            pl.BlockSpec((span, width), lambda i, m, n: (2 * jnp.minimum(i, m[0]), 0)),
            pl.BlockSpec((span, width), lambda i, m, n: (2 * jnp.minimum(i, m[0]) + 1, 0)),
        ],
        out_specs=pl.BlockSpec((width, rows), lambda i, m, n: (0, 0)),
        scratch_shapes=[
            pltpu.VMEM((heads, 1, rows), jnp.float32),
            pltpu.VMEM((heads, 1, rows), jnp.float32),
            pltpu.VMEM((heads, width, rows), jnp.float32),
        ],
    )
    keys_total = steps * span
    result = pl.pallas_call(
        attention_kernel,
        grid_spec=grid_spec,
        out_shape=jax.ShapeDtypeStruct((width, rows), jnp.float32),
        compiler_params=pltpu.CompilerParams(dimension_semantics=("arbitrary",)),
        cost_estimate=pl.CostEstimate(
            flops=4 * heads * rows * keys_total * width,
            transcendentals=heads * rows * keys_total,
            bytes_accessed=key_value_all.size * 2 + 3 * query_flat.size * 2,
        ),
    )(meta, block_lengths, jnp.transpose(query_flat), key_value_all, key_value_all)
    return jnp.transpose(result).astype(jnp.bfloat16)


def shards(
    pixels,
    text_rows,
    patch_counts,
    picture_starts,
    block_lengths,
    vision_gain,
    vision_project,
    vision_output,
    merge_gain,
    merge_weight,
    text_gain,
    text_project,
    text_output,
):
    seq_ways = lax.axis_size("seq")
    tp_ways = lax.axis_size("tp")
    seq_index = lax.axis_index("seq")
    tp_index = lax.axis_index("tp")
    picture_total, local_patches, model_width = pixels.shape
    patch_total = local_patches * tp_ways
    local_width = vision_project.shape[2]
    head_count = local_width // HEAD
    patch_normed = layer_normed(pixels, vision_gain).astype(jnp.bfloat16)
    packed_project = vision_project.reshape(model_width, 3 * local_width)
    projected = jnp.einsum(
        "npd,de->npe",
        gathered_patches(patch_normed, 0),
        packed_project,
        preferred_element_type=jnp.float32,
    ).astype(jnp.bfloat16)
    queries = projected[..., :local_width].reshape(picture_total, patch_total, head_count, HEAD)
    key_heads = projected[..., local_width : 2 * local_width].reshape(
        picture_total, patch_total, head_count, HEAD
    )
    value_heads = projected[..., 2 * local_width :].reshape(
        picture_total, patch_total, head_count, HEAD
    )
    live_counts = lax.dynamic_slice_in_dim(
        patch_counts, seq_index * picture_total, picture_total, 0
    )
    score_scale = 1.0 / math.sqrt(HEAD)
    scores = (
        jnp.einsum("nqhd,nkhd->nhqk", queries, key_heads, preferred_element_type=jnp.float32)
        * score_scale
    )
    allowed = (jnp.arange(patch_total, dtype=jnp.int32)[None, :] < live_counts[:, None])[
        :, None, None, :
    ]
    scores = jnp.where(allowed, scores, MASKED_SCORE)
    highest = jnp.max(scores, -1, keepdims=True)
    weights = jnp.where(allowed, jnp.exp(scores - highest), 0.0)
    mixture = jnp.einsum(
        "nhqk,nkhd->nqhd",
        weights.astype(jnp.bfloat16),
        value_heads,
        preferred_element_type=jnp.float32,
    )
    mixture = mixture / jnp.transpose(jnp.sum(weights, -1), (0, 2, 1))[..., None]
    attended = mixture.astype(jnp.bfloat16).reshape(picture_total, patch_total, local_width)
    patch_major = jnp.transpose(attended, (1, 0, 2)).reshape(
        patch_total * picture_total, local_width
    )

    def vision_term(offset, row_count):
        return jnp.dot(patch_major, vision_output, preferred_element_type=jnp.float32)

    vision_sum = summed_rows(vision_term, local_patches * picture_total, 2)
    vision_sum = jnp.transpose(
        vision_sum.reshape(local_patches, picture_total, model_width), (1, 0, 2)
    )
    vision_rows = (pixels.astype(jnp.float32) + vision_sum).astype(jnp.bfloat16)
    merge_input = layer_normed(vision_rows, merge_gain).astype(jnp.bfloat16)
    merged_total = patch_total // 4
    input_share = merge_weight.shape[0]
    whole_pictures = gathered_patches(merge_input, 1)
    merged_rows = whole_pictures.reshape(picture_total * merged_total, 4 * model_width)
    owned_inputs = lax.dynamic_slice_in_dim(merged_rows, tp_index * input_share, input_share, 1)

    def merge_term(offset, row_count):
        return jnp.dot(owned_inputs, merge_weight, preferred_element_type=jnp.float32)

    part_rows = picture_total * merged_total // tp_ways
    visual_part = summed_rows(merge_term, part_rows, 3).astype(jnp.bfloat16)
    rows_per_block = text_rows.shape[0] * tp_ways
    start_table = picture_starts.reshape(seq_ways, picture_total)
    dest_table = start_table // rows_per_block
    picture_rank = tp_index * part_rows // merged_total
    rank_dest = jnp.sum(
        jnp.where(
            jnp.arange(picture_total, dtype=jnp.int32)[None, :] == picture_rank, dest_table, 0
        ),
        1,
    )
    senders = rank_dest == seq_index
    segment = lax.all_gather(visual_part, "seq", axis=0, tiled=True)
    row_count = segment.shape[0]
    sources = jnp.arange(row_count, dtype=jnp.int32) // part_rows
    wanted = jnp.any(
        (sources[:, None] == jnp.arange(seq_ways, dtype=jnp.int32)[None, :]) & senders[None, :], 1
    )
    selector = (
        (jnp.arange(row_count, dtype=jnp.int32) % part_rows)[None, :]
        == jnp.arange(part_rows, dtype=jnp.int32)[:, None]
    ) & wanted[None, :]
    arrived = jnp.dot(
        selector.astype(jnp.bfloat16), segment, preferred_element_type=jnp.float32
    ).astype(jnp.bfloat16)
    both_blocks = tp_exchange(jnp.concatenate([text_rows, arrived], 0), tp_ways, True, 5)
    text_block = both_blocks[:, : text_rows.shape[0]].reshape(-1, model_width)
    visual_block = both_blocks[:, text_rows.shape[0] :].reshape(-1, model_width)
    landed = dest_table == seq_index
    local_starts = jnp.sum(jnp.where(landed, start_table - seq_index * rows_per_block, 0), 0)
    live_groups = jnp.sum(
        jnp.where(landed, patch_counts.reshape(seq_ways, picture_total) // 4, 0), 0
    )
    slot_index = jnp.arange(merged_total, dtype=jnp.int32)
    targets = (local_starts[:, None] + slot_index[None, :]).reshape(-1)
    in_use = (slot_index[None, :] < live_groups[:, None]).reshape(-1)
    placement = (jnp.arange(rows_per_block, dtype=jnp.int32)[:, None] == targets[None, :]) & in_use[
        None, :
    ]
    covered = jnp.any(placement, 1)
    placed = jnp.dot(
        placement.astype(jnp.bfloat16), visual_block, preferred_element_type=jnp.float32
    ).astype(jnp.bfloat16)
    embedded = jnp.where(covered[:, None], placed, text_block)
    text_normed = rms_normed(embedded, text_gain).astype(jnp.bfloat16)
    text_heads = jnp.dot(
        text_normed,
        text_project.reshape(model_width, 3 * local_width),
        preferred_element_type=jnp.float32,
    )
    positions = seq_index * rows_per_block + jnp.arange(rows_per_block, dtype=jnp.int32)
    query_rows = rotary(
        text_heads[:, :local_width].reshape(rows_per_block, head_count, HEAD), positions
    ).astype(jnp.bfloat16)
    key_rows = rotary(
        text_heads[:, local_width : 2 * local_width].reshape(rows_per_block, head_count, HEAD),
        positions,
    ).astype(jnp.bfloat16)
    value_rows = text_heads[:, 2 * local_width :].astype(jnp.bfloat16)
    key_flat = key_rows.reshape(rows_per_block, local_width)
    key_value_all = lax.all_gather(
        jnp.concatenate([key_flat, value_rows], 0), "seq", axis=0, tiled=True
    )
    attended_rows = causal_attention(
        query_rows.reshape(rows_per_block, local_width),
        key_value_all,
        seq_index,
        block_lengths,
        rows_per_block,
    )
    own_rows = text_rows.shape[0]

    def text_term(offset, row_count):
        return jnp.dot(attended_rows, text_output, preferred_element_type=jnp.float32)

    text_sum = summed_rows(text_term, own_rows, 4)
    residual = lax.dynamic_slice_in_dim(embedded, tp_index * own_rows, own_rows, 0)
    hidden = (residual.astype(jnp.float32) + text_sum).astype(jnp.bfloat16)
    return (hidden, key_flat, value_rows)


def solution(mesh):
    placed = (
        P("seq", "tp", None),
        P(("seq", "tp"), None),
        P(),
        P(),
        P(),
        P(),
        P(None, None, "tp"),
        P("tp", None),
        P(),
        P("tp", None),
        P(),
        P(None, None, "tp"),
        P("tp", None),
    )
    return jax.shard_map(
        shards,
        mesh=mesh,
        in_specs=placed,
        out_specs=(P(("seq", "tp"), None), P("seq", "tp"), P("seq", "tp")),
        check_vma=False,
    )
```

```python
import functools
import math

import jax
import jax.numpy as jnp
from jax import lax
from jax.experimental import pallas as pl
from jax.experimental.pallas import tpu as pltpu
from jax.sharding import PartitionSpec as P

HEAD = 104


LN_EPS = 1e-05
RMS_EPS = 1e-06
MASKED_SCORE = -1e30
KEY_SPAN = 512


def layer_normed(row_values, gain_vector):
    floats = row_values.astype(jnp.float32)
    centre = floats - jnp.mean(floats, -1, keepdims=True)
    spread = jnp.mean(centre * centre, -1, keepdims=True)
    return centre * lax.rsqrt(spread + LN_EPS) * gain_vector


def rms_normed(row_values, gain_vector):
    floats = row_values.astype(jnp.float32)
    return floats * lax.rsqrt(jnp.mean(floats * floats, -1, keepdims=True) + RMS_EPS) * gain_vector


def rotary(heads_in, positions):
    halfway = heads_in.shape[-1] // 2
    rates = 10000.0 ** (-2.0 * jnp.arange(halfway, dtype=jnp.float32) / heads_in.shape[-1])
    angles = positions.astype(jnp.float32)[:, None] * rates[None, :]
    cosine_table = jnp.cos(angles)[:, None, :]
    sine_table = jnp.sin(angles)[:, None, :]
    leading = heads_in[..., :halfway]
    trailing = heads_in[..., halfway:]
    return jnp.concatenate(
        [
            leading * cosine_table - trailing * sine_table,
            trailing * cosine_table + leading * sine_table,
        ],
        -1,
    )


MESH_IDS = pl.DeviceIdType.MESH


def exchange_kernel(axis, ways, gather, x_ref, y_ref, send_sem, recv_sem, local_sem):
    me = lax.axis_index(axis)
    other = lax.axis_index("seq" if axis == "tp" else "tp")

    def device(peer):
        return (other, peer) if axis == "tp" else (peer, other)

    barrier = pltpu.get_barrier_semaphore()
    for shift in range(1, ways):
        peer = lax.rem(me + shift, ways)
        pl.semaphore_signal(barrier, inc=1, device_id=device(peer), device_id_type=MESH_IDS)
    pl.semaphore_wait(barrier, ways - 1)
    sends = []
    for shift in range(1, ways):
        peer = lax.rem(me + shift, ways)
        copy = pltpu.make_async_remote_copy(
            src_ref=x_ref if gather else x_ref.at[peer],
            dst_ref=y_ref.at[me],
            send_sem=send_sem.at[shift],
            recv_sem=recv_sem.at[shift],
            device_id=device(peer),
            device_id_type=MESH_IDS,
        )
        copy.start()
        sends.append(copy)
    local = pltpu.make_async_copy(x_ref if gather else x_ref.at[me], y_ref.at[me], local_sem)
    local.start()
    for copy in sends:
        copy.wait_send()
    for shift in range(1, ways):
        source = lax.rem(me + ways - shift, ways)
        arriving = pltpu.make_async_remote_copy(
            src_ref=x_ref if gather else x_ref.at[source],
            dst_ref=y_ref.at[source],
            send_sem=send_sem.at[shift],
            recv_sem=recv_sem.at[shift],
            device_id=device(source),
            device_id_type=MESH_IDS,
        )
        arriving.wait_recv()
    local.wait()


def tp_exchange(x, ways, gather, collective_id, axis="tp"):
    piece = x.shape if gather else x.shape[1:]
    return pl.pallas_call(
        functools.partial(exchange_kernel, axis, ways, gather),
        out_shape=jax.ShapeDtypeStruct((ways,) + tuple(piece), x.dtype),
        in_specs=[pl.BlockSpec(memory_space=pl.ANY)],
        out_specs=pl.BlockSpec(memory_space=pl.ANY),
        scratch_shapes=[
            pltpu.SemaphoreType.DMA((ways,)),
            pltpu.SemaphoreType.DMA((ways,)),
            pltpu.SemaphoreType.DMA(()),
        ],
        compiler_params=pltpu.CompilerParams(collective_id=collective_id, has_side_effects=True),
    )(x)


def summed_rows(term_task, own_rows, collective_id):
    ways = lax.axis_size("tp")
    partial = term_task(jnp.int32(0), own_rows * ways)
    pieces = partial.reshape((ways, own_rows) + partial.shape[1:]).astype(jnp.bfloat16)
    arrived = tp_exchange(pieces, ways, False, collective_id)
    return jnp.sum(arrived.astype(jnp.float32), 0)


def gathered_patches(piece, collective_id):
    ways = lax.axis_size("tp")
    whole = tp_exchange(piece, ways, True, collective_id)
    return jnp.transpose(whole, (1, 0, 2, 3)).reshape(
        (piece.shape[0], ways * piece.shape[1]) + piece.shape[2:]
    )


def attention_kernel(meta_ref, lengths_ref, qt_ref, k_ref, v_ref, o_ref, m_sc, l_sc, acc_sc):
    step = pl.program_id(0)
    seq = meta_ref[0]
    width, rows = qt_ref.shape
    span = k_ref.shape[0]
    heads = width // HEAD
    score_scale = 1.0 / math.sqrt(HEAD)

    @pl.when(step == 0)
    def _():
        m_sc[...] = jnp.full(m_sc.shape, MASKED_SCORE, jnp.float32)
        l_sc[...] = jnp.zeros(l_sc.shape, jnp.float32)
        acc_sc[...] = jnp.zeros(acc_sc.shape, jnp.float32)

    def update(diagonal):
        qt = qt_ref[...]
        k = k_ref[...]
        v = v_ref[...]
        feature = lax.broadcasted_iota(jnp.int32, (width, rows), 0)
        key_index = lax.broadcasted_iota(jnp.int32, (span, 1), 0)
        bias = jnp.where(key_index < lengths_ref[step], 0.0, MASKED_SCORE).astype(jnp.float32)
        if diagonal:
            causal = lax.broadcasted_iota(jnp.int32, (span, rows), 0) <= lax.broadcasted_iota(
                jnp.int32, (span, rows), 1
            )
        for h in range(heads):
            in_head = (feature >= h * HEAD) & (feature < (h + 1) * HEAD)
            qt_head = jnp.where(in_head, qt, jnp.zeros_like(qt))
            scores = jnp.dot(k, qt_head, preferred_element_type=jnp.float32) * score_scale + bias
            if diagonal:
                scores = jnp.where(causal, scores, MASKED_SCORE)
            m_prev = m_sc[h]
            m_new = jnp.maximum(m_prev, jnp.max(scores, axis=0, keepdims=True))
            weights = jnp.exp(scores - m_new)
            alpha = jnp.exp(m_prev - m_new)
            l_sc[h] = alpha * l_sc[h] + jnp.sum(weights, axis=0, keepdims=True)
            mixed = lax.dot_general(
                v,
                weights.astype(jnp.bfloat16),
                (((0,), (0,)), ((), ())),
                preferred_element_type=jnp.float32,
            )
            acc_sc[h] = acc_sc[h] * alpha + mixed
            m_sc[h] = m_new

    @pl.when(step < seq)
    def _():
        update(False)

    @pl.when(step == seq)
    def _():
        update(True)

    @pl.when(step == pl.num_programs(0) - 1)
    def _():
        feature = lax.broadcasted_iota(jnp.int32, (width, rows), 0)
        result = jnp.zeros((width, rows), jnp.float32)
        for h in range(heads):
            in_head = (feature >= h * HEAD) & (feature < (h + 1) * HEAD)
            result = jnp.where(in_head, acc_sc[h] / l_sc[h], result)
        o_ref[...] = result


def causal_attention(query_flat, key_value_all, seq_index, block_lengths, rows_per_block):
    rows, width = query_flat.shape
    span = rows_per_block
    steps = key_value_all.shape[0] // (2 * span)
    heads = width // HEAD
    meta = jnp.reshape(seq_index, (1,)).astype(jnp.int32)
    grid_spec = pltpu.PrefetchScalarGridSpec(
        num_scalar_prefetch=2,
        grid=(steps,),
        in_specs=[
            pl.BlockSpec((width, rows), lambda i, m, n: (0, 0)),
            pl.BlockSpec((span, width), lambda i, m, n: (2 * jnp.minimum(i, m[0]), 0)),
            pl.BlockSpec((span, width), lambda i, m, n: (2 * jnp.minimum(i, m[0]) + 1, 0)),
        ],
        out_specs=pl.BlockSpec((width, rows), lambda i, m, n: (0, 0)),
        scratch_shapes=[
            pltpu.VMEM((heads, 1, rows), jnp.float32),
            pltpu.VMEM((heads, 1, rows), jnp.float32),
            pltpu.VMEM((heads, width, rows), jnp.float32),
        ],
    )
    keys_total = steps * span
    result = pl.pallas_call(
        attention_kernel,
        grid_spec=grid_spec,
        out_shape=jax.ShapeDtypeStruct((width, rows), jnp.float32),
        compiler_params=pltpu.CompilerParams(dimension_semantics=("arbitrary",)),
        cost_estimate=pl.CostEstimate(
            flops=4 * heads * rows * keys_total * width,
            transcendentals=heads * rows * keys_total,
            bytes_accessed=key_value_all.size * 2 + 3 * query_flat.size * 2,
        ),
    )(meta, block_lengths, jnp.transpose(query_flat), key_value_all, key_value_all)
    return jnp.transpose(result).astype(jnp.bfloat16)


def shards(
    pixels,
    text_rows,
    patch_counts,
    picture_starts,
    block_lengths,
    vision_gain,
    vision_project,
    vision_output,
    merge_gain,
    merge_weight,
    text_gain,
    text_project,
    text_output,
):
    seq_ways = lax.axis_size("seq")
    tp_ways = lax.axis_size("tp")
    seq_index = lax.axis_index("seq")
    tp_index = lax.axis_index("tp")
    picture_total, local_patches, model_width = pixels.shape
    patch_total = local_patches * tp_ways
    local_width = vision_project.shape[2]
    head_count = local_width // HEAD
    patch_normed = layer_normed(pixels, vision_gain).astype(jnp.bfloat16)
    packed_project = vision_project.reshape(model_width, 3 * local_width)
    projected = jnp.einsum(
        "npd,de->npe",
        gathered_patches(patch_normed, 0),
        packed_project,
        preferred_element_type=jnp.float32,
    ).astype(jnp.bfloat16)
    queries = projected[..., :local_width].reshape(picture_total, patch_total, head_count, HEAD)
    key_heads = projected[..., local_width : 2 * local_width].reshape(
        picture_total, patch_total, head_count, HEAD
    )
    value_heads = projected[..., 2 * local_width :].reshape(
        picture_total, patch_total, head_count, HEAD
    )
    live_counts = lax.dynamic_slice_in_dim(
        patch_counts, seq_index * picture_total, picture_total, 0
    )
    score_scale = 1.0 / math.sqrt(HEAD)
    scores = (
        jnp.einsum("nqhd,nkhd->nhqk", queries, key_heads, preferred_element_type=jnp.float32)
        * score_scale
    )
    allowed = (jnp.arange(patch_total, dtype=jnp.int32)[None, :] < live_counts[:, None])[
        :, None, None, :
    ]
    scores = jnp.where(allowed, scores, MASKED_SCORE)
    highest = jnp.max(scores, -1, keepdims=True)
    weights = jnp.where(allowed, jnp.exp(scores - highest), 0.0)
    mixture = jnp.einsum(
        "nhqk,nkhd->nqhd",
        weights.astype(jnp.bfloat16),
        value_heads,
        preferred_element_type=jnp.float32,
    )
    mixture = mixture / jnp.transpose(jnp.sum(weights, -1), (0, 2, 1))[..., None]
    attended = mixture.astype(jnp.bfloat16).reshape(picture_total, patch_total, local_width)
    patch_major = jnp.transpose(attended, (1, 0, 2)).reshape(
        patch_total * picture_total, local_width
    )

    def vision_term(offset, row_count):
        return jnp.dot(patch_major, vision_output, preferred_element_type=jnp.float32)

    vision_sum = summed_rows(vision_term, local_patches * picture_total, 2)
    vision_sum = jnp.transpose(
        vision_sum.reshape(local_patches, picture_total, model_width), (1, 0, 2)
    )
    vision_rows = (pixels.astype(jnp.float32) + vision_sum).astype(jnp.bfloat16)
    merge_input = layer_normed(vision_rows, merge_gain).astype(jnp.bfloat16)
    merged_total = patch_total // 4
    input_share = merge_weight.shape[0]
    whole_pictures = gathered_patches(merge_input, 1)
    merged_rows = whole_pictures.reshape(picture_total * merged_total, 4 * model_width)
    owned_inputs = lax.dynamic_slice_in_dim(merged_rows, tp_index * input_share, input_share, 1)

    def merge_term(offset, row_count):
        return jnp.dot(owned_inputs, merge_weight, preferred_element_type=jnp.float32)

    part_rows = picture_total * merged_total // tp_ways
    visual_part = summed_rows(merge_term, part_rows, 3).astype(jnp.bfloat16)
    rows_per_block = text_rows.shape[0] * tp_ways
    start_table = picture_starts.reshape(seq_ways, picture_total)
    dest_table = start_table // rows_per_block
    picture_rank = tp_index * part_rows // merged_total
    rank_dest = jnp.sum(
        jnp.where(
            jnp.arange(picture_total, dtype=jnp.int32)[None, :] == picture_rank, dest_table, 0
        ),
        1,
    )
    senders = rank_dest == seq_index
    segment = tp_exchange(visual_part, seq_ways, True, 6, "seq").reshape(-1, model_width)
    row_count = segment.shape[0]
    sources = jnp.arange(row_count, dtype=jnp.int32) // part_rows
    wanted = jnp.any(
        (sources[:, None] == jnp.arange(seq_ways, dtype=jnp.int32)[None, :]) & senders[None, :], 1
    )
    selector = (
        (jnp.arange(row_count, dtype=jnp.int32) % part_rows)[None, :]
        == jnp.arange(part_rows, dtype=jnp.int32)[:, None]
    ) & wanted[None, :]
    arrived = jnp.dot(
        selector.astype(jnp.bfloat16), segment, preferred_element_type=jnp.float32
    ).astype(jnp.bfloat16)
    both_blocks = tp_exchange(jnp.concatenate([text_rows, arrived], 0), tp_ways, True, 5)
    text_block = both_blocks[:, : text_rows.shape[0]].reshape(-1, model_width)
    visual_block = both_blocks[:, text_rows.shape[0] :].reshape(-1, model_width)
    landed = dest_table == seq_index
    local_starts = jnp.sum(jnp.where(landed, start_table - seq_index * rows_per_block, 0), 0)
    live_groups = jnp.sum(
        jnp.where(landed, patch_counts.reshape(seq_ways, picture_total) // 4, 0), 0
    )
    slot_index = jnp.arange(merged_total, dtype=jnp.int32)
    targets = (local_starts[:, None] + slot_index[None, :]).reshape(-1)
    in_use = (slot_index[None, :] < live_groups[:, None]).reshape(-1)
    placement = (jnp.arange(rows_per_block, dtype=jnp.int32)[:, None] == targets[None, :]) & in_use[
        None, :
    ]
    covered = jnp.any(placement, 1)
    placed = jnp.dot(
        placement.astype(jnp.bfloat16), visual_block, preferred_element_type=jnp.float32
    ).astype(jnp.bfloat16)
    embedded = jnp.where(covered[:, None], placed, text_block)
    text_normed = rms_normed(embedded, text_gain).astype(jnp.bfloat16)
    text_heads = jnp.dot(
        text_normed,
        text_project.reshape(model_width, 3 * local_width),
        preferred_element_type=jnp.float32,
    )
    positions = seq_index * rows_per_block + jnp.arange(rows_per_block, dtype=jnp.int32)
    query_rows = rotary(
        text_heads[:, :local_width].reshape(rows_per_block, head_count, HEAD), positions
    ).astype(jnp.bfloat16)
    key_rows = rotary(
        text_heads[:, local_width : 2 * local_width].reshape(rows_per_block, head_count, HEAD),
        positions,
    ).astype(jnp.bfloat16)
    value_rows = text_heads[:, 2 * local_width :].astype(jnp.bfloat16)
    key_flat = key_rows.reshape(rows_per_block, local_width)
    key_value_all = lax.all_gather(
        jnp.concatenate([key_flat, value_rows], 0), "seq", axis=0, tiled=True
    )
    attended_rows = causal_attention(
        query_rows.reshape(rows_per_block, local_width),
        key_value_all,
        seq_index,
        block_lengths,
        rows_per_block,
    )
    own_rows = text_rows.shape[0]

    def text_term(offset, row_count):
        return jnp.dot(attended_rows, text_output, preferred_element_type=jnp.float32)

    text_sum = summed_rows(text_term, own_rows, 4)
    residual = lax.dynamic_slice_in_dim(embedded, tp_index * own_rows, own_rows, 0)
    hidden = (residual.astype(jnp.float32) + text_sum).astype(jnp.bfloat16)
    return (hidden, key_flat, value_rows)


def solution(mesh):
    placed = (
        P("seq", "tp", None),
        P(("seq", "tp"), None),
        P(),
        P(),
        P(),
        P(),
        P(None, None, "tp"),
        P("tp", None),
        P(),
        P("tp", None),
        P(),
        P(None, None, "tp"),
        P("tp", None),
    )
    return jax.shard_map(
        shards,
        mesh=mesh,
        in_specs=placed,
        out_specs=(P(("seq", "tp"), None), P("seq", "tp"), P("seq", "tp")),
        check_vma=False,
    )
```

```python
import functools
import math

import jax
import jax.numpy as jnp
from jax import lax
from jax.experimental import pallas as pl
from jax.experimental.pallas import tpu as pltpu
from jax.sharding import PartitionSpec as P

HEAD = 104


LN_EPS = 1e-05
RMS_EPS = 1e-06
MASKED_SCORE = -1e30
KEY_SPAN = 512


def layer_normed(row_values, gain_vector):
    floats = row_values.astype(jnp.float32)
    centre = floats - jnp.mean(floats, -1, keepdims=True)
    spread = jnp.mean(centre * centre, -1, keepdims=True)
    return centre * lax.rsqrt(spread + LN_EPS) * gain_vector


def rms_normed(row_values, gain_vector):
    floats = row_values.astype(jnp.float32)
    return floats * lax.rsqrt(jnp.mean(floats * floats, -1, keepdims=True) + RMS_EPS) * gain_vector


def rotary(heads_in, positions):
    halfway = heads_in.shape[-1] // 2
    rates = 10000.0 ** (-2.0 * jnp.arange(halfway, dtype=jnp.float32) / heads_in.shape[-1])
    angles = positions.astype(jnp.float32)[:, None] * rates[None, :]
    cosine_table = jnp.cos(angles)[:, None, :]
    sine_table = jnp.sin(angles)[:, None, :]
    leading = heads_in[..., :halfway]
    trailing = heads_in[..., halfway:]
    return jnp.concatenate(
        [
            leading * cosine_table - trailing * sine_table,
            trailing * cosine_table + leading * sine_table,
        ],
        -1,
    )


MESH_IDS = pl.DeviceIdType.MESH


def exchange_kernel(ways, gather, x_ref, y_ref, send_sem, recv_sem, local_sem):
    me = lax.axis_index("tp")
    row = lax.axis_index("seq")
    barrier = pltpu.get_barrier_semaphore()
    for shift in range(1, ways):
        peer = lax.rem(me + shift, ways)
        pl.semaphore_signal(barrier, inc=1, device_id=(row, peer), device_id_type=MESH_IDS)
    pl.semaphore_wait(barrier, ways - 1)
    sends = []
    for shift in range(1, ways):
        peer = lax.rem(me + shift, ways)
        copy = pltpu.make_async_remote_copy(
            src_ref=x_ref if gather else x_ref.at[peer],
            dst_ref=y_ref.at[me],
            send_sem=send_sem.at[shift],
            recv_sem=recv_sem.at[shift],
            device_id=(row, peer),
            device_id_type=MESH_IDS,
        )
        copy.start()
        sends.append(copy)
    local = pltpu.make_async_copy(x_ref if gather else x_ref.at[me], y_ref.at[me], local_sem)
    local.start()
    for copy in sends:
        copy.wait_send()
    for shift in range(1, ways):
        source = lax.rem(me + ways - shift, ways)
        arriving = pltpu.make_async_remote_copy(
            src_ref=x_ref if gather else x_ref.at[source],
            dst_ref=y_ref.at[source],
            send_sem=send_sem.at[shift],
            recv_sem=recv_sem.at[shift],
            device_id=(row, source),
            device_id_type=MESH_IDS,
        )
        arriving.wait_recv()
    local.wait()


def tp_exchange(x, ways, gather, collective_id):
    piece = x.shape if gather else x.shape[1:]
    return pl.pallas_call(
        functools.partial(exchange_kernel, ways, gather),
        out_shape=jax.ShapeDtypeStruct((ways,) + tuple(piece), x.dtype),
        in_specs=[pl.BlockSpec(memory_space=pl.ANY)],
        out_specs=pl.BlockSpec(memory_space=pl.ANY),
        scratch_shapes=[
            pltpu.SemaphoreType.DMA((ways,)),
            pltpu.SemaphoreType.DMA((ways,)),
            pltpu.SemaphoreType.DMA(()),
        ],
        compiler_params=pltpu.CompilerParams(collective_id=collective_id, has_side_effects=True),
    )(x)


def summed_rows(term_task, own_rows, collective_id):
    ways = lax.axis_size("tp")
    partial = term_task(jnp.int32(0), own_rows * ways)
    pieces = partial.reshape((ways, own_rows) + partial.shape[1:]).astype(jnp.bfloat16)
    arrived = tp_exchange(pieces, ways, False, collective_id)
    return jnp.sum(arrived.astype(jnp.float32), 0)


def gathered_patches(piece, collective_id):
    ways = lax.axis_size("tp")
    whole = tp_exchange(piece, ways, True, collective_id)
    return jnp.transpose(whole, (1, 0, 2, 3)).reshape(
        (piece.shape[0], ways * piece.shape[1]) + piece.shape[2:]
    )


def attention_kernel(meta_ref, lengths_ref, qt_ref, k_ref, v_ref, o_ref, m_sc, l_sc, acc_sc):
    step = pl.program_id(0)
    seq = meta_ref[0]
    width, rows = qt_ref.shape
    span = k_ref.shape[0]
    heads = width // HEAD
    score_scale = 1.0 / math.sqrt(HEAD)

    @pl.when(step == 0)
    def _():
        m_sc[...] = jnp.full(m_sc.shape, MASKED_SCORE, jnp.float32)
        l_sc[...] = jnp.zeros(l_sc.shape, jnp.float32)
        acc_sc[...] = jnp.zeros(acc_sc.shape, jnp.float32)

    def update(diagonal):
        qt = qt_ref[...]
        k = k_ref[...]
        v = v_ref[...]
        feature = lax.broadcasted_iota(jnp.int32, (width, rows), 0)
        key_index = lax.broadcasted_iota(jnp.int32, (span, 1), 0)
        bias = jnp.where(key_index < lengths_ref[step], 0.0, MASKED_SCORE).astype(jnp.float32)
        if diagonal:
            causal = lax.broadcasted_iota(jnp.int32, (span, rows), 0) <= lax.broadcasted_iota(
                jnp.int32, (span, rows), 1
            )
        for h in range(heads):
            in_head = (feature >= h * HEAD) & (feature < (h + 1) * HEAD)
            qt_head = jnp.where(in_head, qt, jnp.zeros_like(qt))
            scores = jnp.dot(k, qt_head, preferred_element_type=jnp.float32) * score_scale + bias
            if diagonal:
                scores = jnp.where(causal, scores, MASKED_SCORE)
            m_prev = m_sc[h]
            m_new = jnp.maximum(m_prev, jnp.max(scores, axis=0, keepdims=True))
            weights = jnp.exp(scores - m_new)
            alpha = jnp.exp(m_prev - m_new)
            l_sc[h] = alpha * l_sc[h] + jnp.sum(weights, axis=0, keepdims=True)
            mixed = lax.dot_general(
                v,
                weights.astype(jnp.bfloat16),
                (((0,), (0,)), ((), ())),
                preferred_element_type=jnp.float32,
            )
            acc_sc[h] = acc_sc[h] * alpha + mixed
            m_sc[h] = m_new

    @pl.when(step < seq)
    def _():
        update(False)

    @pl.when(step == seq)
    def _():
        update(True)

    @pl.when(step == pl.num_programs(0) - 1)
    def _():
        feature = lax.broadcasted_iota(jnp.int32, (width, rows), 0)
        result = jnp.zeros((width, rows), jnp.float32)
        for h in range(heads):
            in_head = (feature >= h * HEAD) & (feature < (h + 1) * HEAD)
            result = jnp.where(in_head, acc_sc[h] / l_sc[h], result)
        o_ref[...] = result


def causal_attention(query_flat, key_value_all, seq_index, block_lengths, rows_per_block):
    rows, width = query_flat.shape
    span = rows_per_block
    steps = key_value_all.shape[0] // (2 * span)
    heads = width // HEAD
    meta = jnp.reshape(seq_index, (1,)).astype(jnp.int32)
    grid_spec = pltpu.PrefetchScalarGridSpec(
        num_scalar_prefetch=2,
        grid=(steps,),
        in_specs=[
            pl.BlockSpec((width, rows), lambda i, m, n: (0, 0)),
            pl.BlockSpec((span, width), lambda i, m, n: (2 * jnp.minimum(i, m[0]), 0)),
            pl.BlockSpec((span, width), lambda i, m, n: (2 * jnp.minimum(i, m[0]) + 1, 0)),
        ],
        out_specs=pl.BlockSpec((width, rows), lambda i, m, n: (0, 0)),
        scratch_shapes=[
            pltpu.VMEM((heads, 1, rows), jnp.float32),
            pltpu.VMEM((heads, 1, rows), jnp.float32),
            pltpu.VMEM((heads, width, rows), jnp.float32),
        ],
    )
    keys_total = steps * span
    result = pl.pallas_call(
        attention_kernel,
        grid_spec=grid_spec,
        out_shape=jax.ShapeDtypeStruct((width, rows), jnp.float32),
        compiler_params=pltpu.CompilerParams(dimension_semantics=("arbitrary",)),
        cost_estimate=pl.CostEstimate(
            flops=4 * heads * rows * keys_total * width,
            transcendentals=heads * rows * keys_total,
            bytes_accessed=key_value_all.size * 2 + 3 * query_flat.size * 2,
        ),
    )(meta, block_lengths, jnp.transpose(query_flat), key_value_all, key_value_all)
    return jnp.transpose(result).astype(jnp.bfloat16)


def shards(
    pixels,
    text_rows,
    patch_counts,
    picture_starts,
    block_lengths,
    vision_gain,
    vision_project,
    vision_output,
    merge_gain,
    merge_weight,
    text_gain,
    text_project,
    text_output,
):
    seq_ways = lax.axis_size("seq")
    tp_ways = lax.axis_size("tp")
    seq_index = lax.axis_index("seq")
    tp_index = lax.axis_index("tp")
    picture_total, local_patches, model_width = pixels.shape
    patch_total = local_patches * tp_ways
    local_width = vision_project.shape[2]
    head_count = local_width // HEAD
    model_width = pixels.shape[2]
    rows_per_block = text_rows.shape[0] * tp_ways
    text_block = lax.all_gather(text_rows, "tp", axis=0, tiled=True)
    packed_text = text_project.reshape(model_width, 3 * local_width)
    positions = seq_index * rows_per_block + jnp.arange(rows_per_block, dtype=jnp.int32)

    def block_heads(rows_in):
        normed = rms_normed(rows_in, text_gain).astype(jnp.bfloat16)
        return jnp.dot(normed, packed_text, preferred_element_type=jnp.float32)

    def keys_and_values(heads_in):
        keys = rotary(
            heads_in[:, local_width : 2 * local_width].reshape(rows_per_block, head_count, HEAD),
            positions,
        ).astype(jnp.bfloat16)
        return keys.reshape(rows_per_block, local_width), heads_in[:, 2 * local_width :].astype(
            jnp.bfloat16
        )

    early_key, early_value = keys_and_values(block_heads(text_block))
    early_operand, pixels = lax.optimization_barrier(
        (jnp.concatenate([early_key, early_value], 0), pixels)
    )
    early_all = lax.all_gather(early_operand, "seq", axis=0, tiled=True)
    patch_normed = layer_normed(pixels, vision_gain).astype(jnp.bfloat16)
    packed_project = vision_project.reshape(model_width, 3 * local_width)
    projected = jnp.einsum(
        "npd,de->npe",
        gathered_patches(patch_normed, 0),
        packed_project,
        preferred_element_type=jnp.float32,
    ).astype(jnp.bfloat16)
    queries = projected[..., :local_width].reshape(picture_total, patch_total, head_count, HEAD)
    key_heads = projected[..., local_width : 2 * local_width].reshape(
        picture_total, patch_total, head_count, HEAD
    )
    value_heads = projected[..., 2 * local_width :].reshape(
        picture_total, patch_total, head_count, HEAD
    )
    live_counts = lax.dynamic_slice_in_dim(
        patch_counts, seq_index * picture_total, picture_total, 0
    )
    score_scale = 1.0 / math.sqrt(HEAD)
    scores = (
        jnp.einsum("nqhd,nkhd->nhqk", queries, key_heads, preferred_element_type=jnp.float32)
        * score_scale
    )
    allowed = (jnp.arange(patch_total, dtype=jnp.int32)[None, :] < live_counts[:, None])[
        :, None, None, :
    ]
    scores = jnp.where(allowed, scores, MASKED_SCORE)
    highest = jnp.max(scores, -1, keepdims=True)
    weights = jnp.where(allowed, jnp.exp(scores - highest), 0.0)
    mixture = jnp.einsum(
        "nhqk,nkhd->nqhd",
        weights.astype(jnp.bfloat16),
        value_heads,
        preferred_element_type=jnp.float32,
    )
    mixture = mixture / jnp.transpose(jnp.sum(weights, -1), (0, 2, 1))[..., None]
    attended = mixture.astype(jnp.bfloat16).reshape(picture_total, patch_total, local_width)
    patch_major = jnp.transpose(attended, (1, 0, 2)).reshape(
        patch_total * picture_total, local_width
    )

    def vision_term(offset, row_count):
        return jnp.dot(patch_major, vision_output, preferred_element_type=jnp.float32)

    vision_sum = summed_rows(vision_term, local_patches * picture_total, 2)
    vision_sum = jnp.transpose(
        vision_sum.reshape(local_patches, picture_total, model_width), (1, 0, 2)
    )
    vision_rows = (pixels.astype(jnp.float32) + vision_sum).astype(jnp.bfloat16)
    merge_input = layer_normed(vision_rows, merge_gain).astype(jnp.bfloat16)
    merged_total = patch_total // 4
    input_share = merge_weight.shape[0]
    whole_pictures = gathered_patches(merge_input, 1)
    merged_rows = whole_pictures.reshape(picture_total * merged_total, 4 * model_width)
    owned_inputs = lax.dynamic_slice_in_dim(merged_rows, tp_index * input_share, input_share, 1)

    def merge_term(offset, row_count):
        return jnp.dot(owned_inputs, merge_weight, preferred_element_type=jnp.float32)

    part_rows = picture_total * merged_total // tp_ways
    visual_part = summed_rows(merge_term, part_rows, 3).astype(jnp.bfloat16)
    early_all, visual_part = lax.optimization_barrier((early_all, visual_part))
    rows_per_block = text_rows.shape[0] * tp_ways
    start_table = picture_starts.reshape(seq_ways, picture_total)
    dest_table = start_table // rows_per_block
    picture_rank = tp_index * part_rows // merged_total
    rank_dest = jnp.sum(
        jnp.where(
            jnp.arange(picture_total, dtype=jnp.int32)[None, :] == picture_rank, dest_table, 0
        ),
        1,
    )
    senders = rank_dest == seq_index
    segment = lax.all_gather(visual_part, "seq", axis=0, tiled=True)
    row_count = segment.shape[0]
    sources = jnp.arange(row_count, dtype=jnp.int32) // part_rows
    wanted = jnp.any(
        (sources[:, None] == jnp.arange(seq_ways, dtype=jnp.int32)[None, :]) & senders[None, :], 1
    )
    selector = (
        (jnp.arange(row_count, dtype=jnp.int32) % part_rows)[None, :]
        == jnp.arange(part_rows, dtype=jnp.int32)[:, None]
    ) & wanted[None, :]
    arrived = jnp.dot(
        selector.astype(jnp.bfloat16), segment, preferred_element_type=jnp.float32
    ).astype(jnp.bfloat16)
    visual_block = tp_exchange(arrived, tp_ways, True, 5).reshape(-1, model_width)
    landed = dest_table == seq_index
    local_starts = jnp.sum(jnp.where(landed, start_table - seq_index * rows_per_block, 0), 0)
    live_groups = jnp.sum(
        jnp.where(landed, patch_counts.reshape(seq_ways, picture_total) // 4, 0), 0
    )
    slot_index = jnp.arange(merged_total, dtype=jnp.int32)
    targets = (local_starts[:, None] + slot_index[None, :]).reshape(-1)
    in_use = (slot_index[None, :] < live_groups[:, None]).reshape(-1)
    row_index = jnp.arange(rows_per_block, dtype=jnp.int32)
    placement = (row_index[:, None] == targets[None, :]) & in_use[None, :]
    covered = jnp.any(placement, 1)
    placed = jnp.dot(
        placement.astype(jnp.bfloat16), visual_block, preferred_element_type=jnp.float32
    ).astype(jnp.bfloat16)
    embedded = jnp.where(covered[:, None], placed, text_block)
    text_heads = block_heads(embedded)
    query_rows = rotary(
        text_heads[:, :local_width].reshape(rows_per_block, head_count, HEAD), positions
    ).astype(jnp.bfloat16)
    key_flat, value_rows = keys_and_values(text_heads)
    pick = (targets[:, None] == row_index[None, :]).astype(jnp.bfloat16)
    picture_kv = jnp.concatenate(
        [
            jnp.dot(pick, key_flat, preferred_element_type=jnp.float32),
            jnp.dot(pick, value_rows, preferred_element_type=jnp.float32),
        ],
        0,
    ).astype(jnp.bfloat16)
    picture_all = lax.all_gather(picture_kv, "seq", axis=0, tiled=True).reshape(
        seq_ways, 2, picture_total * merged_total, local_width
    )
    block_ids = jnp.arange(seq_ways, dtype=jnp.int32)
    landed_all = dest_table[None, :, :] == block_ids[:, None, None]
    starts_all = jnp.sum(
        jnp.where(landed_all, start_table[None] - block_ids[:, None, None] * rows_per_block, 0), 1
    )
    live_all = jnp.sum(
        jnp.where(landed_all, patch_counts.reshape(seq_ways, picture_total)[None] // 4, 0), 1
    )
    targets_all = (starts_all[:, :, None] + slot_index[None, None, :]).reshape(seq_ways, -1)
    in_use_all = (slot_index[None, None, :] < live_all[:, :, None]).reshape(seq_ways, -1)
    placement_all = (row_index[None, :, None] == targets_all[:, None, :]) & in_use_all[:, None, :]
    covered_all = jnp.any(placement_all, 2)
    patched = jnp.einsum(
        "brs,bksd->bkrd",
        placement_all.astype(jnp.bfloat16),
        picture_all,
        preferred_element_type=jnp.float32,
    ).astype(jnp.bfloat16)
    key_value_all = jnp.where(
        covered_all[:, None, :, None],
        patched,
        early_all.reshape(seq_ways, 2, rows_per_block, local_width),
    ).reshape(-1, local_width)
    attended_rows = causal_attention(
        query_rows.reshape(rows_per_block, local_width),
        key_value_all,
        seq_index,
        block_lengths,
        rows_per_block,
    )
    own_rows = text_rows.shape[0]

    def text_term(offset, row_count):
        return jnp.dot(attended_rows, text_output, preferred_element_type=jnp.float32)

    text_sum = summed_rows(text_term, own_rows, 4)
    residual = lax.dynamic_slice_in_dim(embedded, tp_index * own_rows, own_rows, 0)
    hidden = (residual.astype(jnp.float32) + text_sum).astype(jnp.bfloat16)
    return (hidden, key_flat, value_rows)


def solution(mesh):
    placed = (
        P("seq", "tp", None),
        P(("seq", "tp"), None),
        P(),
        P(),
        P(),
        P(),
        P(None, None, "tp"),
        P("tp", None),
        P(),
        P("tp", None),
        P(),
        P(None, None, "tp"),
        P("tp", None),
    )
    return jax.shard_map(
        shards,
        mesh=mesh,
        in_specs=placed,
        out_specs=(P(("seq", "tp"), None), P("seq", "tp"), P("seq", "tp")),
        check_vma=False,
    )
```

```python
import functools
import math

import jax
import jax.numpy as jnp
from jax import lax
from jax.experimental import pallas as pl
from jax.experimental.pallas import tpu as pltpu
from jax.sharding import PartitionSpec as P

HEAD = 104


LN_EPS = 1e-05
RMS_EPS = 1e-06
MASKED_SCORE = -1e30
KEY_SPAN = 512


def layer_normed(row_values, gain_vector):
    floats = row_values.astype(jnp.float32)
    centre = floats - jnp.mean(floats, -1, keepdims=True)
    spread = jnp.mean(centre * centre, -1, keepdims=True)
    return centre * lax.rsqrt(spread + LN_EPS) * gain_vector


def rms_normed(row_values, gain_vector):
    floats = row_values.astype(jnp.float32)
    return floats * lax.rsqrt(jnp.mean(floats * floats, -1, keepdims=True) + RMS_EPS) * gain_vector


def rotary(heads_in, positions):
    halfway = heads_in.shape[-1] // 2
    rates = 10000.0 ** (-2.0 * jnp.arange(halfway, dtype=jnp.float32) / heads_in.shape[-1])
    angles = positions.astype(jnp.float32)[:, None] * rates[None, :]
    cosine_table = jnp.cos(angles)[:, None, :]
    sine_table = jnp.sin(angles)[:, None, :]
    leading = heads_in[..., :halfway]
    trailing = heads_in[..., halfway:]
    return jnp.concatenate(
        [
            leading * cosine_table - trailing * sine_table,
            trailing * cosine_table + leading * sine_table,
        ],
        -1,
    )


MESH_IDS = pl.DeviceIdType.MESH


def exchange_kernel(axis, ways, stride, gather, x_ref, y_ref, send_sem, recv_sem, local_sem):
    position = lax.axis_index(axis)
    me = lax.rem(lax.div(position, stride), ways)
    base = position - me * stride
    other = lax.axis_index("seq" if axis == "tp" else "tp")

    def device(member):
        index = base + member * stride
        return (other, index) if axis == "tp" else (index, other)

    barrier = pltpu.get_barrier_semaphore()
    for shift in range(1, ways):
        peer = lax.rem(me + shift, ways)
        pl.semaphore_signal(barrier, inc=1, device_id=device(peer), device_id_type=MESH_IDS)
    pl.semaphore_wait(barrier, ways - 1)
    sends = []
    for shift in range(1, ways):
        peer = lax.rem(me + shift, ways)
        copy = pltpu.make_async_remote_copy(
            src_ref=x_ref if gather else x_ref.at[peer],
            dst_ref=y_ref.at[me],
            send_sem=send_sem.at[shift],
            recv_sem=recv_sem.at[shift],
            device_id=device(peer),
            device_id_type=MESH_IDS,
        )
        copy.start()
        sends.append(copy)
    local = pltpu.make_async_copy(x_ref if gather else x_ref.at[me], y_ref.at[me], local_sem)
    local.start()
    for copy in sends:
        copy.wait_send()
    for shift in range(1, ways):
        source = lax.rem(me + ways - shift, ways)
        arriving = pltpu.make_async_remote_copy(
            src_ref=x_ref if gather else x_ref.at[source],
            dst_ref=y_ref.at[source],
            send_sem=send_sem.at[shift],
            recv_sem=recv_sem.at[shift],
            device_id=device(source),
            device_id_type=MESH_IDS,
        )
        arriving.wait_recv()
    local.wait()


def tp_exchange(x, ways, gather, collective_id, axis="tp", stride=1):
    piece = x.shape if gather else x.shape[1:]
    return pl.pallas_call(
        functools.partial(exchange_kernel, axis, ways, stride, gather),
        out_shape=jax.ShapeDtypeStruct((ways,) + tuple(piece), x.dtype),
        in_specs=[pl.BlockSpec(memory_space=pl.ANY)],
        out_specs=pl.BlockSpec(memory_space=pl.ANY),
        scratch_shapes=[
            pltpu.SemaphoreType.DMA((ways,)),
            pltpu.SemaphoreType.DMA((ways,)),
            pltpu.SemaphoreType.DMA(()),
        ],
        compiler_params=pltpu.CompilerParams(collective_id=collective_id, has_side_effects=True),
    )(x)


def seq_gathered(piece, seq_ways, collective_ids):
    inner = math.gcd(seq_ways, 8)
    near = tp_exchange(piece, inner, True, collective_ids[0], "seq", 1)
    if seq_ways == inner:
        return near
    far = tp_exchange(near, seq_ways // inner, True, collective_ids[1], "seq", inner)
    return far.reshape((seq_ways,) + piece.shape)


def summed_rows(term_task, own_rows, collective_id):
    ways = lax.axis_size("tp")
    partial = term_task(jnp.int32(0), own_rows * ways)
    pieces = partial.reshape((ways, own_rows) + partial.shape[1:]).astype(jnp.bfloat16)
    arrived = tp_exchange(pieces, ways, False, collective_id)
    return jnp.sum(arrived.astype(jnp.float32), 0)


def gathered_patches(piece, collective_id):
    ways = lax.axis_size("tp")
    whole = tp_exchange(piece, ways, True, collective_id)
    return jnp.transpose(whole, (1, 0, 2, 3)).reshape(
        (piece.shape[0], ways * piece.shape[1]) + piece.shape[2:]
    )


def attention_kernel(meta_ref, lengths_ref, qt_ref, k_ref, v_ref, o_ref, m_sc, l_sc, acc_sc):
    step = pl.program_id(0)
    seq = meta_ref[0]
    width, rows = qt_ref.shape
    span = k_ref.shape[0]
    heads = width // HEAD
    score_scale = 1.0 / math.sqrt(HEAD)

    @pl.when(step == 0)
    def _():
        m_sc[...] = jnp.full(m_sc.shape, MASKED_SCORE, jnp.float32)
        l_sc[...] = jnp.zeros(l_sc.shape, jnp.float32)
        acc_sc[...] = jnp.zeros(acc_sc.shape, jnp.float32)

    def update(diagonal):
        qt = qt_ref[...]
        k = k_ref[...]
        v = v_ref[...]
        feature = lax.broadcasted_iota(jnp.int32, (width, rows), 0)
        key_index = lax.broadcasted_iota(jnp.int32, (span, 1), 0)
        bias = jnp.where(key_index < lengths_ref[step], 0.0, MASKED_SCORE).astype(jnp.float32)
        if diagonal:
            causal = lax.broadcasted_iota(jnp.int32, (span, rows), 0) <= lax.broadcasted_iota(
                jnp.int32, (span, rows), 1
            )
        for h in range(heads):
            in_head = (feature >= h * HEAD) & (feature < (h + 1) * HEAD)
            qt_head = jnp.where(in_head, qt, jnp.zeros_like(qt))
            scores = jnp.dot(k, qt_head, preferred_element_type=jnp.float32) * score_scale + bias
            if diagonal:
                scores = jnp.where(causal, scores, MASKED_SCORE)
            m_prev = m_sc[h]
            m_new = jnp.maximum(m_prev, jnp.max(scores, axis=0, keepdims=True))
            weights = jnp.exp(scores - m_new)
            alpha = jnp.exp(m_prev - m_new)
            l_sc[h] = alpha * l_sc[h] + jnp.sum(weights, axis=0, keepdims=True)
            mixed = lax.dot_general(
                v,
                weights.astype(jnp.bfloat16),
                (((0,), (0,)), ((), ())),
                preferred_element_type=jnp.float32,
            )
            acc_sc[h] = acc_sc[h] * alpha + mixed
            m_sc[h] = m_new

    @pl.when(step < seq)
    def _():
        update(False)

    @pl.when(step == seq)
    def _():
        update(True)

    @pl.when(step == pl.num_programs(0) - 1)
    def _():
        feature = lax.broadcasted_iota(jnp.int32, (width, rows), 0)
        result = jnp.zeros((width, rows), jnp.float32)
        for h in range(heads):
            in_head = (feature >= h * HEAD) & (feature < (h + 1) * HEAD)
            result = jnp.where(in_head, acc_sc[h] / l_sc[h], result)
        o_ref[...] = result


def causal_attention(query_flat, key_value_all, seq_index, block_lengths, rows_per_block):
    rows, width = query_flat.shape
    span = rows_per_block
    steps = key_value_all.shape[0] // (2 * span)
    heads = width // HEAD
    meta = jnp.reshape(seq_index, (1,)).astype(jnp.int32)
    grid_spec = pltpu.PrefetchScalarGridSpec(
        num_scalar_prefetch=2,
        grid=(steps,),
        in_specs=[
            pl.BlockSpec((width, rows), lambda i, m, n: (0, 0)),
            pl.BlockSpec((span, width), lambda i, m, n: (2 * jnp.minimum(i, m[0]), 0)),
            pl.BlockSpec((span, width), lambda i, m, n: (2 * jnp.minimum(i, m[0]) + 1, 0)),
        ],
        out_specs=pl.BlockSpec((width, rows), lambda i, m, n: (0, 0)),
        scratch_shapes=[
            pltpu.VMEM((heads, 1, rows), jnp.float32),
            pltpu.VMEM((heads, 1, rows), jnp.float32),
            pltpu.VMEM((heads, width, rows), jnp.float32),
        ],
    )
    keys_total = steps * span
    result = pl.pallas_call(
        attention_kernel,
        grid_spec=grid_spec,
        out_shape=jax.ShapeDtypeStruct((width, rows), jnp.float32),
        compiler_params=pltpu.CompilerParams(dimension_semantics=("arbitrary",)),
        cost_estimate=pl.CostEstimate(
            flops=4 * heads * rows * keys_total * width,
            transcendentals=heads * rows * keys_total,
            bytes_accessed=key_value_all.size * 2 + 3 * query_flat.size * 2,
        ),
    )(meta, block_lengths, jnp.transpose(query_flat), key_value_all, key_value_all)
    return jnp.transpose(result).astype(jnp.bfloat16)


def shards(
    pixels,
    text_rows,
    patch_counts,
    picture_starts,
    block_lengths,
    vision_gain,
    vision_project,
    vision_output,
    merge_gain,
    merge_weight,
    text_gain,
    text_project,
    text_output,
):
    seq_ways = lax.axis_size("seq")
    tp_ways = lax.axis_size("tp")
    seq_index = lax.axis_index("seq")
    tp_index = lax.axis_index("tp")
    picture_total, local_patches, model_width = pixels.shape
    patch_total = local_patches * tp_ways
    local_width = vision_project.shape[2]
    head_count = local_width // HEAD
    patch_normed = layer_normed(pixels, vision_gain).astype(jnp.bfloat16)
    packed_project = vision_project.reshape(model_width, 3 * local_width)
    projected = jnp.einsum(
        "npd,de->npe",
        gathered_patches(patch_normed, 0),
        packed_project,
        preferred_element_type=jnp.float32,
    ).astype(jnp.bfloat16)
    queries = projected[..., :local_width].reshape(picture_total, patch_total, head_count, HEAD)
    key_heads = projected[..., local_width : 2 * local_width].reshape(
        picture_total, patch_total, head_count, HEAD
    )
    value_heads = projected[..., 2 * local_width :].reshape(
        picture_total, patch_total, head_count, HEAD
    )
    live_counts = lax.dynamic_slice_in_dim(
        patch_counts, seq_index * picture_total, picture_total, 0
    )
    score_scale = 1.0 / math.sqrt(HEAD)
    scores = (
        jnp.einsum("nqhd,nkhd->nhqk", queries, key_heads, preferred_element_type=jnp.float32)
        * score_scale
    )
    allowed = (jnp.arange(patch_total, dtype=jnp.int32)[None, :] < live_counts[:, None])[
        :, None, None, :
    ]
    scores = jnp.where(allowed, scores, MASKED_SCORE)
    highest = jnp.max(scores, -1, keepdims=True)
    weights = jnp.where(allowed, jnp.exp(scores - highest), 0.0)
    mixture = jnp.einsum(
        "nhqk,nkhd->nqhd",
        weights.astype(jnp.bfloat16),
        value_heads,
        preferred_element_type=jnp.float32,
    )
    mixture = mixture / jnp.transpose(jnp.sum(weights, -1), (0, 2, 1))[..., None]
    attended = mixture.astype(jnp.bfloat16).reshape(picture_total, patch_total, local_width)
    patch_major = jnp.transpose(attended, (1, 0, 2)).reshape(
        patch_total * picture_total, local_width
    )

    def vision_term(offset, row_count):
        return jnp.dot(patch_major, vision_output, preferred_element_type=jnp.float32)

    vision_sum = summed_rows(vision_term, local_patches * picture_total, 2)
    vision_sum = jnp.transpose(
        vision_sum.reshape(local_patches, picture_total, model_width), (1, 0, 2)
    )
    vision_rows = (pixels.astype(jnp.float32) + vision_sum).astype(jnp.bfloat16)
    merge_input = layer_normed(vision_rows, merge_gain).astype(jnp.bfloat16)
    merged_total = patch_total // 4
    input_share = merge_weight.shape[0]
    whole_pictures = gathered_patches(merge_input, 1)
    merged_rows = whole_pictures.reshape(picture_total * merged_total, 4 * model_width)
    owned_inputs = lax.dynamic_slice_in_dim(merged_rows, tp_index * input_share, input_share, 1)

    def merge_term(offset, row_count):
        return jnp.dot(owned_inputs, merge_weight, preferred_element_type=jnp.float32)

    part_rows = picture_total * merged_total // tp_ways
    visual_part = summed_rows(merge_term, part_rows, 3).astype(jnp.bfloat16)
    rows_per_block = text_rows.shape[0] * tp_ways
    start_table = picture_starts.reshape(seq_ways, picture_total)
    dest_table = start_table // rows_per_block
    picture_rank = tp_index * part_rows // merged_total
    rank_dest = jnp.sum(
        jnp.where(
            jnp.arange(picture_total, dtype=jnp.int32)[None, :] == picture_rank, dest_table, 0
        ),
        1,
    )
    senders = rank_dest == seq_index
    segment = seq_gathered(visual_part, seq_ways, (6, 7)).reshape(-1, model_width)
    row_count = segment.shape[0]
    sources = jnp.arange(row_count, dtype=jnp.int32) // part_rows
    wanted = jnp.any(
        (sources[:, None] == jnp.arange(seq_ways, dtype=jnp.int32)[None, :]) & senders[None, :], 1
    )
    selector = (
        (jnp.arange(row_count, dtype=jnp.int32) % part_rows)[None, :]
        == jnp.arange(part_rows, dtype=jnp.int32)[:, None]
    ) & wanted[None, :]
    arrived = jnp.dot(
        selector.astype(jnp.bfloat16), segment, preferred_element_type=jnp.float32
    ).astype(jnp.bfloat16)
    text_block = lax.all_gather(text_rows, "tp", axis=0, tiled=True)
    visual_block = tp_exchange(arrived, tp_ways, True, 5).reshape(-1, model_width)
    landed = dest_table == seq_index
    local_starts = jnp.sum(jnp.where(landed, start_table - seq_index * rows_per_block, 0), 0)
    live_groups = jnp.sum(
        jnp.where(landed, patch_counts.reshape(seq_ways, picture_total) // 4, 0), 0
    )
    slot_index = jnp.arange(merged_total, dtype=jnp.int32)
    targets = (local_starts[:, None] + slot_index[None, :]).reshape(-1)
    in_use = (slot_index[None, :] < live_groups[:, None]).reshape(-1)
    placement = (jnp.arange(rows_per_block, dtype=jnp.int32)[:, None] == targets[None, :]) & in_use[
        None, :
    ]
    covered = jnp.any(placement, 1)
    placed = jnp.dot(
        placement.astype(jnp.bfloat16), visual_block, preferred_element_type=jnp.float32
    ).astype(jnp.bfloat16)
    embedded = jnp.where(covered[:, None], placed, text_block)
    text_normed = rms_normed(embedded, text_gain).astype(jnp.bfloat16)
    text_heads = jnp.dot(
        text_normed,
        text_project.reshape(model_width, 3 * local_width),
        preferred_element_type=jnp.float32,
    )
    positions = seq_index * rows_per_block + jnp.arange(rows_per_block, dtype=jnp.int32)
    query_rows = rotary(
        text_heads[:, :local_width].reshape(rows_per_block, head_count, HEAD), positions
    ).astype(jnp.bfloat16)
    key_rows = rotary(
        text_heads[:, local_width : 2 * local_width].reshape(rows_per_block, head_count, HEAD),
        positions,
    ).astype(jnp.bfloat16)
    value_rows = text_heads[:, 2 * local_width :].astype(jnp.bfloat16)
    key_flat = key_rows.reshape(rows_per_block, local_width)
    key_value_all = lax.all_gather(
        jnp.concatenate([key_flat, value_rows], 0), "seq", axis=0, tiled=True
    )
    attended_rows = causal_attention(
        query_rows.reshape(rows_per_block, local_width),
        key_value_all,
        seq_index,
        block_lengths,
        rows_per_block,
    )
    own_rows = text_rows.shape[0]

    def text_term(offset, row_count):
        return jnp.dot(attended_rows, text_output, preferred_element_type=jnp.float32)

    text_sum = summed_rows(text_term, own_rows, 4)
    residual = lax.dynamic_slice_in_dim(embedded, tp_index * own_rows, own_rows, 0)
    hidden = (residual.astype(jnp.float32) + text_sum).astype(jnp.bfloat16)
    return (hidden, key_flat, value_rows)


def solution(mesh):
    placed = (
        P("seq", "tp", None),
        P(("seq", "tp"), None),
        P(),
        P(),
        P(),
        P(),
        P(None, None, "tp"),
        P("tp", None),
        P(),
        P("tp", None),
        P(),
        P(None, None, "tp"),
        P("tp", None),
    )
    return jax.shard_map(
        shards,
        mesh=mesh,
        in_specs=placed,
        out_specs=(P(("seq", "tp"), None), P("seq", "tp"), P("seq", "tp")),
        check_vma=False,
    )
```

```python
import functools
import math

import jax
import jax.numpy as jnp
from jax import lax
from jax.experimental import pallas as pl
from jax.experimental.pallas import tpu as pltpu
from jax.sharding import PartitionSpec as P

HEAD = 104


LN_EPS = 1e-05
RMS_EPS = 1e-06
MASKED_SCORE = -1e30
KEY_SPAN = 512


def layer_normed(row_values, gain_vector):
    floats = row_values.astype(jnp.float32)
    centre = floats - jnp.mean(floats, -1, keepdims=True)
    spread = jnp.mean(centre * centre, -1, keepdims=True)
    return centre * lax.rsqrt(spread + LN_EPS) * gain_vector


def rms_normed(row_values, gain_vector):
    floats = row_values.astype(jnp.float32)
    return floats * lax.rsqrt(jnp.mean(floats * floats, -1, keepdims=True) + RMS_EPS) * gain_vector


def rotary(heads_in, positions):
    halfway = heads_in.shape[-1] // 2
    rates = 10000.0 ** (-2.0 * jnp.arange(halfway, dtype=jnp.float32) / heads_in.shape[-1])
    angles = positions.astype(jnp.float32)[:, None] * rates[None, :]
    cosine_table = jnp.cos(angles)[:, None, :]
    sine_table = jnp.sin(angles)[:, None, :]
    leading = heads_in[..., :halfway]
    trailing = heads_in[..., halfway:]
    return jnp.concatenate(
        [
            leading * cosine_table - trailing * sine_table,
            trailing * cosine_table + leading * sine_table,
        ],
        -1,
    )


MESH_IDS = pl.DeviceIdType.MESH


def exchange_kernel(axis, ways, stride, gather, x_ref, y_ref, send_sem, recv_sem, local_sem):
    position = lax.axis_index(axis)
    me = lax.rem(lax.div(position, stride), ways)
    base = position - me * stride
    other = lax.axis_index("seq" if axis == "tp" else "tp")

    def device(member):
        index = base + member * stride
        return (other, index) if axis == "tp" else (index, other)

    barrier = pltpu.get_barrier_semaphore()
    for shift in range(1, ways):
        peer = lax.rem(me + shift, ways)
        pl.semaphore_signal(barrier, inc=1, device_id=device(peer), device_id_type=MESH_IDS)
    pl.semaphore_wait(barrier, ways - 1)
    sends = []
    for shift in range(1, ways):
        peer = lax.rem(me + shift, ways)
        copy = pltpu.make_async_remote_copy(
            src_ref=x_ref if gather else x_ref.at[peer],
            dst_ref=y_ref.at[me],
            send_sem=send_sem.at[shift],
            recv_sem=recv_sem.at[shift],
            device_id=device(peer),
            device_id_type=MESH_IDS,
        )
        copy.start()
        sends.append(copy)
    local = pltpu.make_async_copy(x_ref if gather else x_ref.at[me], y_ref.at[me], local_sem)
    local.start()
    for copy in sends:
        copy.wait_send()
    for shift in range(1, ways):
        source = lax.rem(me + ways - shift, ways)
        arriving = pltpu.make_async_remote_copy(
            src_ref=x_ref if gather else x_ref.at[source],
            dst_ref=y_ref.at[source],
            send_sem=send_sem.at[shift],
            recv_sem=recv_sem.at[shift],
            device_id=device(source),
            device_id_type=MESH_IDS,
        )
        arriving.wait_recv()
    local.wait()


def tp_exchange(x, ways, gather, collective_id, axis="tp", stride=1):
    piece = x.shape if gather else x.shape[1:]
    return pl.pallas_call(
        functools.partial(exchange_kernel, axis, ways, stride, gather),
        out_shape=jax.ShapeDtypeStruct((ways,) + tuple(piece), x.dtype),
        in_specs=[pl.BlockSpec(memory_space=pl.ANY)],
        out_specs=pl.BlockSpec(memory_space=pl.ANY),
        scratch_shapes=[
            pltpu.SemaphoreType.DMA((ways,)),
            pltpu.SemaphoreType.DMA((ways,)),
            pltpu.SemaphoreType.DMA(()),
        ],
        compiler_params=pltpu.CompilerParams(collective_id=collective_id, has_side_effects=True),
    )(x)


def seq_gathered(piece, seq_ways, collective_ids):
    inner = math.gcd(seq_ways, 8)
    if seq_ways == inner:
        return tp_exchange(piece, inner, True, collective_ids[0], "seq", 1)
    far = tp_exchange(piece, seq_ways // inner, True, collective_ids[1], "seq", inner)
    near = tp_exchange(far, inner, True, collective_ids[0], "seq", 1)
    return jnp.swapaxes(near, 0, 1).reshape((seq_ways,) + piece.shape)


def summed_rows(term_task, own_rows, collective_id):
    ways = lax.axis_size("tp")
    partial = term_task(jnp.int32(0), own_rows * ways)
    pieces = partial.reshape((ways, own_rows) + partial.shape[1:]).astype(jnp.bfloat16)
    arrived = tp_exchange(pieces, ways, False, collective_id)
    return jnp.sum(arrived.astype(jnp.float32), 0)


def gathered_patches(piece, collective_id):
    ways = lax.axis_size("tp")
    whole = tp_exchange(piece, ways, True, collective_id)
    return jnp.transpose(whole, (1, 0, 2, 3)).reshape(
        (piece.shape[0], ways * piece.shape[1]) + piece.shape[2:]
    )


def attention_kernel(meta_ref, lengths_ref, qt_ref, k_ref, v_ref, o_ref, m_sc, l_sc, acc_sc):
    step = pl.program_id(0)
    seq = meta_ref[0]
    width, rows = qt_ref.shape
    span = k_ref.shape[0]
    heads = width // HEAD
    score_scale = 1.0 / math.sqrt(HEAD)

    @pl.when(step == 0)
    def _():
        m_sc[...] = jnp.full(m_sc.shape, MASKED_SCORE, jnp.float32)
        l_sc[...] = jnp.zeros(l_sc.shape, jnp.float32)
        acc_sc[...] = jnp.zeros(acc_sc.shape, jnp.float32)

    def update(diagonal):
        qt = qt_ref[...]
        k = k_ref[...]
        v = v_ref[...]
        feature = lax.broadcasted_iota(jnp.int32, (width, rows), 0)
        key_index = lax.broadcasted_iota(jnp.int32, (span, 1), 0)
        bias = jnp.where(key_index < lengths_ref[step], 0.0, MASKED_SCORE).astype(jnp.float32)
        if diagonal:
            causal = lax.broadcasted_iota(jnp.int32, (span, rows), 0) <= lax.broadcasted_iota(
                jnp.int32, (span, rows), 1
            )
        for h in range(heads):
            in_head = (feature >= h * HEAD) & (feature < (h + 1) * HEAD)
            qt_head = jnp.where(in_head, qt, jnp.zeros_like(qt))
            scores = jnp.dot(k, qt_head, preferred_element_type=jnp.float32) * score_scale + bias
            if diagonal:
                scores = jnp.where(causal, scores, MASKED_SCORE)
            m_prev = m_sc[h]
            m_new = jnp.maximum(m_prev, jnp.max(scores, axis=0, keepdims=True))
            weights = jnp.exp(scores - m_new)
            alpha = jnp.exp(m_prev - m_new)
            l_sc[h] = alpha * l_sc[h] + jnp.sum(weights, axis=0, keepdims=True)
            mixed = lax.dot_general(
                v,
                weights.astype(jnp.bfloat16),
                (((0,), (0,)), ((), ())),
                preferred_element_type=jnp.float32,
            )
            acc_sc[h] = acc_sc[h] * alpha + mixed
            m_sc[h] = m_new

    @pl.when(step < seq)
    def _():
        update(False)

    @pl.when(step == seq)
    def _():
        update(True)

    @pl.when(step == pl.num_programs(0) - 1)
    def _():
        feature = lax.broadcasted_iota(jnp.int32, (width, rows), 0)
        result = jnp.zeros((width, rows), jnp.float32)
        for h in range(heads):
            in_head = (feature >= h * HEAD) & (feature < (h + 1) * HEAD)
            result = jnp.where(in_head, acc_sc[h] / l_sc[h], result)
        o_ref[...] = result


def causal_attention(query_flat, key_value_all, seq_index, block_lengths, rows_per_block):
    rows, width = query_flat.shape
    span = rows_per_block
    steps = key_value_all.shape[0] // (2 * span)
    heads = width // HEAD
    meta = jnp.reshape(seq_index, (1,)).astype(jnp.int32)
    grid_spec = pltpu.PrefetchScalarGridSpec(
        num_scalar_prefetch=2,
        grid=(steps,),
        in_specs=[
            pl.BlockSpec((width, rows), lambda i, m, n: (0, 0)),
            pl.BlockSpec((span, width), lambda i, m, n: (2 * jnp.minimum(i, m[0]), 0)),
            pl.BlockSpec((span, width), lambda i, m, n: (2 * jnp.minimum(i, m[0]) + 1, 0)),
        ],
        out_specs=pl.BlockSpec((width, rows), lambda i, m, n: (0, 0)),
        scratch_shapes=[
            pltpu.VMEM((heads, 1, rows), jnp.float32),
            pltpu.VMEM((heads, 1, rows), jnp.float32),
            pltpu.VMEM((heads, width, rows), jnp.float32),
        ],
    )
    keys_total = steps * span
    result = pl.pallas_call(
        attention_kernel,
        grid_spec=grid_spec,
        out_shape=jax.ShapeDtypeStruct((width, rows), jnp.float32),
        compiler_params=pltpu.CompilerParams(dimension_semantics=("arbitrary",)),
        cost_estimate=pl.CostEstimate(
            flops=4 * heads * rows * keys_total * width,
            transcendentals=heads * rows * keys_total,
            bytes_accessed=key_value_all.size * 2 + 3 * query_flat.size * 2,
        ),
    )(meta, block_lengths, jnp.transpose(query_flat), key_value_all, key_value_all)
    return jnp.transpose(result).astype(jnp.bfloat16)


def shards(
    pixels,
    text_rows,
    patch_counts,
    picture_starts,
    block_lengths,
    vision_gain,
    vision_project,
    vision_output,
    merge_gain,
    merge_weight,
    text_gain,
    text_project,
    text_output,
):
    seq_ways = lax.axis_size("seq")
    tp_ways = lax.axis_size("tp")
    seq_index = lax.axis_index("seq")
    tp_index = lax.axis_index("tp")
    picture_total, local_patches, model_width = pixels.shape
    patch_total = local_patches * tp_ways
    local_width = vision_project.shape[2]
    head_count = local_width // HEAD
    patch_normed = layer_normed(pixels, vision_gain).astype(jnp.bfloat16)
    packed_project = vision_project.reshape(model_width, 3 * local_width)
    projected = jnp.einsum(
        "npd,de->npe",
        gathered_patches(patch_normed, 0),
        packed_project,
        preferred_element_type=jnp.float32,
    ).astype(jnp.bfloat16)
    queries = projected[..., :local_width].reshape(picture_total, patch_total, head_count, HEAD)
    key_heads = projected[..., local_width : 2 * local_width].reshape(
        picture_total, patch_total, head_count, HEAD
    )
    value_heads = projected[..., 2 * local_width :].reshape(
        picture_total, patch_total, head_count, HEAD
    )
    live_counts = lax.dynamic_slice_in_dim(
        patch_counts, seq_index * picture_total, picture_total, 0
    )
    score_scale = 1.0 / math.sqrt(HEAD)
    scores = (
        jnp.einsum("nqhd,nkhd->nhqk", queries, key_heads, preferred_element_type=jnp.float32)
        * score_scale
    )
    allowed = (jnp.arange(patch_total, dtype=jnp.int32)[None, :] < live_counts[:, None])[
        :, None, None, :
    ]
    scores = jnp.where(allowed, scores, MASKED_SCORE)
    highest = jnp.max(scores, -1, keepdims=True)
    weights = jnp.where(allowed, jnp.exp(scores - highest), 0.0)
    mixture = jnp.einsum(
        "nhqk,nkhd->nqhd",
        weights.astype(jnp.bfloat16),
        value_heads,
        preferred_element_type=jnp.float32,
    )
    mixture = mixture / jnp.transpose(jnp.sum(weights, -1), (0, 2, 1))[..., None]
    attended = mixture.astype(jnp.bfloat16).reshape(picture_total, patch_total, local_width)
    patch_major = jnp.transpose(attended, (1, 0, 2)).reshape(
        patch_total * picture_total, local_width
    )

    def vision_term(offset, row_count):
        return jnp.dot(patch_major, vision_output, preferred_element_type=jnp.float32)

    vision_sum = summed_rows(vision_term, local_patches * picture_total, 2)
    vision_sum = jnp.transpose(
        vision_sum.reshape(local_patches, picture_total, model_width), (1, 0, 2)
    )
    vision_rows = (pixels.astype(jnp.float32) + vision_sum).astype(jnp.bfloat16)
    merge_input = layer_normed(vision_rows, merge_gain).astype(jnp.bfloat16)
    merged_total = patch_total // 4
    input_share = merge_weight.shape[0]
    whole_pictures = gathered_patches(merge_input, 1)
    merged_rows = whole_pictures.reshape(picture_total * merged_total, 4 * model_width)
    owned_inputs = lax.dynamic_slice_in_dim(merged_rows, tp_index * input_share, input_share, 1)

    def merge_term(offset, row_count):
        return jnp.dot(owned_inputs, merge_weight, preferred_element_type=jnp.float32)

    part_rows = picture_total * merged_total // tp_ways
    visual_part = summed_rows(merge_term, part_rows, 3).astype(jnp.bfloat16)
    rows_per_block = text_rows.shape[0] * tp_ways
    start_table = picture_starts.reshape(seq_ways, picture_total)
    dest_table = start_table // rows_per_block
    picture_rank = tp_index * part_rows // merged_total
    rank_dest = jnp.sum(
        jnp.where(
            jnp.arange(picture_total, dtype=jnp.int32)[None, :] == picture_rank, dest_table, 0
        ),
        1,
    )
    senders = rank_dest == seq_index
    segment = seq_gathered(visual_part, seq_ways, (6, 7)).reshape(-1, model_width)
    row_count = segment.shape[0]
    sources = jnp.arange(row_count, dtype=jnp.int32) // part_rows
    wanted = jnp.any(
        (sources[:, None] == jnp.arange(seq_ways, dtype=jnp.int32)[None, :]) & senders[None, :], 1
    )
    selector = (
        (jnp.arange(row_count, dtype=jnp.int32) % part_rows)[None, :]
        == jnp.arange(part_rows, dtype=jnp.int32)[:, None]
    ) & wanted[None, :]
    arrived = jnp.dot(
        selector.astype(jnp.bfloat16), segment, preferred_element_type=jnp.float32
    ).astype(jnp.bfloat16)
    text_block = lax.all_gather(text_rows, "tp", axis=0, tiled=True)
    visual_block = tp_exchange(arrived, tp_ways, True, 5).reshape(-1, model_width)
    landed = dest_table == seq_index
    local_starts = jnp.sum(jnp.where(landed, start_table - seq_index * rows_per_block, 0), 0)
    live_groups = jnp.sum(
        jnp.where(landed, patch_counts.reshape(seq_ways, picture_total) // 4, 0), 0
    )
    slot_index = jnp.arange(merged_total, dtype=jnp.int32)
    targets = (local_starts[:, None] + slot_index[None, :]).reshape(-1)
    in_use = (slot_index[None, :] < live_groups[:, None]).reshape(-1)
    placement = (jnp.arange(rows_per_block, dtype=jnp.int32)[:, None] == targets[None, :]) & in_use[
        None, :
    ]
    covered = jnp.any(placement, 1)
    placed = jnp.dot(
        placement.astype(jnp.bfloat16), visual_block, preferred_element_type=jnp.float32
    ).astype(jnp.bfloat16)
    embedded = jnp.where(covered[:, None], placed, text_block)
    text_normed = rms_normed(embedded, text_gain).astype(jnp.bfloat16)
    text_heads = jnp.dot(
        text_normed,
        text_project.reshape(model_width, 3 * local_width),
        preferred_element_type=jnp.float32,
    )
    positions = seq_index * rows_per_block + jnp.arange(rows_per_block, dtype=jnp.int32)
    query_rows = rotary(
        text_heads[:, :local_width].reshape(rows_per_block, head_count, HEAD), positions
    ).astype(jnp.bfloat16)
    key_rows = rotary(
        text_heads[:, local_width : 2 * local_width].reshape(rows_per_block, head_count, HEAD),
        positions,
    ).astype(jnp.bfloat16)
    value_rows = text_heads[:, 2 * local_width :].astype(jnp.bfloat16)
    key_flat = key_rows.reshape(rows_per_block, local_width)
    key_value_all = lax.all_gather(
        jnp.concatenate([key_flat, value_rows], 0), "seq", axis=0, tiled=True
    )
    attended_rows = causal_attention(
        query_rows.reshape(rows_per_block, local_width),
        key_value_all,
        seq_index,
        block_lengths,
        rows_per_block,
    )
    own_rows = text_rows.shape[0]

    def text_term(offset, row_count):
        return jnp.dot(attended_rows, text_output, preferred_element_type=jnp.float32)

    text_sum = summed_rows(text_term, own_rows, 4)
    residual = lax.dynamic_slice_in_dim(embedded, tp_index * own_rows, own_rows, 0)
    hidden = (residual.astype(jnp.float32) + text_sum).astype(jnp.bfloat16)
    return (hidden, key_flat, value_rows)


def solution(mesh):
    placed = (
        P("seq", "tp", None),
        P(("seq", "tp"), None),
        P(),
        P(),
        P(),
        P(),
        P(None, None, "tp"),
        P("tp", None),
        P(),
        P("tp", None),
        P(),
        P(None, None, "tp"),
        P("tp", None),
    )
    return jax.shard_map(
        shards,
        mesh=mesh,
        in_specs=placed,
        out_specs=(P(("seq", "tp"), None), P("seq", "tp"), P("seq", "tp")),
        check_vma=False,
    )
```

```python
import functools
import math

import jax
import jax.numpy as jnp
from jax import lax
from jax.experimental import pallas as pl
from jax.experimental.pallas import tpu as pltpu
from jax.sharding import PartitionSpec as P

HEAD = 104


LN_EPS = 1e-05
RMS_EPS = 1e-06
MASKED_SCORE = -1e30
KEY_SPAN = 512


def layer_normed(row_values, gain_vector):
    floats = row_values.astype(jnp.float32)
    centre = floats - jnp.mean(floats, -1, keepdims=True)
    spread = jnp.mean(centre * centre, -1, keepdims=True)
    return centre * lax.rsqrt(spread + LN_EPS) * gain_vector


def rms_normed(row_values, gain_vector):
    floats = row_values.astype(jnp.float32)
    return floats * lax.rsqrt(jnp.mean(floats * floats, -1, keepdims=True) + RMS_EPS) * gain_vector


def rotary(heads_in, positions):
    halfway = heads_in.shape[-1] // 2
    rates = 10000.0 ** (-2.0 * jnp.arange(halfway, dtype=jnp.float32) / heads_in.shape[-1])
    angles = positions.astype(jnp.float32)[:, None] * rates[None, :]
    cosine_table = jnp.cos(angles)[:, None, :]
    sine_table = jnp.sin(angles)[:, None, :]
    leading = heads_in[..., :halfway]
    trailing = heads_in[..., halfway:]
    return jnp.concatenate(
        [
            leading * cosine_table - trailing * sine_table,
            trailing * cosine_table + leading * sine_table,
        ],
        -1,
    )


MESH_IDS = pl.DeviceIdType.MESH


def exchange_kernel(axis, ways, stride, gather, x_ref, y_ref, send_sem, recv_sem, local_sem):
    position = lax.axis_index(axis)
    me = lax.rem(lax.div(position, stride), ways)
    base = position - me * stride
    other = lax.axis_index("seq" if axis == "tp" else "tp")

    def device(member):
        index = base + member * stride
        return (other, index) if axis == "tp" else (index, other)

    barrier = pltpu.get_barrier_semaphore()
    for shift in range(1, ways):
        peer = lax.rem(me + shift, ways)
        pl.semaphore_signal(barrier, inc=1, device_id=device(peer), device_id_type=MESH_IDS)
    pl.semaphore_wait(barrier, ways - 1)
    sends = []
    for shift in range(1, ways):
        peer = lax.rem(me + shift, ways)
        copy = pltpu.make_async_remote_copy(
            src_ref=x_ref if gather else x_ref.at[peer],
            dst_ref=y_ref.at[me],
            send_sem=send_sem.at[shift],
            recv_sem=recv_sem.at[shift],
            device_id=device(peer),
            device_id_type=MESH_IDS,
        )
        copy.start()
        sends.append(copy)
    local = pltpu.make_async_copy(x_ref if gather else x_ref.at[me], y_ref.at[me], local_sem)
    local.start()
    for copy in sends:
        copy.wait_send()
    for shift in range(1, ways):
        source = lax.rem(me + ways - shift, ways)
        arriving = pltpu.make_async_remote_copy(
            src_ref=x_ref if gather else x_ref.at[source],
            dst_ref=y_ref.at[source],
            send_sem=send_sem.at[shift],
            recv_sem=recv_sem.at[shift],
            device_id=device(source),
            device_id_type=MESH_IDS,
        )
        arriving.wait_recv()
    local.wait()


def tp_exchange(x, ways, gather, collective_id, axis="tp", stride=1):
    piece = x.shape if gather else x.shape[1:]
    return pl.pallas_call(
        functools.partial(exchange_kernel, axis, ways, stride, gather),
        out_shape=jax.ShapeDtypeStruct((ways,) + tuple(piece), x.dtype),
        in_specs=[pl.BlockSpec(memory_space=pl.ANY)],
        out_specs=pl.BlockSpec(memory_space=pl.ANY),
        scratch_shapes=[
            pltpu.SemaphoreType.DMA((ways,)),
            pltpu.SemaphoreType.DMA((ways,)),
            pltpu.SemaphoreType.DMA(()),
        ],
        compiler_params=pltpu.CompilerParams(collective_id=collective_id, has_side_effects=True),
    )(x)


def seq_gathered(piece, seq_ways, collective_ids):
    inner = math.gcd(seq_ways, 8)
    if seq_ways == inner:
        return tp_exchange(piece, inner, True, collective_ids[0], "seq", 1)
    far = tp_exchange(piece, seq_ways // inner, True, collective_ids[1], "seq", inner)
    near = tp_exchange(far, inner, True, collective_ids[0], "seq", 1)
    return jnp.swapaxes(near, 0, 1).reshape((seq_ways,) + piece.shape)


def summed_rows(term_task, own_rows, collective_id):
    ways = lax.axis_size("tp")
    partial = term_task(jnp.int32(0), own_rows * ways)
    pieces = partial.reshape((ways, own_rows) + partial.shape[1:]).astype(jnp.bfloat16)
    arrived = tp_exchange(pieces, ways, False, collective_id)
    return jnp.sum(arrived.astype(jnp.float32), 0)


def gathered_patches(piece, collective_id):
    ways = lax.axis_size("tp")
    whole = tp_exchange(piece, ways, True, collective_id)
    return jnp.transpose(whole, (1, 0, 2, 3)).reshape(
        (piece.shape[0], ways * piece.shape[1]) + piece.shape[2:]
    )


def attention_kernel(meta_ref, lengths_ref, qt_ref, k_ref, v_ref, o_ref, m_sc, l_sc, acc_sc):
    step = pl.program_id(0)
    seq = meta_ref[0]
    width, rows = qt_ref.shape
    span = k_ref.shape[1]
    heads = width // HEAD
    score_scale = 1.0 / math.sqrt(HEAD)

    @pl.when(step == 0)
    def _():
        m_sc[...] = jnp.full(m_sc.shape, MASKED_SCORE, jnp.float32)
        l_sc[...] = jnp.zeros(l_sc.shape, jnp.float32)
        acc_sc[...] = jnp.zeros(acc_sc.shape, jnp.float32)

    def update(diagonal):
        qt = qt_ref[...]
        k = k_ref[...]
        v = v_ref[...]
        feature = lax.broadcasted_iota(jnp.int32, (width, rows), 0)
        key_index = lax.broadcasted_iota(jnp.int32, (span, 1), 0)
        bias = jnp.where(key_index < lengths_ref[step], 0.0, MASKED_SCORE).astype(jnp.float32)
        if diagonal:
            causal = lax.broadcasted_iota(jnp.int32, (span, rows), 0) <= lax.broadcasted_iota(
                jnp.int32, (span, rows), 1
            )
        for h in range(heads):
            in_head = (feature >= h * HEAD) & (feature < (h + 1) * HEAD)
            qt_head = jnp.where(in_head, qt, jnp.zeros_like(qt))
            scores = (
                lax.dot_general(
                    k, qt_head, (((0,), (0,)), ((), ())), preferred_element_type=jnp.float32
                )
                * score_scale
                + bias
            )
            if diagonal:
                scores = jnp.where(causal, scores, MASKED_SCORE)
            m_prev = m_sc[h]
            m_new = jnp.maximum(m_prev, jnp.max(scores, axis=0, keepdims=True))
            weights = jnp.exp(scores - m_new)
            alpha = jnp.exp(m_prev - m_new)
            l_sc[h] = alpha * l_sc[h] + jnp.sum(weights, axis=0, keepdims=True)
            mixed = jnp.dot(v, weights.astype(jnp.bfloat16), preferred_element_type=jnp.float32)
            acc_sc[h] = acc_sc[h] * alpha + mixed
            m_sc[h] = m_new

    @pl.when(step < seq)
    def _():
        update(False)

    @pl.when(step == seq)
    def _():
        update(True)

    @pl.when(step == pl.num_programs(0) - 1)
    def _():
        feature = lax.broadcasted_iota(jnp.int32, (width, rows), 0)
        result = jnp.zeros((width, rows), jnp.float32)
        for h in range(heads):
            in_head = (feature >= h * HEAD) & (feature < (h + 1) * HEAD)
            result = jnp.where(in_head, acc_sc[h] / l_sc[h], result)
        o_ref[...] = result


def causal_attention(query_flat, key_value_all, seq_index, block_lengths, rows_per_block):
    rows, width = query_flat.shape
    span = rows_per_block
    steps = key_value_all.shape[0] // (2 * width)
    heads = width // HEAD
    meta = jnp.reshape(seq_index, (1,)).astype(jnp.int32)
    grid_spec = pltpu.PrefetchScalarGridSpec(
        num_scalar_prefetch=2,
        grid=(steps,),
        in_specs=[
            pl.BlockSpec((width, rows), lambda i, m, n: (0, 0)),
            pl.BlockSpec((width, span), lambda i, m, n: (2 * jnp.minimum(i, m[0]), 0)),
            pl.BlockSpec((width, span), lambda i, m, n: (2 * jnp.minimum(i, m[0]) + 1, 0)),
        ],
        out_specs=pl.BlockSpec((width, rows), lambda i, m, n: (0, 0)),
        scratch_shapes=[
            pltpu.VMEM((heads, 1, rows), jnp.float32),
            pltpu.VMEM((heads, 1, rows), jnp.float32),
            pltpu.VMEM((heads, width, rows), jnp.float32),
        ],
    )
    keys_total = steps * span
    result = pl.pallas_call(
        attention_kernel,
        grid_spec=grid_spec,
        out_shape=jax.ShapeDtypeStruct((width, rows), jnp.float32),
        compiler_params=pltpu.CompilerParams(dimension_semantics=("arbitrary",)),
        cost_estimate=pl.CostEstimate(
            flops=4 * heads * rows * keys_total * width,
            transcendentals=heads * rows * keys_total,
            bytes_accessed=key_value_all.size * 2 + 3 * query_flat.size * 2,
        ),
    )(meta, block_lengths, jnp.transpose(query_flat), key_value_all, key_value_all)
    return jnp.transpose(result).astype(jnp.bfloat16)


def shards(
    pixels,
    text_rows,
    patch_counts,
    picture_starts,
    block_lengths,
    vision_gain,
    vision_project,
    vision_output,
    merge_gain,
    merge_weight,
    text_gain,
    text_project,
    text_output,
):
    seq_ways = lax.axis_size("seq")
    tp_ways = lax.axis_size("tp")
    seq_index = lax.axis_index("seq")
    tp_index = lax.axis_index("tp")
    picture_total, local_patches, model_width = pixels.shape
    patch_total = local_patches * tp_ways
    local_width = vision_project.shape[2]
    head_count = local_width // HEAD
    patch_normed = layer_normed(pixels, vision_gain).astype(jnp.bfloat16)
    packed_project = vision_project.reshape(model_width, 3 * local_width)
    projected = jnp.einsum(
        "npd,de->npe",
        gathered_patches(patch_normed, 0),
        packed_project,
        preferred_element_type=jnp.float32,
    ).astype(jnp.bfloat16)
    queries = projected[..., :local_width].reshape(picture_total, patch_total, head_count, HEAD)
    key_heads = projected[..., local_width : 2 * local_width].reshape(
        picture_total, patch_total, head_count, HEAD
    )
    value_heads = projected[..., 2 * local_width :].reshape(
        picture_total, patch_total, head_count, HEAD
    )
    live_counts = lax.dynamic_slice_in_dim(
        patch_counts, seq_index * picture_total, picture_total, 0
    )
    score_scale = 1.0 / math.sqrt(HEAD)
    scores = (
        jnp.einsum("nqhd,nkhd->nhqk", queries, key_heads, preferred_element_type=jnp.float32)
        * score_scale
    )
    allowed = (jnp.arange(patch_total, dtype=jnp.int32)[None, :] < live_counts[:, None])[
        :, None, None, :
    ]
    scores = jnp.where(allowed, scores, MASKED_SCORE)
    highest = jnp.max(scores, -1, keepdims=True)
    weights = jnp.where(allowed, jnp.exp(scores - highest), 0.0)
    mixture = jnp.einsum(
        "nhqk,nkhd->nqhd",
        weights.astype(jnp.bfloat16),
        value_heads,
        preferred_element_type=jnp.float32,
    )
    mixture = mixture / jnp.transpose(jnp.sum(weights, -1), (0, 2, 1))[..., None]
    attended = mixture.astype(jnp.bfloat16).reshape(picture_total, patch_total, local_width)
    patch_major = jnp.transpose(attended, (1, 0, 2)).reshape(
        patch_total * picture_total, local_width
    )

    def vision_term(offset, row_count):
        return jnp.dot(patch_major, vision_output, preferred_element_type=jnp.float32)

    vision_sum = summed_rows(vision_term, local_patches * picture_total, 2)
    vision_sum = jnp.transpose(
        vision_sum.reshape(local_patches, picture_total, model_width), (1, 0, 2)
    )
    vision_rows = (pixels.astype(jnp.float32) + vision_sum).astype(jnp.bfloat16)
    merge_input = layer_normed(vision_rows, merge_gain).astype(jnp.bfloat16)
    merged_total = patch_total // 4
    input_share = merge_weight.shape[0]
    whole_pictures = gathered_patches(merge_input, 1)
    merged_rows = whole_pictures.reshape(picture_total * merged_total, 4 * model_width)
    owned_inputs = lax.dynamic_slice_in_dim(merged_rows, tp_index * input_share, input_share, 1)

    def merge_term(offset, row_count):
        return jnp.dot(owned_inputs, merge_weight, preferred_element_type=jnp.float32)

    part_rows = picture_total * merged_total // tp_ways
    visual_part = summed_rows(merge_term, part_rows, 3).astype(jnp.bfloat16)
    rows_per_block = text_rows.shape[0] * tp_ways
    start_table = picture_starts.reshape(seq_ways, picture_total)
    dest_table = start_table // rows_per_block
    picture_rank = tp_index * part_rows // merged_total
    rank_dest = jnp.sum(
        jnp.where(
            jnp.arange(picture_total, dtype=jnp.int32)[None, :] == picture_rank, dest_table, 0
        ),
        1,
    )
    senders = rank_dest == seq_index
    segment = seq_gathered(visual_part, seq_ways, (6, 7)).reshape(-1, model_width)
    row_count = segment.shape[0]
    sources = jnp.arange(row_count, dtype=jnp.int32) // part_rows
    wanted = jnp.any(
        (sources[:, None] == jnp.arange(seq_ways, dtype=jnp.int32)[None, :]) & senders[None, :], 1
    )
    selector = (
        (jnp.arange(row_count, dtype=jnp.int32) % part_rows)[None, :]
        == jnp.arange(part_rows, dtype=jnp.int32)[:, None]
    ) & wanted[None, :]
    arrived = jnp.dot(
        selector.astype(jnp.bfloat16), segment, preferred_element_type=jnp.float32
    ).astype(jnp.bfloat16)
    text_block = lax.all_gather(text_rows, "tp", axis=0, tiled=True)
    visual_block = tp_exchange(arrived, tp_ways, True, 5).reshape(-1, model_width)
    landed = dest_table == seq_index
    local_starts = jnp.sum(jnp.where(landed, start_table - seq_index * rows_per_block, 0), 0)
    live_groups = jnp.sum(
        jnp.where(landed, patch_counts.reshape(seq_ways, picture_total) // 4, 0), 0
    )
    slot_index = jnp.arange(merged_total, dtype=jnp.int32)
    targets = (local_starts[:, None] + slot_index[None, :]).reshape(-1)
    in_use = (slot_index[None, :] < live_groups[:, None]).reshape(-1)
    placement = (jnp.arange(rows_per_block, dtype=jnp.int32)[:, None] == targets[None, :]) & in_use[
        None, :
    ]
    covered = jnp.any(placement, 1)
    placed = jnp.dot(
        placement.astype(jnp.bfloat16), visual_block, preferred_element_type=jnp.float32
    ).astype(jnp.bfloat16)
    embedded = jnp.where(covered[:, None], placed, text_block)
    text_normed = rms_normed(embedded, text_gain).astype(jnp.bfloat16)
    text_heads = jnp.dot(
        text_normed,
        text_project.reshape(model_width, 3 * local_width),
        preferred_element_type=jnp.float32,
    )
    positions = seq_index * rows_per_block + jnp.arange(rows_per_block, dtype=jnp.int32)
    query_rows = rotary(
        text_heads[:, :local_width].reshape(rows_per_block, head_count, HEAD), positions
    ).astype(jnp.bfloat16)
    key_rows = rotary(
        text_heads[:, local_width : 2 * local_width].reshape(rows_per_block, head_count, HEAD),
        positions,
    ).astype(jnp.bfloat16)
    value_rows = text_heads[:, 2 * local_width :].astype(jnp.bfloat16)
    key_flat = key_rows.reshape(rows_per_block, local_width)
    key_value_all = lax.all_gather(
        jnp.concatenate([jnp.transpose(key_flat), jnp.transpose(value_rows)], 0),
        "seq",
        axis=0,
        tiled=True,
    )
    attended_rows = causal_attention(
        query_rows.reshape(rows_per_block, local_width),
        key_value_all,
        seq_index,
        block_lengths,
        rows_per_block,
    )
    own_rows = text_rows.shape[0]

    def text_term(offset, row_count):
        return jnp.dot(attended_rows, text_output, preferred_element_type=jnp.float32)

    text_sum = summed_rows(text_term, own_rows, 4)
    residual = lax.dynamic_slice_in_dim(embedded, tp_index * own_rows, own_rows, 0)
    hidden = (residual.astype(jnp.float32) + text_sum).astype(jnp.bfloat16)
    return (hidden, key_flat, value_rows)


def solution(mesh):
    placed = (
        P("seq", "tp", None),
        P(("seq", "tp"), None),
        P(),
        P(),
        P(),
        P(),
        P(None, None, "tp"),
        P("tp", None),
        P(),
        P("tp", None),
        P(),
        P(None, None, "tp"),
        P("tp", None),
    )
    return jax.shard_map(
        shards,
        mesh=mesh,
        in_specs=placed,
        out_specs=(P(("seq", "tp"), None), P("seq", "tp"), P("seq", "tp")),
        check_vma=False,
    )
```

```python
import functools
import math

import jax
import jax.numpy as jnp
from jax import lax
from jax.experimental import pallas as pl
from jax.experimental.pallas import tpu as pltpu
from jax.sharding import PartitionSpec as P

HEAD = 104


LN_EPS = 1e-05
RMS_EPS = 1e-06
MASKED_SCORE = -1e30
KEY_SPAN = 512


def layer_normed(row_values, gain_vector):
    floats = row_values.astype(jnp.float32)
    centre = floats - jnp.mean(floats, -1, keepdims=True)
    spread = jnp.mean(centre * centre, -1, keepdims=True)
    return centre * lax.rsqrt(spread + LN_EPS) * gain_vector


def rms_normed(row_values, gain_vector):
    floats = row_values.astype(jnp.float32)
    return floats * lax.rsqrt(jnp.mean(floats * floats, -1, keepdims=True) + RMS_EPS) * gain_vector


def rotary(heads_in, positions):
    halfway = heads_in.shape[-1] // 2
    rates = 10000.0 ** (-2.0 * jnp.arange(halfway, dtype=jnp.float32) / heads_in.shape[-1])
    angles = positions.astype(jnp.float32)[:, None] * rates[None, :]
    cosine_table = jnp.cos(angles)[:, None, :]
    sine_table = jnp.sin(angles)[:, None, :]
    leading = heads_in[..., :halfway]
    trailing = heads_in[..., halfway:]
    return jnp.concatenate(
        [
            leading * cosine_table - trailing * sine_table,
            trailing * cosine_table + leading * sine_table,
        ],
        -1,
    )


MESH_IDS = pl.DeviceIdType.MESH


def exchange_kernel(axis, ways, stride, gather, x_ref, y_ref, send_sem, recv_sem, local_sem):
    position = lax.axis_index(axis)
    me = lax.rem(lax.div(position, stride), ways)
    base = position - me * stride
    other = lax.axis_index("seq" if axis == "tp" else "tp")

    def device(member):
        index = base + member * stride
        return (other, index) if axis == "tp" else (index, other)

    barrier = pltpu.get_barrier_semaphore()
    for shift in range(1, ways):
        peer = lax.rem(me + shift, ways)
        pl.semaphore_signal(barrier, inc=1, device_id=device(peer), device_id_type=MESH_IDS)
    pl.semaphore_wait(barrier, ways - 1)
    sends = []
    for shift in range(1, ways):
        peer = lax.rem(me + shift, ways)
        copy = pltpu.make_async_remote_copy(
            src_ref=x_ref if gather else x_ref.at[peer],
            dst_ref=y_ref.at[me],
            send_sem=send_sem.at[shift],
            recv_sem=recv_sem.at[shift],
            device_id=device(peer),
            device_id_type=MESH_IDS,
        )
        copy.start()
        sends.append(copy)
    local = pltpu.make_async_copy(x_ref if gather else x_ref.at[me], y_ref.at[me], local_sem)
    local.start()
    for copy in sends:
        copy.wait_send()
    for shift in range(1, ways):
        source = lax.rem(me + ways - shift, ways)
        arriving = pltpu.make_async_remote_copy(
            src_ref=x_ref if gather else x_ref.at[source],
            dst_ref=y_ref.at[source],
            send_sem=send_sem.at[shift],
            recv_sem=recv_sem.at[shift],
            device_id=device(source),
            device_id_type=MESH_IDS,
        )
        arriving.wait_recv()
    local.wait()


def tp_exchange(x, ways, gather, collective_id, axis="tp", stride=1):
    piece = x.shape if gather else x.shape[1:]
    return pl.pallas_call(
        functools.partial(exchange_kernel, axis, ways, stride, gather),
        out_shape=jax.ShapeDtypeStruct((ways,) + tuple(piece), x.dtype),
        in_specs=[pl.BlockSpec(memory_space=pl.ANY)],
        out_specs=pl.BlockSpec(memory_space=pl.ANY),
        scratch_shapes=[
            pltpu.SemaphoreType.DMA((ways,)),
            pltpu.SemaphoreType.DMA((ways,)),
            pltpu.SemaphoreType.DMA(()),
        ],
        compiler_params=pltpu.CompilerParams(collective_id=collective_id, has_side_effects=True),
    )(x)


def seq_gathered(piece, seq_ways, collective_ids):
    inner = math.gcd(seq_ways, 8)
    if seq_ways == inner:
        return tp_exchange(piece, inner, True, collective_ids[0], "seq", 1)
    far = tp_exchange(piece, seq_ways // inner, True, collective_ids[1], "seq", inner)
    near = tp_exchange(far, inner, True, collective_ids[0], "seq", 1)
    return jnp.swapaxes(near, 0, 1).reshape((seq_ways,) + piece.shape)


def summed_rows(term_task, own_rows, collective_id):
    ways = lax.axis_size("tp")
    partial = term_task(jnp.int32(0), own_rows * ways)
    pieces = partial.reshape((ways, own_rows) + partial.shape[1:]).astype(jnp.bfloat16)
    arrived = tp_exchange(pieces, ways, False, collective_id)
    return jnp.sum(arrived.astype(jnp.float32), 0)


def gathered_patches(piece, collective_id):
    ways = lax.axis_size("tp")
    whole = tp_exchange(piece, ways, True, collective_id)
    return jnp.transpose(whole, (1, 0, 2, 3)).reshape(
        (piece.shape[0], ways * piece.shape[1]) + piece.shape[2:]
    )


def attention_kernel(meta_ref, lengths_ref, qt_ref, k_ref, v_ref, o_ref, m_sc, l_sc, acc_sc):
    step = pl.program_id(0)
    seq = meta_ref[0]
    width, rows = qt_ref.shape
    span = k_ref.shape[1]
    heads = width // HEAD
    score_scale = 1.0 / math.sqrt(HEAD)

    @pl.when(step == 0)
    def _():
        m_sc[...] = jnp.full(m_sc.shape, MASKED_SCORE, jnp.float32)
        l_sc[...] = jnp.zeros(l_sc.shape, jnp.float32)
        acc_sc[...] = jnp.zeros(acc_sc.shape, jnp.float32)

    def update(diagonal):
        qt = qt_ref[...]
        k = k_ref[...]
        v = v_ref[...]
        feature = lax.broadcasted_iota(jnp.int32, (width, rows), 0)
        key_index = lax.broadcasted_iota(jnp.int32, (span, 1), 0)
        bias = jnp.where(key_index < lengths_ref[step], 0.0, MASKED_SCORE).astype(jnp.float32)
        if diagonal:
            causal = lax.broadcasted_iota(jnp.int32, (span, rows), 0) <= lax.broadcasted_iota(
                jnp.int32, (span, rows), 1
            )
        for h in range(heads):
            in_head = (feature >= h * HEAD) & (feature < (h + 1) * HEAD)
            qt_head = jnp.where(in_head, qt, jnp.zeros_like(qt))
            scores = (
                lax.dot_general(
                    k, qt_head, (((0,), (0,)), ((), ())), preferred_element_type=jnp.float32
                )
                * score_scale
                + bias
            )
            if diagonal:
                scores = jnp.where(causal, scores, MASKED_SCORE)
            m_prev = m_sc[h]
            m_new = jnp.maximum(m_prev, jnp.max(scores, axis=0, keepdims=True))
            weights = jnp.exp(scores - m_new)
            alpha = jnp.exp(m_prev - m_new)
            l_sc[h] = alpha * l_sc[h] + jnp.sum(weights, axis=0, keepdims=True)
            mixed = jnp.dot(v, weights.astype(jnp.bfloat16), preferred_element_type=jnp.float32)
            acc_sc[h] = acc_sc[h] * alpha + mixed
            m_sc[h] = m_new

    @pl.when(step < seq)
    def _():
        update(False)

    @pl.when(step == seq)
    def _():
        update(True)

    @pl.when(step == pl.num_programs(0) - 1)
    def _():
        feature = lax.broadcasted_iota(jnp.int32, (width, rows), 0)
        result = jnp.zeros((width, rows), jnp.float32)
        for h in range(heads):
            in_head = (feature >= h * HEAD) & (feature < (h + 1) * HEAD)
            result = jnp.where(in_head, acc_sc[h] / l_sc[h], result)
        o_ref[...] = result


def causal_attention(query_flat, key_value_all, seq_index, block_lengths, rows_per_block):
    rows, width = query_flat.shape
    span = rows_per_block
    steps = key_value_all.shape[0] // (2 * width)
    heads = width // HEAD
    meta = jnp.reshape(seq_index, (1,)).astype(jnp.int32)
    grid_spec = pltpu.PrefetchScalarGridSpec(
        num_scalar_prefetch=2,
        grid=(steps,),
        in_specs=[
            pl.BlockSpec((width, rows), lambda i, m, n: (0, 0)),
            pl.BlockSpec((width, span), lambda i, m, n: (2 * jnp.minimum(i, m[0]), 0)),
            pl.BlockSpec((width, span), lambda i, m, n: (2 * jnp.minimum(i, m[0]) + 1, 0)),
        ],
        out_specs=pl.BlockSpec((width, rows), lambda i, m, n: (0, 0)),
        scratch_shapes=[
            pltpu.VMEM((heads, 1, rows), jnp.float32),
            pltpu.VMEM((heads, 1, rows), jnp.float32),
            pltpu.VMEM((heads, width, rows), jnp.float32),
        ],
    )
    keys_total = steps * span
    result = pl.pallas_call(
        attention_kernel,
        grid_spec=grid_spec,
        out_shape=jax.ShapeDtypeStruct((width, rows), jnp.float32),
        compiler_params=pltpu.CompilerParams(dimension_semantics=("arbitrary",)),
        cost_estimate=pl.CostEstimate(
            flops=4 * heads * rows * keys_total * width,
            transcendentals=heads * rows * keys_total,
            bytes_accessed=key_value_all.size * 2 + 3 * query_flat.size * 2,
        ),
    )(meta, block_lengths, jnp.transpose(query_flat), key_value_all, key_value_all)
    return jnp.transpose(result).astype(jnp.bfloat16)


def shards(
    pixels,
    text_rows,
    patch_counts,
    picture_starts,
    block_lengths,
    vision_gain,
    vision_project,
    vision_output,
    merge_gain,
    merge_weight,
    text_gain,
    text_project,
    text_output,
):
    seq_ways = lax.axis_size("seq")
    tp_ways = lax.axis_size("tp")
    seq_index = lax.axis_index("seq")
    tp_index = lax.axis_index("tp")
    picture_total, local_patches, model_width = pixels.shape
    patch_total = local_patches * tp_ways
    local_width = vision_project.shape[2]
    head_count = local_width // HEAD
    patch_normed = layer_normed(pixels, vision_gain).astype(jnp.bfloat16)
    packed_project = vision_project.reshape(model_width, 3 * local_width)
    projected = jnp.einsum(
        "npd,de->npe",
        gathered_patches(patch_normed, 0),
        packed_project,
        preferred_element_type=jnp.float32,
    ).astype(jnp.bfloat16)
    queries = projected[..., :local_width].reshape(picture_total, patch_total, head_count, HEAD)
    key_heads = projected[..., local_width : 2 * local_width].reshape(
        picture_total, patch_total, head_count, HEAD
    )
    value_heads = projected[..., 2 * local_width :].reshape(
        picture_total, patch_total, head_count, HEAD
    )
    live_counts = lax.dynamic_slice_in_dim(
        patch_counts, seq_index * picture_total, picture_total, 0
    )
    score_scale = 1.0 / math.sqrt(HEAD)
    scores = (
        jnp.einsum("nqhd,nkhd->nhqk", queries, key_heads, preferred_element_type=jnp.float32)
        * score_scale
    )
    allowed = (jnp.arange(patch_total, dtype=jnp.int32)[None, :] < live_counts[:, None])[
        :, None, None, :
    ]
    scores = jnp.where(allowed, scores, MASKED_SCORE)
    highest = jnp.max(scores, -1, keepdims=True)
    weights = jnp.where(allowed, jnp.exp(scores - highest), 0.0)
    mixture = jnp.einsum(
        "nhqk,nkhd->nqhd",
        weights.astype(jnp.bfloat16),
        value_heads,
        preferred_element_type=jnp.float32,
    )
    mixture = mixture / jnp.transpose(jnp.sum(weights, -1), (0, 2, 1))[..., None]
    attended = mixture.astype(jnp.bfloat16).reshape(picture_total, patch_total, local_width)
    patch_major = jnp.transpose(attended, (1, 0, 2)).reshape(
        patch_total * picture_total, local_width
    )

    def vision_term(offset, row_count):
        return jnp.dot(patch_major, vision_output, preferred_element_type=jnp.float32)

    vision_sum = summed_rows(vision_term, local_patches * picture_total, 2)
    vision_sum = jnp.transpose(
        vision_sum.reshape(local_patches, picture_total, model_width), (1, 0, 2)
    )
    vision_rows = (pixels.astype(jnp.float32) + vision_sum).astype(jnp.bfloat16)
    merge_input = layer_normed(vision_rows, merge_gain).astype(jnp.bfloat16)
    merged_total = patch_total // 4
    input_share = merge_weight.shape[0]
    groups = input_share * tp_ways // model_width
    halves = tp_ways // groups
    outgoing = merge_input.reshape(
        picture_total, local_patches // groups, groups, halves, input_share
    )
    outgoing = jnp.transpose(outgoing, (2, 3, 0, 1, 4)).reshape(
        tp_ways, picture_total, local_patches // groups, input_share
    )
    incoming = tp_exchange(outgoing, tp_ways, False, 1)
    owned_inputs = jnp.transpose(incoming, (1, 0, 2, 3)).reshape(
        picture_total * merged_total, input_share
    )

    def merge_term(offset, row_count):
        return jnp.dot(owned_inputs, merge_weight, preferred_element_type=jnp.float32)

    part_rows = picture_total * merged_total // tp_ways
    visual_part = summed_rows(merge_term, part_rows, 3).astype(jnp.bfloat16)
    rows_per_block = text_rows.shape[0] * tp_ways
    start_table = picture_starts.reshape(seq_ways, picture_total)
    dest_table = start_table // rows_per_block
    picture_rank = tp_index * part_rows // merged_total
    rank_dest = jnp.sum(
        jnp.where(
            jnp.arange(picture_total, dtype=jnp.int32)[None, :] == picture_rank, dest_table, 0
        ),
        1,
    )
    senders = rank_dest == seq_index
    segment = seq_gathered(visual_part, seq_ways, (6, 7)).reshape(-1, model_width)
    row_count = segment.shape[0]
    sources = jnp.arange(row_count, dtype=jnp.int32) // part_rows
    wanted = jnp.any(
        (sources[:, None] == jnp.arange(seq_ways, dtype=jnp.int32)[None, :]) & senders[None, :], 1
    )
    selector = (
        (jnp.arange(row_count, dtype=jnp.int32) % part_rows)[None, :]
        == jnp.arange(part_rows, dtype=jnp.int32)[:, None]
    ) & wanted[None, :]
    arrived = jnp.dot(
        selector.astype(jnp.bfloat16), segment, preferred_element_type=jnp.float32
    ).astype(jnp.bfloat16)
    text_block = lax.all_gather(text_rows, "tp", axis=0, tiled=True)
    visual_block = tp_exchange(arrived, tp_ways, True, 5).reshape(-1, model_width)
    landed = dest_table == seq_index
    local_starts = jnp.sum(jnp.where(landed, start_table - seq_index * rows_per_block, 0), 0)
    live_groups = jnp.sum(
        jnp.where(landed, patch_counts.reshape(seq_ways, picture_total) // 4, 0), 0
    )
    slot_index = jnp.arange(merged_total, dtype=jnp.int32)
    targets = (local_starts[:, None] + slot_index[None, :]).reshape(-1)
    in_use = (slot_index[None, :] < live_groups[:, None]).reshape(-1)
    placement = (jnp.arange(rows_per_block, dtype=jnp.int32)[:, None] == targets[None, :]) & in_use[
        None, :
    ]
    covered = jnp.any(placement, 1)
    placed = jnp.dot(
        placement.astype(jnp.bfloat16), visual_block, preferred_element_type=jnp.float32
    ).astype(jnp.bfloat16)
    embedded = jnp.where(covered[:, None], placed, text_block)
    text_normed = rms_normed(embedded, text_gain).astype(jnp.bfloat16)
    text_heads = jnp.dot(
        text_normed,
        text_project.reshape(model_width, 3 * local_width),
        preferred_element_type=jnp.float32,
    )
    positions = seq_index * rows_per_block + jnp.arange(rows_per_block, dtype=jnp.int32)
    query_rows = rotary(
        text_heads[:, :local_width].reshape(rows_per_block, head_count, HEAD), positions
    ).astype(jnp.bfloat16)
    key_rows = rotary(
        text_heads[:, local_width : 2 * local_width].reshape(rows_per_block, head_count, HEAD),
        positions,
    ).astype(jnp.bfloat16)
    value_rows = text_heads[:, 2 * local_width :].astype(jnp.bfloat16)
    key_flat = key_rows.reshape(rows_per_block, local_width)
    key_value_all = lax.all_gather(
        jnp.concatenate([jnp.transpose(key_flat), jnp.transpose(value_rows)], 0),
        "seq",
        axis=0,
        tiled=True,
    )
    attended_rows = causal_attention(
        query_rows.reshape(rows_per_block, local_width),
        key_value_all,
        seq_index,
        block_lengths,
        rows_per_block,
    )
    own_rows = text_rows.shape[0]

    def text_term(offset, row_count):
        return jnp.dot(attended_rows, text_output, preferred_element_type=jnp.float32)

    text_sum = summed_rows(text_term, own_rows, 4)
    residual = lax.dynamic_slice_in_dim(embedded, tp_index * own_rows, own_rows, 0)
    hidden = (residual.astype(jnp.float32) + text_sum).astype(jnp.bfloat16)
    return (hidden, key_flat, value_rows)


def solution(mesh):
    placed = (
        P("seq", "tp", None),
        P(("seq", "tp"), None),
        P(),
        P(),
        P(),
        P(),
        P(None, None, "tp"),
        P("tp", None),
        P(),
        P("tp", None),
        P(),
        P(None, None, "tp"),
        P("tp", None),
    )
    return jax.shard_map(
        shards,
        mesh=mesh,
        in_specs=placed,
        out_specs=(P(("seq", "tp"), None), P("seq", "tp"), P("seq", "tp")),
        check_vma=False,
    )
```

```python
import functools
import math

import jax
import jax.numpy as jnp
from jax import lax
from jax.experimental import pallas as pl
from jax.experimental.pallas import tpu as pltpu
from jax.sharding import PartitionSpec as P

HEAD = 104


LN_EPS = 1e-05
RMS_EPS = 1e-06
MASKED_SCORE = -1e30
KEY_SPAN = 512


def layer_normed(row_values, gain_vector):
    floats = row_values.astype(jnp.float32)
    centre = floats - jnp.mean(floats, -1, keepdims=True)
    spread = jnp.mean(centre * centre, -1, keepdims=True)
    return centre * lax.rsqrt(spread + LN_EPS) * gain_vector


def rms_normed(row_values, gain_vector):
    floats = row_values.astype(jnp.float32)
    return floats * lax.rsqrt(jnp.mean(floats * floats, -1, keepdims=True) + RMS_EPS) * gain_vector


def rotary(heads_in, positions):
    halfway = heads_in.shape[-1] // 2
    rates = 10000.0 ** (-2.0 * jnp.arange(halfway, dtype=jnp.float32) / heads_in.shape[-1])
    angles = positions.astype(jnp.float32)[:, None] * rates[None, :]
    cosine_table = jnp.cos(angles)[:, None, :]
    sine_table = jnp.sin(angles)[:, None, :]
    leading = heads_in[..., :halfway]
    trailing = heads_in[..., halfway:]
    return jnp.concatenate(
        [
            leading * cosine_table - trailing * sine_table,
            trailing * cosine_table + leading * sine_table,
        ],
        -1,
    )


MESH_IDS = pl.DeviceIdType.MESH


def exchange_kernel(axis, ways, stride, gather, x_ref, y_ref, send_sem, recv_sem, local_sem):
    position = lax.axis_index(axis)
    me = lax.rem(lax.div(position, stride), ways)
    base = position - me * stride
    other = lax.axis_index("seq" if axis == "tp" else "tp")

    def device(member):
        index = base + member * stride
        return (other, index) if axis == "tp" else (index, other)

    barrier = pltpu.get_barrier_semaphore()
    for shift in range(1, ways):
        peer = lax.rem(me + shift, ways)
        pl.semaphore_signal(barrier, inc=1, device_id=device(peer), device_id_type=MESH_IDS)
    pl.semaphore_wait(barrier, ways - 1)
    sends = []
    for shift in range(1, ways):
        peer = lax.rem(me + shift, ways)
        copy = pltpu.make_async_remote_copy(
            src_ref=x_ref if gather else x_ref.at[peer],
            dst_ref=y_ref.at[me],
            send_sem=send_sem.at[shift],
            recv_sem=recv_sem.at[shift],
            device_id=device(peer),
            device_id_type=MESH_IDS,
        )
        copy.start()
        sends.append(copy)
    local = pltpu.make_async_copy(x_ref if gather else x_ref.at[me], y_ref.at[me], local_sem)
    local.start()
    for copy in sends:
        copy.wait_send()
    for shift in range(1, ways):
        source = lax.rem(me + ways - shift, ways)
        arriving = pltpu.make_async_remote_copy(
            src_ref=x_ref if gather else x_ref.at[source],
            dst_ref=y_ref.at[source],
            send_sem=send_sem.at[shift],
            recv_sem=recv_sem.at[shift],
            device_id=device(source),
            device_id_type=MESH_IDS,
        )
        arriving.wait_recv()
    local.wait()


def tp_exchange(x, ways, gather, collective_id, axis="tp", stride=1):
    piece = x.shape if gather else x.shape[1:]
    return pl.pallas_call(
        functools.partial(exchange_kernel, axis, ways, stride, gather),
        out_shape=jax.ShapeDtypeStruct((ways,) + tuple(piece), x.dtype),
        in_specs=[pl.BlockSpec(memory_space=pl.ANY)],
        out_specs=pl.BlockSpec(memory_space=pl.ANY),
        scratch_shapes=[
            pltpu.SemaphoreType.DMA((ways,)),
            pltpu.SemaphoreType.DMA((ways,)),
            pltpu.SemaphoreType.DMA(()),
        ],
        compiler_params=pltpu.CompilerParams(collective_id=collective_id, has_side_effects=True),
    )(x)


def seq_gathered(piece, seq_ways, collective_ids):
    inner = math.gcd(seq_ways, 8)
    if seq_ways == inner:
        return tp_exchange(piece, inner, True, collective_ids[0], "seq", 1)
    far = tp_exchange(piece, seq_ways // inner, True, collective_ids[1], "seq", inner)
    near = tp_exchange(far, inner, True, collective_ids[0], "seq", 1)
    return jnp.swapaxes(near, 0, 1).reshape((seq_ways,) + piece.shape)


def summed_rows(term_task, own_rows, collective_id):
    ways = lax.axis_size("tp")
    partial = term_task(jnp.int32(0), own_rows * ways)
    pieces = partial.reshape((ways, own_rows) + partial.shape[1:]).astype(jnp.bfloat16)
    arrived = tp_exchange(pieces, ways, False, collective_id)
    return jnp.sum(arrived.astype(jnp.float32), 0)


def gathered_patches(piece, collective_id):
    ways = lax.axis_size("tp")
    whole = tp_exchange(piece, ways, True, collective_id)
    return jnp.transpose(whole, (1, 0, 2, 3)).reshape(
        (piece.shape[0], ways * piece.shape[1]) + piece.shape[2:]
    )


def attention_kernel(meta_ref, lengths_ref, qt_ref, k_ref, v_ref, o_ref, m_sc, l_sc, acc_sc):
    step = pl.program_id(0)
    seq = meta_ref[0]
    width, rows = qt_ref.shape
    span = k_ref.shape[1]
    heads = width // HEAD
    score_scale = 1.0 / math.sqrt(HEAD)

    @pl.when(step == 0)
    def _():
        m_sc[...] = jnp.full(m_sc.shape, MASKED_SCORE, jnp.float32)
        l_sc[...] = jnp.zeros(l_sc.shape, jnp.float32)
        acc_sc[...] = jnp.zeros(acc_sc.shape, jnp.float32)

    def update(diagonal):
        qt = qt_ref[...]
        k = k_ref[...]
        v = v_ref[...]
        feature = lax.broadcasted_iota(jnp.int32, (width, rows), 0)
        key_index = lax.broadcasted_iota(jnp.int32, (span, 1), 0)
        bias = jnp.where(key_index < lengths_ref[step], 0.0, MASKED_SCORE).astype(jnp.float32)
        if diagonal:
            causal = lax.broadcasted_iota(jnp.int32, (span, rows), 0) <= lax.broadcasted_iota(
                jnp.int32, (span, rows), 1
            )
        for h in range(heads):
            in_head = (feature >= h * HEAD) & (feature < (h + 1) * HEAD)
            qt_head = jnp.where(in_head, qt, jnp.zeros_like(qt))
            scores = (
                lax.dot_general(
                    k, qt_head, (((0,), (0,)), ((), ())), preferred_element_type=jnp.float32
                )
                * score_scale
                + bias
            )
            if diagonal:
                scores = jnp.where(causal, scores, MASKED_SCORE)
            m_prev = m_sc[h]
            m_new = jnp.maximum(m_prev, jnp.max(scores, axis=0, keepdims=True))
            weights = jnp.exp(scores - m_new)
            alpha = jnp.exp(m_prev - m_new)
            l_sc[h] = alpha * l_sc[h] + jnp.sum(weights, axis=0, keepdims=True)
            mixed = jnp.dot(v, weights.astype(jnp.bfloat16), preferred_element_type=jnp.float32)
            acc_sc[h] = acc_sc[h] * alpha + mixed
            m_sc[h] = m_new

    @pl.when(step < seq)
    def _():
        update(False)

    @pl.when(step == seq)
    def _():
        update(True)

    @pl.when(step == pl.num_programs(0) - 1)
    def _():
        feature = lax.broadcasted_iota(jnp.int32, (width, rows), 0)
        result = jnp.zeros((width, rows), jnp.float32)
        for h in range(heads):
            in_head = (feature >= h * HEAD) & (feature < (h + 1) * HEAD)
            result = jnp.where(in_head, acc_sc[h] / l_sc[h], result)
        o_ref[...] = result


def causal_attention(query_flat, key_value_all, seq_index, block_lengths, rows_per_block):
    rows, width = query_flat.shape
    span = rows_per_block
    steps = key_value_all.shape[0] // (2 * width)
    heads = width // HEAD
    meta = jnp.reshape(seq_index, (1,)).astype(jnp.int32)
    grid_spec = pltpu.PrefetchScalarGridSpec(
        num_scalar_prefetch=2,
        grid=(steps,),
        in_specs=[
            pl.BlockSpec((width, rows), lambda i, m, n: (0, 0)),
            pl.BlockSpec((width, span), lambda i, m, n: (2 * jnp.minimum(i, m[0]), 0)),
            pl.BlockSpec((width, span), lambda i, m, n: (2 * jnp.minimum(i, m[0]) + 1, 0)),
        ],
        out_specs=pl.BlockSpec((width, rows), lambda i, m, n: (0, 0)),
        scratch_shapes=[
            pltpu.VMEM((heads, 1, rows), jnp.float32),
            pltpu.VMEM((heads, 1, rows), jnp.float32),
            pltpu.VMEM((heads, width, rows), jnp.float32),
        ],
    )
    keys_total = steps * span
    result = pl.pallas_call(
        attention_kernel,
        grid_spec=grid_spec,
        out_shape=jax.ShapeDtypeStruct((width, rows), jnp.float32),
        compiler_params=pltpu.CompilerParams(dimension_semantics=("arbitrary",)),
        cost_estimate=pl.CostEstimate(
            flops=4 * heads * rows * keys_total * width,
            transcendentals=heads * rows * keys_total,
            bytes_accessed=key_value_all.size * 2 + 3 * query_flat.size * 2,
        ),
    )(meta, block_lengths, jnp.transpose(query_flat), key_value_all, key_value_all)
    return jnp.transpose(result).astype(jnp.bfloat16)


def shards(
    pixels,
    text_rows,
    patch_counts,
    picture_starts,
    block_lengths,
    vision_gain,
    vision_project,
    vision_output,
    merge_gain,
    merge_weight,
    text_gain,
    text_project,
    text_output,
):
    seq_ways = lax.axis_size("seq")
    tp_ways = lax.axis_size("tp")
    seq_index = lax.axis_index("seq")
    tp_index = lax.axis_index("tp")
    picture_total, local_patches, model_width = pixels.shape
    patch_total = local_patches * tp_ways
    local_width = vision_project.shape[2]
    head_count = local_width // HEAD
    patch_normed = layer_normed(pixels, vision_gain).astype(jnp.bfloat16)
    packed_project = vision_project.reshape(model_width, 3 * local_width)
    projected = jnp.einsum(
        "npd,de->npe",
        gathered_patches(patch_normed, 0),
        packed_project,
        preferred_element_type=jnp.float32,
    ).astype(jnp.bfloat16)
    queries = projected[..., :local_width].reshape(picture_total, patch_total, head_count, HEAD)
    key_heads = projected[..., local_width : 2 * local_width].reshape(
        picture_total, patch_total, head_count, HEAD
    )
    value_heads = projected[..., 2 * local_width :].reshape(
        picture_total, patch_total, head_count, HEAD
    )
    live_counts = lax.dynamic_slice_in_dim(
        patch_counts, seq_index * picture_total, picture_total, 0
    )
    score_scale = 1.0 / math.sqrt(HEAD)
    scores = (
        jnp.einsum("nqhd,nkhd->nhqk", queries, key_heads, preferred_element_type=jnp.float32)
        * score_scale
    )
    allowed = (jnp.arange(patch_total, dtype=jnp.int32)[None, :] < live_counts[:, None])[
        :, None, None, :
    ]
    scores = jnp.where(allowed, scores, MASKED_SCORE)
    highest = jnp.max(scores, -1, keepdims=True)
    weights = jnp.where(allowed, jnp.exp(scores - highest), 0.0)
    mixture = jnp.einsum(
        "nhqk,nkhd->nqhd",
        weights.astype(jnp.bfloat16),
        value_heads,
        preferred_element_type=jnp.float32,
    )
    mixture = mixture / jnp.transpose(jnp.sum(weights, -1), (0, 2, 1))[..., None]
    attended = mixture.astype(jnp.bfloat16).reshape(picture_total, patch_total, local_width)
    patch_major = jnp.transpose(attended, (1, 0, 2)).reshape(
        patch_total * picture_total, local_width
    )

    def vision_term(offset, row_count):
        return jnp.dot(patch_major, vision_output, preferred_element_type=jnp.float32)

    vision_sum = summed_rows(vision_term, local_patches * picture_total, 2)
    vision_sum = jnp.transpose(
        vision_sum.reshape(local_patches, picture_total, model_width), (1, 0, 2)
    )
    vision_rows = (pixels.astype(jnp.float32) + vision_sum).astype(jnp.bfloat16)
    merge_input = layer_normed(vision_rows, merge_gain).astype(jnp.bfloat16)
    merged_total = patch_total // 4
    input_share = merge_weight.shape[0]
    groups = input_share * tp_ways // model_width
    halves = tp_ways // groups
    outgoing = merge_input.reshape(
        picture_total, local_patches // groups, groups, halves, input_share
    )
    outgoing = jnp.transpose(outgoing, (2, 3, 0, 1, 4)).reshape(
        tp_ways, picture_total, local_patches // groups, input_share
    )
    incoming = tp_exchange(outgoing, tp_ways, False, 1)
    owned_inputs = jnp.transpose(incoming, (1, 0, 2, 3)).reshape(
        picture_total * merged_total, input_share
    )

    def merge_term(offset, row_count):
        return jnp.dot(owned_inputs, merge_weight, preferred_element_type=jnp.float32)

    part_rows = picture_total * merged_total // tp_ways
    visual_part = summed_rows(merge_term, part_rows, 3).astype(jnp.bfloat16)
    rows_per_block = text_rows.shape[0] * tp_ways
    start_table = picture_starts.reshape(seq_ways, picture_total)
    dest_table = start_table // rows_per_block
    picture_rank = tp_index * part_rows // merged_total
    rank_dest = jnp.sum(
        jnp.where(
            jnp.arange(picture_total, dtype=jnp.int32)[None, :] == picture_rank, dest_table, 0
        ),
        1,
    )
    senders = rank_dest == seq_index
    segment = seq_gathered(visual_part, seq_ways, (6, 7)).reshape(-1, model_width)
    row_count = segment.shape[0]
    sources = jnp.arange(row_count, dtype=jnp.int32) // part_rows
    wanted = jnp.any(
        (sources[:, None] == jnp.arange(seq_ways, dtype=jnp.int32)[None, :]) & senders[None, :], 1
    )
    selector = (
        (jnp.arange(row_count, dtype=jnp.int32) % part_rows)[None, :]
        == jnp.arange(part_rows, dtype=jnp.int32)[:, None]
    ) & wanted[None, :]
    arrived = jnp.dot(
        selector.astype(jnp.bfloat16), segment, preferred_element_type=jnp.float32
    ).astype(jnp.bfloat16)
    text_block = lax.all_gather(text_rows, "tp", axis=0, tiled=True)
    visual_block = tp_exchange(arrived, tp_ways, True, 5).reshape(-1, model_width)
    landed = dest_table == seq_index
    local_starts = jnp.sum(jnp.where(landed, start_table - seq_index * rows_per_block, 0), 0)
    live_groups = jnp.sum(
        jnp.where(landed, patch_counts.reshape(seq_ways, picture_total) // 4, 0), 0
    )
    slot_index = jnp.arange(merged_total, dtype=jnp.int32)
    targets = (local_starts[:, None] + slot_index[None, :]).reshape(-1)
    in_use = (slot_index[None, :] < live_groups[:, None]).reshape(-1)
    placement = (jnp.arange(rows_per_block, dtype=jnp.int32)[:, None] == targets[None, :]) & in_use[
        None, :
    ]
    covered = jnp.any(placement, 1)
    placed = jnp.dot(
        placement.astype(jnp.bfloat16), visual_block, preferred_element_type=jnp.float32
    ).astype(jnp.bfloat16)
    embedded = jnp.where(covered[:, None], placed, text_block)
    text_normed = rms_normed(embedded, text_gain).astype(jnp.bfloat16)
    text_heads = jnp.dot(
        text_normed,
        text_project.reshape(model_width, 3 * local_width),
        preferred_element_type=jnp.float32,
    )
    positions = seq_index * rows_per_block + jnp.arange(rows_per_block, dtype=jnp.int32)
    query_rows = rotary(
        text_heads[:, :local_width].reshape(rows_per_block, head_count, HEAD), positions
    ).astype(jnp.bfloat16)
    key_rows = rotary(
        text_heads[:, local_width : 2 * local_width].reshape(rows_per_block, head_count, HEAD),
        positions,
    ).astype(jnp.bfloat16)
    value_rows = text_heads[:, 2 * local_width :].astype(jnp.bfloat16)
    key_flat = key_rows.reshape(rows_per_block, local_width)
    key_value_all = lax.all_gather(
        jnp.concatenate([jnp.transpose(key_flat), jnp.transpose(value_rows)], 0),
        "seq",
        axis=0,
        tiled=True,
    )
    attended_rows = causal_attention(
        query_rows.reshape(rows_per_block, local_width),
        key_value_all,
        seq_index,
        block_lengths,
        rows_per_block,
    )
    own_rows = text_rows.shape[0]

    full_output = lax.all_gather(text_output, "tp", axis=0, tiled=True)
    head_pieces = tp_exchange(
        attended_rows.reshape(tp_ways, own_rows, local_width), tp_ways, False, 4
    )
    mixed_rows = jnp.transpose(head_pieces, (1, 0, 2)).reshape(own_rows, tp_ways * local_width)
    text_sum = jnp.dot(mixed_rows, full_output, preferred_element_type=jnp.float32)
    residual = lax.dynamic_slice_in_dim(embedded, tp_index * own_rows, own_rows, 0)
    hidden = (residual.astype(jnp.float32) + text_sum).astype(jnp.bfloat16)
    return (hidden, key_flat, value_rows)


def solution(mesh):
    placed = (
        P("seq", "tp", None),
        P(("seq", "tp"), None),
        P(),
        P(),
        P(),
        P(),
        P(None, None, "tp"),
        P("tp", None),
        P(),
        P("tp", None),
        P(),
        P(None, None, "tp"),
        P("tp", None),
    )
    return jax.shard_map(
        shards,
        mesh=mesh,
        in_specs=placed,
        out_specs=(P(("seq", "tp"), None), P("seq", "tp"), P("seq", "tp")),
        check_vma=False,
    )
```

```python
import functools
import math

import jax
import jax.numpy as jnp
from jax import lax
from jax.experimental import pallas as pl
from jax.experimental.pallas import tpu as pltpu
from jax.sharding import PartitionSpec as P

HEAD = 104


LN_EPS = 1e-05
RMS_EPS = 1e-06
MASKED_SCORE = -1e30
KEY_SPAN = 512


def layer_normed(row_values, gain_vector):
    floats = row_values.astype(jnp.float32)
    centre = floats - jnp.mean(floats, -1, keepdims=True)
    spread = jnp.mean(centre * centre, -1, keepdims=True)
    return centre * lax.rsqrt(spread + LN_EPS) * gain_vector


def rms_normed(row_values, gain_vector):
    floats = row_values.astype(jnp.float32)
    return floats * lax.rsqrt(jnp.mean(floats * floats, -1, keepdims=True) + RMS_EPS) * gain_vector


def rotary(heads_in, positions):
    halfway = heads_in.shape[-1] // 2
    rates = 10000.0 ** (-2.0 * jnp.arange(halfway, dtype=jnp.float32) / heads_in.shape[-1])
    angles = positions.astype(jnp.float32)[:, None] * rates[None, :]
    cosine_table = jnp.cos(angles)[:, None, :]
    sine_table = jnp.sin(angles)[:, None, :]
    leading = heads_in[..., :halfway]
    trailing = heads_in[..., halfway:]
    return jnp.concatenate(
        [
            leading * cosine_table - trailing * sine_table,
            trailing * cosine_table + leading * sine_table,
        ],
        -1,
    )


MESH_IDS = pl.DeviceIdType.MESH


def exchange_kernel(axis, ways, stride, gather, x_ref, y_ref, send_sem, recv_sem, local_sem):
    position = lax.axis_index(axis)
    me = lax.rem(lax.div(position, stride), ways)
    base = position - me * stride
    other = lax.axis_index("seq" if axis == "tp" else "tp")

    def device(member):
        index = base + member * stride
        return (other, index) if axis == "tp" else (index, other)

    barrier = pltpu.get_barrier_semaphore()
    for shift in range(1, ways):
        peer = lax.rem(me + shift, ways)
        pl.semaphore_signal(barrier, inc=1, device_id=device(peer), device_id_type=MESH_IDS)
    pl.semaphore_wait(barrier, ways - 1)
    sends = []
    for shift in range(1, ways):
        peer = lax.rem(me + shift, ways)
        copy = pltpu.make_async_remote_copy(
            src_ref=x_ref if gather else x_ref.at[peer],
            dst_ref=y_ref.at[me],
            send_sem=send_sem.at[shift],
            recv_sem=recv_sem.at[shift],
            device_id=device(peer),
            device_id_type=MESH_IDS,
        )
        copy.start()
        sends.append(copy)
    local = pltpu.make_async_copy(x_ref if gather else x_ref.at[me], y_ref.at[me], local_sem)
    local.start()
    for copy in sends:
        copy.wait_send()
    for shift in range(1, ways):
        source = lax.rem(me + ways - shift, ways)
        arriving = pltpu.make_async_remote_copy(
            src_ref=x_ref if gather else x_ref.at[source],
            dst_ref=y_ref.at[source],
            send_sem=send_sem.at[shift],
            recv_sem=recv_sem.at[shift],
            device_id=device(source),
            device_id_type=MESH_IDS,
        )
        arriving.wait_recv()
    local.wait()


def tp_exchange(x, ways, gather, collective_id, axis="tp", stride=1):
    piece = x.shape if gather else x.shape[1:]
    return pl.pallas_call(
        functools.partial(exchange_kernel, axis, ways, stride, gather),
        out_shape=jax.ShapeDtypeStruct((ways,) + tuple(piece), x.dtype),
        in_specs=[pl.BlockSpec(memory_space=pl.ANY)],
        out_specs=pl.BlockSpec(memory_space=pl.ANY),
        scratch_shapes=[
            pltpu.SemaphoreType.DMA((ways,)),
            pltpu.SemaphoreType.DMA((ways,)),
            pltpu.SemaphoreType.DMA(()),
        ],
        compiler_params=pltpu.CompilerParams(collective_id=collective_id, has_side_effects=True),
    )(x)


def seq_gathered(piece, seq_ways, collective_ids):
    inner = math.gcd(seq_ways, 8)
    if seq_ways == inner:
        return tp_exchange(piece, inner, True, collective_ids[0], "seq", 1)
    far = tp_exchange(piece, seq_ways // inner, True, collective_ids[1], "seq", inner)
    near = tp_exchange(far, inner, True, collective_ids[0], "seq", 1)
    return jnp.swapaxes(near, 0, 1).reshape((seq_ways,) + piece.shape)


def summed_rows(term_task, own_rows, collective_id):
    ways = lax.axis_size("tp")
    partial = term_task(jnp.int32(0), own_rows * ways)
    pieces = partial.reshape((ways, own_rows) + partial.shape[1:]).astype(jnp.bfloat16)
    arrived = tp_exchange(pieces, ways, False, collective_id)
    return jnp.sum(arrived.astype(jnp.float32), 0)


def gathered_patches(piece, collective_id):
    ways = lax.axis_size("tp")
    whole = tp_exchange(piece, ways, True, collective_id)
    return jnp.transpose(whole, (1, 0, 2, 3)).reshape(
        (piece.shape[0], ways * piece.shape[1]) + piece.shape[2:]
    )


def attention_kernel(meta_ref, lengths_ref, qt_ref, k_ref, v_ref, o_ref, m_sc, l_sc, acc_sc):
    step = pl.program_id(0)
    seq = meta_ref[0]
    width, rows = qt_ref.shape
    span = k_ref.shape[1]
    heads = width // HEAD
    score_scale = 1.0 / math.sqrt(HEAD)

    @pl.when(step == 0)
    def _():
        m_sc[...] = jnp.full(m_sc.shape, MASKED_SCORE, jnp.float32)
        l_sc[...] = jnp.zeros(l_sc.shape, jnp.float32)
        acc_sc[...] = jnp.zeros(acc_sc.shape, jnp.float32)

    def update(diagonal):
        qt = qt_ref[...]
        k = k_ref[...]
        v = v_ref[...]
        feature = lax.broadcasted_iota(jnp.int32, (width, rows), 0)
        key_index = lax.broadcasted_iota(jnp.int32, (span, 1), 0)
        bias = jnp.where(key_index < lengths_ref[step], 0.0, MASKED_SCORE).astype(jnp.float32)
        if diagonal:
            causal = lax.broadcasted_iota(jnp.int32, (span, rows), 0) <= lax.broadcasted_iota(
                jnp.int32, (span, rows), 1
            )
        for h in range(heads):
            in_head = (feature >= h * HEAD) & (feature < (h + 1) * HEAD)
            qt_head = jnp.where(in_head, qt, jnp.zeros_like(qt))
            scores = (
                lax.dot_general(
                    k, qt_head, (((0,), (0,)), ((), ())), preferred_element_type=jnp.float32
                )
                * score_scale
                + bias
            )
            if diagonal:
                scores = jnp.where(causal, scores, MASKED_SCORE)
            m_prev = m_sc[h]
            m_new = jnp.maximum(m_prev, jnp.max(scores, axis=0, keepdims=True))
            weights = jnp.exp(scores - m_new)
            alpha = jnp.exp(m_prev - m_new)
            l_sc[h] = alpha * l_sc[h] + jnp.sum(weights, axis=0, keepdims=True)
            mixed = jnp.dot(v, weights.astype(jnp.bfloat16), preferred_element_type=jnp.float32)
            acc_sc[h] = acc_sc[h] * alpha + mixed
            m_sc[h] = m_new

    @pl.when(step < seq)
    def _():
        update(False)

    @pl.when(step == seq)
    def _():
        update(True)

    @pl.when(step == pl.num_programs(0) - 1)
    def _():
        feature = lax.broadcasted_iota(jnp.int32, (width, rows), 0)
        result = jnp.zeros((width, rows), jnp.float32)
        for h in range(heads):
            in_head = (feature >= h * HEAD) & (feature < (h + 1) * HEAD)
            result = jnp.where(in_head, acc_sc[h] / l_sc[h], result)
        o_ref[...] = result


def causal_attention(query_flat, key_value_all, seq_index, block_lengths, rows_per_block):
    rows, width = query_flat.shape
    span = rows_per_block
    steps = key_value_all.shape[0] // (2 * width)
    heads = width // HEAD
    meta = jnp.reshape(seq_index, (1,)).astype(jnp.int32)
    grid_spec = pltpu.PrefetchScalarGridSpec(
        num_scalar_prefetch=2,
        grid=(steps,),
        in_specs=[
            pl.BlockSpec((width, rows), lambda i, m, n: (0, 0)),
            pl.BlockSpec((width, span), lambda i, m, n: (2 * jnp.minimum(i, m[0]), 0)),
            pl.BlockSpec((width, span), lambda i, m, n: (2 * jnp.minimum(i, m[0]) + 1, 0)),
        ],
        out_specs=pl.BlockSpec((width, rows), lambda i, m, n: (0, 0)),
        scratch_shapes=[
            pltpu.VMEM((heads, 1, rows), jnp.float32),
            pltpu.VMEM((heads, 1, rows), jnp.float32),
            pltpu.VMEM((heads, width, rows), jnp.float32),
        ],
    )
    keys_total = steps * span
    result = pl.pallas_call(
        attention_kernel,
        grid_spec=grid_spec,
        out_shape=jax.ShapeDtypeStruct((width, rows), jnp.float32),
        compiler_params=pltpu.CompilerParams(dimension_semantics=("arbitrary",)),
        cost_estimate=pl.CostEstimate(
            flops=4 * heads * rows * keys_total * width,
            transcendentals=heads * rows * keys_total,
            bytes_accessed=key_value_all.size * 2 + 3 * query_flat.size * 2,
        ),
    )(meta, block_lengths, jnp.transpose(query_flat), key_value_all, key_value_all)
    return jnp.transpose(result).astype(jnp.bfloat16)


def shards(
    pixels,
    text_rows,
    patch_counts,
    picture_starts,
    block_lengths,
    vision_gain,
    vision_project,
    vision_output,
    merge_gain,
    merge_weight,
    text_gain,
    text_project,
    text_output,
):
    seq_ways = lax.axis_size("seq")
    tp_ways = lax.axis_size("tp")
    seq_index = lax.axis_index("seq")
    tp_index = lax.axis_index("tp")
    picture_total, local_patches, model_width = pixels.shape
    patch_total = local_patches * tp_ways
    local_width = vision_project.shape[2]
    head_count = local_width // HEAD
    patch_normed = layer_normed(pixels, vision_gain).astype(jnp.bfloat16)
    packed_project = vision_project.reshape(model_width, 3 * local_width)
    projected = jnp.einsum(
        "npd,de->npe",
        gathered_patches(patch_normed, 0),
        packed_project,
        preferred_element_type=jnp.float32,
    ).astype(jnp.bfloat16)
    queries = projected[..., :local_width].reshape(picture_total, patch_total, head_count, HEAD)
    key_heads = projected[..., local_width : 2 * local_width].reshape(
        picture_total, patch_total, head_count, HEAD
    )
    value_heads = projected[..., 2 * local_width :].reshape(
        picture_total, patch_total, head_count, HEAD
    )
    live_counts = lax.dynamic_slice_in_dim(
        patch_counts, seq_index * picture_total, picture_total, 0
    )
    score_scale = 1.0 / math.sqrt(HEAD)
    scores = (
        jnp.einsum("nqhd,nkhd->nhqk", queries, key_heads, preferred_element_type=jnp.float32)
        * score_scale
    )
    allowed = (jnp.arange(patch_total, dtype=jnp.int32)[None, :] < live_counts[:, None])[
        :, None, None, :
    ]
    scores = jnp.where(allowed, scores, MASKED_SCORE)
    highest = jnp.max(scores, -1, keepdims=True)
    weights = jnp.where(allowed, jnp.exp(scores - highest), 0.0)
    mixture = jnp.einsum(
        "nhqk,nkhd->nqhd",
        weights.astype(jnp.bfloat16),
        value_heads,
        preferred_element_type=jnp.float32,
    )
    mixture = mixture / jnp.transpose(jnp.sum(weights, -1), (0, 2, 1))[..., None]
    attended = mixture.astype(jnp.bfloat16).reshape(picture_total, patch_total, local_width)
    patch_major = jnp.transpose(attended, (1, 0, 2)).reshape(
        patch_total * picture_total, local_width
    )

    def vision_term(offset, row_count):
        return jnp.dot(patch_major, vision_output, preferred_element_type=jnp.float32)

    vision_sum = summed_rows(vision_term, local_patches * picture_total, 2)
    vision_sum = jnp.transpose(
        vision_sum.reshape(local_patches, picture_total, model_width), (1, 0, 2)
    )
    vision_rows = (pixels.astype(jnp.float32) + vision_sum).astype(jnp.bfloat16)
    merge_input = layer_normed(vision_rows, merge_gain).astype(jnp.bfloat16)
    merged_total = patch_total // 4
    input_share = merge_weight.shape[0]
    groups = input_share * tp_ways // model_width
    halves = tp_ways // groups
    outgoing = merge_input.reshape(
        picture_total, local_patches // groups, groups, halves, input_share
    )
    outgoing = jnp.transpose(outgoing, (2, 3, 0, 1, 4)).reshape(
        tp_ways, picture_total, local_patches // groups, input_share
    )
    incoming = tp_exchange(outgoing, tp_ways, False, 1)
    owned_inputs = jnp.transpose(incoming, (1, 0, 2, 3)).reshape(
        picture_total * merged_total, input_share
    )

    def merge_term(offset, row_count):
        return jnp.dot(owned_inputs, merge_weight, preferred_element_type=jnp.float32)

    part_rows = picture_total * merged_total // tp_ways
    visual_part = summed_rows(merge_term, part_rows, 3).astype(jnp.bfloat16)
    rows_per_block = text_rows.shape[0] * tp_ways
    start_table = picture_starts.reshape(seq_ways, picture_total)
    dest_table = start_table // rows_per_block
    picture_rank = tp_index * part_rows // merged_total
    rank_dest = jnp.sum(
        jnp.where(
            jnp.arange(picture_total, dtype=jnp.int32)[None, :] == picture_rank, dest_table, 0
        ),
        1,
    )
    senders = rank_dest == seq_index
    segment = seq_gathered(visual_part, seq_ways, (6, 7)).reshape(-1, model_width)
    full_output = lax.all_gather(text_output, "tp", axis=0, tiled=True)
    full_output, segment = lax.optimization_barrier((full_output, segment))
    row_count = segment.shape[0]
    sources = jnp.arange(row_count, dtype=jnp.int32) // part_rows
    wanted = jnp.any(
        (sources[:, None] == jnp.arange(seq_ways, dtype=jnp.int32)[None, :]) & senders[None, :], 1
    )
    selector = (
        (jnp.arange(row_count, dtype=jnp.int32) % part_rows)[None, :]
        == jnp.arange(part_rows, dtype=jnp.int32)[:, None]
    ) & wanted[None, :]
    arrived = jnp.dot(
        selector.astype(jnp.bfloat16), segment, preferred_element_type=jnp.float32
    ).astype(jnp.bfloat16)
    text_block = lax.all_gather(text_rows, "tp", axis=0, tiled=True)
    visual_block = tp_exchange(arrived, tp_ways, True, 5).reshape(-1, model_width)
    landed = dest_table == seq_index
    local_starts = jnp.sum(jnp.where(landed, start_table - seq_index * rows_per_block, 0), 0)
    live_groups = jnp.sum(
        jnp.where(landed, patch_counts.reshape(seq_ways, picture_total) // 4, 0), 0
    )
    slot_index = jnp.arange(merged_total, dtype=jnp.int32)
    targets = (local_starts[:, None] + slot_index[None, :]).reshape(-1)
    in_use = (slot_index[None, :] < live_groups[:, None]).reshape(-1)
    placement = (jnp.arange(rows_per_block, dtype=jnp.int32)[:, None] == targets[None, :]) & in_use[
        None, :
    ]
    covered = jnp.any(placement, 1)
    placed = jnp.dot(
        placement.astype(jnp.bfloat16), visual_block, preferred_element_type=jnp.float32
    ).astype(jnp.bfloat16)
    embedded = jnp.where(covered[:, None], placed, text_block)
    text_normed = rms_normed(embedded, text_gain).astype(jnp.bfloat16)
    text_heads = jnp.dot(
        text_normed,
        text_project.reshape(model_width, 3 * local_width),
        preferred_element_type=jnp.float32,
    )
    positions = seq_index * rows_per_block + jnp.arange(rows_per_block, dtype=jnp.int32)
    query_rows = rotary(
        text_heads[:, :local_width].reshape(rows_per_block, head_count, HEAD), positions
    ).astype(jnp.bfloat16)
    key_rows = rotary(
        text_heads[:, local_width : 2 * local_width].reshape(rows_per_block, head_count, HEAD),
        positions,
    ).astype(jnp.bfloat16)
    value_rows = text_heads[:, 2 * local_width :].astype(jnp.bfloat16)
    key_flat = key_rows.reshape(rows_per_block, local_width)
    key_value_all = lax.all_gather(
        jnp.concatenate([jnp.transpose(key_flat), jnp.transpose(value_rows)], 0),
        "seq",
        axis=0,
        tiled=True,
    )
    attended_rows = causal_attention(
        query_rows.reshape(rows_per_block, local_width),
        key_value_all,
        seq_index,
        block_lengths,
        rows_per_block,
    )
    own_rows = text_rows.shape[0]

    head_pieces = tp_exchange(
        attended_rows.reshape(tp_ways, own_rows, local_width), tp_ways, False, 4
    )
    mixed_rows = jnp.transpose(head_pieces, (1, 0, 2)).reshape(own_rows, tp_ways * local_width)
    text_sum = jnp.dot(mixed_rows, full_output, preferred_element_type=jnp.float32)
    residual = lax.dynamic_slice_in_dim(embedded, tp_index * own_rows, own_rows, 0)
    hidden = (residual.astype(jnp.float32) + text_sum).astype(jnp.bfloat16)
    return (hidden, key_flat, value_rows)


def solution(mesh):
    placed = (
        P("seq", "tp", None),
        P(("seq", "tp"), None),
        P(),
        P(),
        P(),
        P(),
        P(None, None, "tp"),
        P("tp", None),
        P(),
        P("tp", None),
        P(),
        P(None, None, "tp"),
        P("tp", None),
    )
    return jax.shard_map(
        shards,
        mesh=mesh,
        in_specs=placed,
        out_specs=(P(("seq", "tp"), None), P("seq", "tp"), P("seq", "tp")),
        check_vma=False,
    )
```

```python
import functools
import math

import jax
import jax.numpy as jnp
from jax import lax
from jax.experimental import pallas as pl
from jax.experimental.pallas import tpu as pltpu
from jax.sharding import PartitionSpec as P

HEAD = 104


LN_EPS = 1e-05
RMS_EPS = 1e-06
MASKED_SCORE = -1e30
KEY_SPAN = 512


def layer_normed(row_values, gain_vector):
    floats = row_values.astype(jnp.float32)
    centre = floats - jnp.mean(floats, -1, keepdims=True)
    spread = jnp.mean(centre * centre, -1, keepdims=True)
    return centre * lax.rsqrt(spread + LN_EPS) * gain_vector


def rms_normed(row_values, gain_vector):
    floats = row_values.astype(jnp.float32)
    return floats * lax.rsqrt(jnp.mean(floats * floats, -1, keepdims=True) + RMS_EPS) * gain_vector


def rotary(heads_in, positions):
    halfway = heads_in.shape[-1] // 2
    rates = 10000.0 ** (-2.0 * jnp.arange(halfway, dtype=jnp.float32) / heads_in.shape[-1])
    angles = positions.astype(jnp.float32)[:, None] * rates[None, :]
    cosine_table = jnp.cos(angles)[:, None, :]
    sine_table = jnp.sin(angles)[:, None, :]
    leading = heads_in[..., :halfway]
    trailing = heads_in[..., halfway:]
    return jnp.concatenate(
        [
            leading * cosine_table - trailing * sine_table,
            trailing * cosine_table + leading * sine_table,
        ],
        -1,
    )


MESH_IDS = pl.DeviceIdType.MESH


def exchange_kernel(axis, ways, stride, gather, x_ref, y_ref, send_sem, recv_sem, local_sem):
    position = lax.axis_index(axis)
    me = lax.rem(lax.div(position, stride), ways)
    base = position - me * stride
    other = lax.axis_index("seq" if axis == "tp" else "tp")

    def device(member):
        index = base + member * stride
        return (other, index) if axis == "tp" else (index, other)

    barrier = pltpu.get_barrier_semaphore()
    for shift in range(1, ways):
        peer = lax.rem(me + shift, ways)
        pl.semaphore_signal(barrier, inc=1, device_id=device(peer), device_id_type=MESH_IDS)
    pl.semaphore_wait(barrier, ways - 1)
    sends = []
    for shift in range(1, ways):
        peer = lax.rem(me + shift, ways)
        copy = pltpu.make_async_remote_copy(
            src_ref=x_ref if gather else x_ref.at[peer],
            dst_ref=y_ref.at[me],
            send_sem=send_sem.at[shift],
            recv_sem=recv_sem.at[shift],
            device_id=device(peer),
            device_id_type=MESH_IDS,
        )
        copy.start()
        sends.append(copy)
    local = pltpu.make_async_copy(x_ref if gather else x_ref.at[me], y_ref.at[me], local_sem)
    local.start()
    for copy in sends:
        copy.wait_send()
    for shift in range(1, ways):
        source = lax.rem(me + ways - shift, ways)
        arriving = pltpu.make_async_remote_copy(
            src_ref=x_ref if gather else x_ref.at[source],
            dst_ref=y_ref.at[source],
            send_sem=send_sem.at[shift],
            recv_sem=recv_sem.at[shift],
            device_id=device(source),
            device_id_type=MESH_IDS,
        )
        arriving.wait_recv()
    local.wait()


def tp_exchange(x, ways, gather, collective_id, axis="tp", stride=1):
    piece = x.shape if gather else x.shape[1:]
    return pl.pallas_call(
        functools.partial(exchange_kernel, axis, ways, stride, gather),
        out_shape=jax.ShapeDtypeStruct((ways,) + tuple(piece), x.dtype),
        in_specs=[pl.BlockSpec(memory_space=pl.ANY)],
        out_specs=pl.BlockSpec(memory_space=pl.ANY),
        scratch_shapes=[
            pltpu.SemaphoreType.DMA((ways,)),
            pltpu.SemaphoreType.DMA((ways,)),
            pltpu.SemaphoreType.DMA(()),
        ],
        compiler_params=pltpu.CompilerParams(collective_id=collective_id, has_side_effects=True),
    )(x)


def seq_gathered(piece, seq_ways, collective_ids):
    inner = math.gcd(seq_ways, 8)
    if seq_ways == inner:
        return tp_exchange(piece, inner, True, collective_ids[0], "seq", 1)
    far = tp_exchange(piece, seq_ways // inner, True, collective_ids[1], "seq", inner)
    near = tp_exchange(far, inner, True, collective_ids[0], "seq", 1)
    return jnp.swapaxes(near, 0, 1).reshape((seq_ways,) + piece.shape)


def summed_rows(term_task, own_rows, collective_id):
    ways = lax.axis_size("tp")
    partial = term_task(jnp.int32(0), own_rows * ways)
    pieces = partial.reshape((ways, own_rows) + partial.shape[1:]).astype(jnp.bfloat16)
    arrived = tp_exchange(pieces, ways, False, collective_id)
    return jnp.sum(arrived.astype(jnp.float32), 0)


def gathered_patches(piece, collective_id):
    ways = lax.axis_size("tp")
    whole = tp_exchange(piece, ways, True, collective_id)
    return jnp.transpose(whole, (1, 0, 2, 3)).reshape(
        (piece.shape[0], ways * piece.shape[1]) + piece.shape[2:]
    )


def attention_kernel(meta_ref, lengths_ref, qt_ref, k_ref, v_ref, o_ref, m_sc, l_sc, acc_sc):
    step = pl.program_id(0)
    seq = meta_ref[0]
    width, rows = qt_ref.shape
    span = k_ref.shape[1]
    heads = width // HEAD
    score_scale = 1.0 / math.sqrt(HEAD)

    @pl.when(step == 0)
    def _():
        m_sc[...] = jnp.full(m_sc.shape, MASKED_SCORE, jnp.float32)
        l_sc[...] = jnp.zeros(l_sc.shape, jnp.float32)
        acc_sc[...] = jnp.zeros(acc_sc.shape, jnp.float32)

    def update(diagonal):
        qt = qt_ref[...]
        k = k_ref[...]
        v = v_ref[...]
        feature = lax.broadcasted_iota(jnp.int32, (width, rows), 0)
        key_index = lax.broadcasted_iota(jnp.int32, (span, 1), 0)
        bias = jnp.where(key_index < lengths_ref[step], 0.0, MASKED_SCORE).astype(jnp.float32)
        if diagonal:
            causal = lax.broadcasted_iota(jnp.int32, (span, rows), 0) <= lax.broadcasted_iota(
                jnp.int32, (span, rows), 1
            )
        for h in range(heads):
            in_head = (feature >= h * HEAD) & (feature < (h + 1) * HEAD)
            qt_head = jnp.where(in_head, qt, jnp.zeros_like(qt))
            scores = (
                lax.dot_general(
                    k, qt_head, (((0,), (0,)), ((), ())), preferred_element_type=jnp.float32
                )
                * score_scale
                + bias
            )
            if diagonal:
                scores = jnp.where(causal, scores, MASKED_SCORE)
            m_prev = m_sc[h]
            m_new = jnp.maximum(m_prev, jnp.max(scores, axis=0, keepdims=True))
            weights = jnp.exp(scores - m_new)
            alpha = jnp.exp(m_prev - m_new)
            l_sc[h] = alpha * l_sc[h] + jnp.sum(weights, axis=0, keepdims=True)
            mixed = jnp.dot(v, weights.astype(jnp.bfloat16), preferred_element_type=jnp.float32)
            acc_sc[h] = acc_sc[h] * alpha + mixed
            m_sc[h] = m_new

    @pl.when(step < seq)
    def _():
        update(False)

    @pl.when(step == seq)
    def _():
        update(True)

    @pl.when(step == pl.num_programs(0) - 1)
    def _():
        feature = lax.broadcasted_iota(jnp.int32, (width, rows), 0)
        result = jnp.zeros((width, rows), jnp.float32)
        for h in range(heads):
            in_head = (feature >= h * HEAD) & (feature < (h + 1) * HEAD)
            result = jnp.where(in_head, acc_sc[h] / l_sc[h], result)
        o_ref[...] = result


def causal_attention(query_flat, key_value_all, seq_index, block_lengths, rows_per_block):
    rows, width = query_flat.shape
    span = rows_per_block
    steps = key_value_all.shape[0] // (2 * width)
    heads = width // HEAD
    meta = jnp.reshape(seq_index, (1,)).astype(jnp.int32)
    grid_spec = pltpu.PrefetchScalarGridSpec(
        num_scalar_prefetch=2,
        grid=(steps,),
        in_specs=[
            pl.BlockSpec((width, rows), lambda i, m, n: (0, 0)),
            pl.BlockSpec((width, span), lambda i, m, n: (2 * jnp.minimum(i, m[0]), 0)),
            pl.BlockSpec((width, span), lambda i, m, n: (2 * jnp.minimum(i, m[0]) + 1, 0)),
        ],
        out_specs=pl.BlockSpec((width, rows), lambda i, m, n: (0, 0)),
        scratch_shapes=[
            pltpu.VMEM((heads, 1, rows), jnp.float32),
            pltpu.VMEM((heads, 1, rows), jnp.float32),
            pltpu.VMEM((heads, width, rows), jnp.float32),
        ],
    )
    keys_total = steps * span
    result = pl.pallas_call(
        attention_kernel,
        grid_spec=grid_spec,
        out_shape=jax.ShapeDtypeStruct((width, rows), jnp.float32),
        compiler_params=pltpu.CompilerParams(dimension_semantics=("arbitrary",)),
        cost_estimate=pl.CostEstimate(
            flops=4 * heads * rows * keys_total * width,
            transcendentals=heads * rows * keys_total,
            bytes_accessed=key_value_all.size * 2 + 3 * query_flat.size * 2,
        ),
    )(meta, block_lengths, jnp.transpose(query_flat), key_value_all, key_value_all)
    return jnp.transpose(result).astype(jnp.bfloat16)


def shards(
    pixels,
    text_rows,
    patch_counts,
    picture_starts,
    block_lengths,
    vision_gain,
    vision_project,
    vision_output,
    merge_gain,
    merge_weight,
    text_gain,
    text_project,
    text_output,
):
    seq_ways = lax.axis_size("seq")
    tp_ways = lax.axis_size("tp")
    seq_index = lax.axis_index("seq")
    tp_index = lax.axis_index("tp")
    picture_total, local_patches, model_width = pixels.shape
    patch_total = local_patches * tp_ways
    local_width = vision_project.shape[2]
    head_count = local_width // HEAD
    patch_normed = layer_normed(pixels, vision_gain).astype(jnp.bfloat16)
    packed_project = vision_project.reshape(model_width, 3 * local_width)
    projected = jnp.einsum(
        "npd,de->npe",
        gathered_patches(patch_normed, 0),
        packed_project,
        preferred_element_type=jnp.float32,
    ).astype(jnp.bfloat16)
    queries = projected[..., :local_width].reshape(picture_total, patch_total, head_count, HEAD)
    key_heads = projected[..., local_width : 2 * local_width].reshape(
        picture_total, patch_total, head_count, HEAD
    )
    value_heads = projected[..., 2 * local_width :].reshape(
        picture_total, patch_total, head_count, HEAD
    )
    live_counts = lax.dynamic_slice_in_dim(
        patch_counts, seq_index * picture_total, picture_total, 0
    )
    score_scale = 1.0 / math.sqrt(HEAD)
    scores = (
        jnp.einsum("nqhd,nkhd->nhqk", queries, key_heads, preferred_element_type=jnp.float32)
        * score_scale
    )
    allowed = (jnp.arange(patch_total, dtype=jnp.int32)[None, :] < live_counts[:, None])[
        :, None, None, :
    ]
    scores = jnp.where(allowed, scores, MASKED_SCORE)
    highest = jnp.max(scores, -1, keepdims=True)
    weights = jnp.where(allowed, jnp.exp(scores - highest), 0.0)
    mixture = jnp.einsum(
        "nhqk,nkhd->nqhd",
        weights.astype(jnp.bfloat16),
        value_heads,
        preferred_element_type=jnp.float32,
    )
    mixture = mixture / jnp.transpose(jnp.sum(weights, -1), (0, 2, 1))[..., None]
    attended = mixture.astype(jnp.bfloat16).reshape(picture_total, patch_total, local_width)
    patch_major = jnp.transpose(attended, (1, 0, 2)).reshape(
        patch_total * picture_total, local_width
    )

    def vision_term(offset, row_count):
        return jnp.dot(patch_major, vision_output, preferred_element_type=jnp.float32)

    vision_sum = summed_rows(vision_term, local_patches * picture_total, 2)
    vision_sum = jnp.transpose(
        vision_sum.reshape(local_patches, picture_total, model_width), (1, 0, 2)
    )
    vision_rows = (pixels.astype(jnp.float32) + vision_sum).astype(jnp.bfloat16)
    merge_input = layer_normed(vision_rows, merge_gain).astype(jnp.bfloat16)
    merged_total = patch_total // 4
    input_share = merge_weight.shape[0]
    groups = input_share * tp_ways // model_width
    halves = tp_ways // groups
    outgoing = merge_input.reshape(
        picture_total, local_patches // groups, groups, halves, input_share
    )
    outgoing = jnp.transpose(outgoing, (2, 3, 0, 1, 4)).reshape(
        tp_ways, picture_total, local_patches // groups, input_share
    )
    incoming = tp_exchange(outgoing, tp_ways, False, 1)
    owned_inputs = jnp.transpose(incoming, (1, 0, 2, 3)).reshape(
        picture_total * merged_total, input_share
    )

    def merge_term(offset, row_count):
        return jnp.dot(owned_inputs, merge_weight, preferred_element_type=jnp.float32)

    part_rows = picture_total * merged_total // tp_ways
    visual_part = summed_rows(merge_term, part_rows, 3).astype(jnp.bfloat16)
    rows_per_block = text_rows.shape[0] * tp_ways
    start_table = picture_starts.reshape(seq_ways, picture_total)
    dest_table = start_table // rows_per_block
    picture_rank = tp_index * part_rows // merged_total
    rank_dest = jnp.sum(
        jnp.where(
            jnp.arange(picture_total, dtype=jnp.int32)[None, :] == picture_rank, dest_table, 0
        ),
        1,
    )
    senders = rank_dest == seq_index
    late_output, visual_part = lax.optimization_barrier((text_output, visual_part))
    full_output = lax.all_gather(late_output, "tp", axis=0, tiled=True)
    segment = seq_gathered(visual_part, seq_ways, (6, 7)).reshape(-1, model_width)
    row_count = segment.shape[0]
    sources = jnp.arange(row_count, dtype=jnp.int32) // part_rows
    wanted = jnp.any(
        (sources[:, None] == jnp.arange(seq_ways, dtype=jnp.int32)[None, :]) & senders[None, :], 1
    )
    selector = (
        (jnp.arange(row_count, dtype=jnp.int32) % part_rows)[None, :]
        == jnp.arange(part_rows, dtype=jnp.int32)[:, None]
    ) & wanted[None, :]
    arrived = jnp.dot(
        selector.astype(jnp.bfloat16), segment, preferred_element_type=jnp.float32
    ).astype(jnp.bfloat16)
    text_block = lax.all_gather(text_rows, "tp", axis=0, tiled=True)
    visual_block = tp_exchange(arrived, tp_ways, True, 5).reshape(-1, model_width)
    landed = dest_table == seq_index
    local_starts = jnp.sum(jnp.where(landed, start_table - seq_index * rows_per_block, 0), 0)
    live_groups = jnp.sum(
        jnp.where(landed, patch_counts.reshape(seq_ways, picture_total) // 4, 0), 0
    )
    slot_index = jnp.arange(merged_total, dtype=jnp.int32)
    targets = (local_starts[:, None] + slot_index[None, :]).reshape(-1)
    in_use = (slot_index[None, :] < live_groups[:, None]).reshape(-1)
    placement = (jnp.arange(rows_per_block, dtype=jnp.int32)[:, None] == targets[None, :]) & in_use[
        None, :
    ]
    covered = jnp.any(placement, 1)
    placed = jnp.dot(
        placement.astype(jnp.bfloat16), visual_block, preferred_element_type=jnp.float32
    ).astype(jnp.bfloat16)
    embedded = jnp.where(covered[:, None], placed, text_block)
    full_output, embedded = lax.optimization_barrier((full_output, embedded))
    text_normed = rms_normed(embedded, text_gain).astype(jnp.bfloat16)
    text_heads = jnp.dot(
        text_normed,
        text_project.reshape(model_width, 3 * local_width),
        preferred_element_type=jnp.float32,
    )
    positions = seq_index * rows_per_block + jnp.arange(rows_per_block, dtype=jnp.int32)
    query_rows = rotary(
        text_heads[:, :local_width].reshape(rows_per_block, head_count, HEAD), positions
    ).astype(jnp.bfloat16)
    key_rows = rotary(
        text_heads[:, local_width : 2 * local_width].reshape(rows_per_block, head_count, HEAD),
        positions,
    ).astype(jnp.bfloat16)
    value_rows = text_heads[:, 2 * local_width :].astype(jnp.bfloat16)
    key_flat = key_rows.reshape(rows_per_block, local_width)
    key_value_all = lax.all_gather(
        jnp.concatenate([jnp.transpose(key_flat), jnp.transpose(value_rows)], 0),
        "seq",
        axis=0,
        tiled=True,
    )
    attended_rows = causal_attention(
        query_rows.reshape(rows_per_block, local_width),
        key_value_all,
        seq_index,
        block_lengths,
        rows_per_block,
    )
    own_rows = text_rows.shape[0]

    head_pieces = tp_exchange(
        attended_rows.reshape(tp_ways, own_rows, local_width), tp_ways, False, 4
    )
    mixed_rows = jnp.transpose(head_pieces, (1, 0, 2)).reshape(own_rows, tp_ways * local_width)
    text_sum = jnp.dot(mixed_rows, full_output, preferred_element_type=jnp.float32)
    residual = lax.dynamic_slice_in_dim(embedded, tp_index * own_rows, own_rows, 0)
    hidden = (residual.astype(jnp.float32) + text_sum).astype(jnp.bfloat16)
    return (hidden, key_flat, value_rows)


def solution(mesh):
    placed = (
        P("seq", "tp", None),
        P(("seq", "tp"), None),
        P(),
        P(),
        P(),
        P(),
        P(None, None, "tp"),
        P("tp", None),
        P(),
        P("tp", None),
        P(),
        P(None, None, "tp"),
        P("tp", None),
    )
    return jax.shard_map(
        shards,
        mesh=mesh,
        in_specs=placed,
        out_specs=(P(("seq", "tp"), None), P("seq", "tp"), P("seq", "tp")),
        check_vma=False,
    )
```

```python
import functools
import math

import jax
import jax.numpy as jnp
from jax import lax
from jax.experimental import pallas as pl
from jax.experimental.pallas import tpu as pltpu
from jax.sharding import PartitionSpec as P

HEAD = 104


LN_EPS = 1e-05
RMS_EPS = 1e-06
MASKED_SCORE = -1e30
KEY_SPAN = 512


def layer_normed(row_values, gain_vector):
    floats = row_values.astype(jnp.float32)
    centre = floats - jnp.mean(floats, -1, keepdims=True)
    spread = jnp.mean(centre * centre, -1, keepdims=True)
    return centre * lax.rsqrt(spread + LN_EPS) * gain_vector


def rms_normed(row_values, gain_vector):
    floats = row_values.astype(jnp.float32)
    return floats * lax.rsqrt(jnp.mean(floats * floats, -1, keepdims=True) + RMS_EPS) * gain_vector


def rotary(heads_in, positions):
    halfway = heads_in.shape[-1] // 2
    rates = 10000.0 ** (-2.0 * jnp.arange(halfway, dtype=jnp.float32) / heads_in.shape[-1])
    angles = positions.astype(jnp.float32)[:, None] * rates[None, :]
    cosine_table = jnp.cos(angles)[:, None, :]
    sine_table = jnp.sin(angles)[:, None, :]
    leading = heads_in[..., :halfway]
    trailing = heads_in[..., halfway:]
    return jnp.concatenate(
        [
            leading * cosine_table - trailing * sine_table,
            trailing * cosine_table + leading * sine_table,
        ],
        -1,
    )


MESH_IDS = pl.DeviceIdType.MESH


def exchange_kernel(axis, ways, stride, gather, x_ref, y_ref, send_sem, recv_sem, local_sem):
    position = lax.axis_index(axis)
    me = lax.rem(lax.div(position, stride), ways)
    base = position - me * stride
    other = lax.axis_index("seq" if axis == "tp" else "tp")

    def device(member):
        index = base + member * stride
        return (other, index) if axis == "tp" else (index, other)

    barrier = pltpu.get_barrier_semaphore()
    for shift in range(1, ways):
        peer = lax.rem(me + shift, ways)
        pl.semaphore_signal(barrier, inc=1, device_id=device(peer), device_id_type=MESH_IDS)
    pl.semaphore_wait(barrier, ways - 1)
    sends = []
    for shift in range(1, ways):
        peer = lax.rem(me + shift, ways)
        copy = pltpu.make_async_remote_copy(
            src_ref=x_ref if gather else x_ref.at[peer],
            dst_ref=y_ref.at[me],
            send_sem=send_sem.at[shift],
            recv_sem=recv_sem.at[shift],
            device_id=device(peer),
            device_id_type=MESH_IDS,
        )
        copy.start()
        sends.append(copy)
    local = pltpu.make_async_copy(x_ref if gather else x_ref.at[me], y_ref.at[me], local_sem)
    local.start()
    for copy in sends:
        copy.wait_send()
    for shift in range(1, ways):
        source = lax.rem(me + ways - shift, ways)
        arriving = pltpu.make_async_remote_copy(
            src_ref=x_ref if gather else x_ref.at[source],
            dst_ref=y_ref.at[source],
            send_sem=send_sem.at[shift],
            recv_sem=recv_sem.at[shift],
            device_id=device(source),
            device_id_type=MESH_IDS,
        )
        arriving.wait_recv()
    local.wait()


def tp_exchange(x, ways, gather, collective_id, axis="tp", stride=1):
    piece = x.shape if gather else x.shape[1:]
    return pl.pallas_call(
        functools.partial(exchange_kernel, axis, ways, stride, gather),
        out_shape=jax.ShapeDtypeStruct((ways,) + tuple(piece), x.dtype),
        in_specs=[pl.BlockSpec(memory_space=pl.ANY)],
        out_specs=pl.BlockSpec(memory_space=pl.ANY),
        scratch_shapes=[
            pltpu.SemaphoreType.DMA((ways,)),
            pltpu.SemaphoreType.DMA((ways,)),
            pltpu.SemaphoreType.DMA(()),
        ],
        compiler_params=pltpu.CompilerParams(collective_id=collective_id, has_side_effects=True),
    )(x)


def seq_gathered(piece, seq_ways, collective_ids):
    inner = math.gcd(seq_ways, 8)
    if seq_ways == inner:
        return tp_exchange(piece, inner, True, collective_ids[0], "seq", 1)
    far = tp_exchange(piece, seq_ways // inner, True, collective_ids[1], "seq", inner)
    near = tp_exchange(far, inner, True, collective_ids[0], "seq", 1)
    return jnp.swapaxes(near, 0, 1).reshape((seq_ways,) + piece.shape)


def summed_rows(term_task, own_rows, collective_id):
    ways = lax.axis_size("tp")
    partial = term_task(jnp.int32(0), own_rows * ways)
    pieces = partial.reshape((ways, own_rows) + partial.shape[1:]).astype(jnp.bfloat16)
    arrived = tp_exchange(pieces, ways, False, collective_id)
    return jnp.sum(arrived.astype(jnp.float32), 0)


def gathered_patches(piece, collective_id):
    ways = lax.axis_size("tp")
    whole = tp_exchange(piece, ways, True, collective_id)
    return jnp.transpose(whole, (1, 0, 2, 3)).reshape(
        (piece.shape[0], ways * piece.shape[1]) + piece.shape[2:]
    )


def attention_kernel(meta_ref, lengths_ref, qt_ref, k_ref, v_ref, o_ref, m_sc, l_sc, acc_sc):
    step = pl.program_id(0)
    seq = meta_ref[0]
    width, rows = qt_ref.shape
    span = k_ref.shape[1]
    heads = width // HEAD
    score_scale = 1.0 / math.sqrt(HEAD)

    @pl.when(step == 0)
    def _():
        m_sc[...] = jnp.full(m_sc.shape, MASKED_SCORE, jnp.float32)
        l_sc[...] = jnp.zeros(l_sc.shape, jnp.float32)
        acc_sc[...] = jnp.zeros(acc_sc.shape, jnp.float32)

    def update(diagonal):
        qt = qt_ref[...]
        k = k_ref[...]
        v = v_ref[...]
        feature = lax.broadcasted_iota(jnp.int32, (width, rows), 0)
        key_index = lax.broadcasted_iota(jnp.int32, (span, 1), 0)
        bias = jnp.where(key_index < lengths_ref[step], 0.0, MASKED_SCORE).astype(jnp.float32)
        if diagonal:
            causal = lax.broadcasted_iota(jnp.int32, (span, rows), 0) <= lax.broadcasted_iota(
                jnp.int32, (span, rows), 1
            )
        for h in range(heads):
            in_head = (feature >= h * HEAD) & (feature < (h + 1) * HEAD)
            qt_head = jnp.where(in_head, qt, jnp.zeros_like(qt))
            scores = (
                lax.dot_general(
                    k, qt_head, (((0,), (0,)), ((), ())), preferred_element_type=jnp.float32
                )
                * score_scale
                + bias
            )
            if diagonal:
                scores = jnp.where(causal, scores, MASKED_SCORE)
            m_prev = m_sc[h]
            m_new = jnp.maximum(m_prev, jnp.max(scores, axis=0, keepdims=True))
            weights = jnp.exp(scores - m_new)
            alpha = jnp.exp(m_prev - m_new)
            l_sc[h] = alpha * l_sc[h] + jnp.sum(weights, axis=0, keepdims=True)
            mixed = jnp.dot(v, weights.astype(jnp.bfloat16), preferred_element_type=jnp.float32)
            acc_sc[h] = acc_sc[h] * alpha + mixed
            m_sc[h] = m_new

    @pl.when(step < seq)
    def _():
        update(False)

    @pl.when(step == seq)
    def _():
        update(True)

    @pl.when(step == pl.num_programs(0) - 1)
    def _():
        feature = lax.broadcasted_iota(jnp.int32, (width, rows), 0)
        result = jnp.zeros((width, rows), jnp.float32)
        for h in range(heads):
            in_head = (feature >= h * HEAD) & (feature < (h + 1) * HEAD)
            result = jnp.where(in_head, acc_sc[h] / l_sc[h], result)
        o_ref[...] = result


def causal_attention(query_flat, key_value_all, seq_index, block_lengths, rows_per_block):
    rows, width = query_flat.shape
    span = rows_per_block
    steps = key_value_all.shape[0] // (2 * width)
    heads = width // HEAD
    meta = jnp.reshape(seq_index, (1,)).astype(jnp.int32)
    grid_spec = pltpu.PrefetchScalarGridSpec(
        num_scalar_prefetch=2,
        grid=(steps,),
        in_specs=[
            pl.BlockSpec((width, rows), lambda i, m, n: (0, 0)),
            pl.BlockSpec((width, span), lambda i, m, n: (2 * jnp.minimum(i, m[0]), 0)),
            pl.BlockSpec((width, span), lambda i, m, n: (2 * jnp.minimum(i, m[0]) + 1, 0)),
        ],
        out_specs=pl.BlockSpec((width, rows), lambda i, m, n: (0, 0)),
        scratch_shapes=[
            pltpu.VMEM((heads, 1, rows), jnp.float32),
            pltpu.VMEM((heads, 1, rows), jnp.float32),
            pltpu.VMEM((heads, width, rows), jnp.float32),
        ],
    )
    keys_total = steps * span
    result = pl.pallas_call(
        attention_kernel,
        grid_spec=grid_spec,
        out_shape=jax.ShapeDtypeStruct((width, rows), jnp.float32),
        compiler_params=pltpu.CompilerParams(dimension_semantics=("arbitrary",)),
        cost_estimate=pl.CostEstimate(
            flops=4 * heads * rows * keys_total * width,
            transcendentals=heads * rows * keys_total,
            bytes_accessed=key_value_all.size * 2 + 3 * query_flat.size * 2,
        ),
    )(meta, block_lengths, jnp.transpose(query_flat), key_value_all, key_value_all)
    return jnp.transpose(result).astype(jnp.bfloat16)


def shards(
    pixels,
    text_rows,
    patch_counts,
    picture_starts,
    block_lengths,
    vision_gain,
    vision_project,
    vision_output,
    merge_gain,
    merge_weight,
    text_gain,
    text_project,
    text_output,
):
    seq_ways = lax.axis_size("seq")
    tp_ways = lax.axis_size("tp")
    seq_index = lax.axis_index("seq")
    tp_index = lax.axis_index("tp")
    picture_total, local_patches, model_width = pixels.shape
    patch_total = local_patches * tp_ways
    local_width = vision_project.shape[2]
    head_count = local_width // HEAD
    patch_normed = layer_normed(pixels, vision_gain).astype(jnp.bfloat16)
    packed_project = vision_project.reshape(model_width, 3 * local_width)
    projected = jnp.einsum(
        "npd,de->npe",
        gathered_patches(patch_normed, 0),
        packed_project,
        preferred_element_type=jnp.float32,
    ).astype(jnp.bfloat16)
    queries = projected[..., :local_width].reshape(picture_total, patch_total, head_count, HEAD)
    key_heads = projected[..., local_width : 2 * local_width].reshape(
        picture_total, patch_total, head_count, HEAD
    )
    value_heads = projected[..., 2 * local_width :].reshape(
        picture_total, patch_total, head_count, HEAD
    )
    live_counts = lax.dynamic_slice_in_dim(
        patch_counts, seq_index * picture_total, picture_total, 0
    )
    score_scale = 1.0 / math.sqrt(HEAD)
    scores = (
        jnp.einsum("nqhd,nkhd->nhqk", queries, key_heads, preferred_element_type=jnp.float32)
        * score_scale
    )
    allowed = (jnp.arange(patch_total, dtype=jnp.int32)[None, :] < live_counts[:, None])[
        :, None, None, :
    ]
    scores = jnp.where(allowed, scores, MASKED_SCORE)
    highest = jnp.max(scores, -1, keepdims=True)
    weights = jnp.where(allowed, jnp.exp(scores - highest), 0.0)
    mixture = jnp.einsum(
        "nhqk,nkhd->nqhd",
        weights.astype(jnp.bfloat16),
        value_heads,
        preferred_element_type=jnp.float32,
    )
    mixture = mixture / jnp.transpose(jnp.sum(weights, -1), (0, 2, 1))[..., None]
    attended = mixture.astype(jnp.bfloat16).reshape(picture_total, patch_total, local_width)
    patch_major = jnp.transpose(attended, (1, 0, 2)).reshape(
        patch_total * picture_total, local_width
    )

    def vision_term(offset, row_count):
        return jnp.dot(patch_major, vision_output, preferred_element_type=jnp.float32)

    vision_sum = summed_rows(vision_term, local_patches * picture_total, 2)
    vision_sum = jnp.transpose(
        vision_sum.reshape(local_patches, picture_total, model_width), (1, 0, 2)
    )
    vision_rows = (pixels.astype(jnp.float32) + vision_sum).astype(jnp.bfloat16)
    merge_input = layer_normed(vision_rows, merge_gain).astype(jnp.bfloat16)
    merged_total = patch_total // 4
    input_share = merge_weight.shape[0]
    groups = input_share * tp_ways // model_width
    halves = tp_ways // groups
    outgoing = merge_input.reshape(
        picture_total, local_patches // groups, groups, halves, input_share
    )
    outgoing = jnp.transpose(outgoing, (2, 3, 0, 1, 4)).reshape(
        tp_ways, picture_total, local_patches // groups, input_share
    )
    incoming = tp_exchange(outgoing, tp_ways, False, 1)
    owned_inputs = jnp.transpose(incoming, (1, 0, 2, 3)).reshape(
        picture_total * merged_total, input_share
    )

    def merge_term(offset, row_count):
        return jnp.dot(owned_inputs, merge_weight, preferred_element_type=jnp.float32)

    part_rows = picture_total * merged_total // tp_ways
    visual_part = summed_rows(merge_term, part_rows, 3).astype(jnp.bfloat16)
    rows_per_block = text_rows.shape[0] * tp_ways
    start_table = picture_starts.reshape(seq_ways, picture_total)
    dest_table = start_table // rows_per_block
    picture_rank = tp_index * part_rows // merged_total
    rank_dest = jnp.sum(
        jnp.where(
            jnp.arange(picture_total, dtype=jnp.int32)[None, :] == picture_rank, dest_table, 0
        ),
        1,
    )
    senders = rank_dest == seq_index
    segment = seq_gathered(visual_part, seq_ways, (6, 7)).reshape(-1, model_width)
    row_count = segment.shape[0]
    sources = jnp.arange(row_count, dtype=jnp.int32) // part_rows
    wanted = jnp.any(
        (sources[:, None] == jnp.arange(seq_ways, dtype=jnp.int32)[None, :]) & senders[None, :], 1
    )
    selector = (
        (jnp.arange(row_count, dtype=jnp.int32) % part_rows)[None, :]
        == jnp.arange(part_rows, dtype=jnp.int32)[:, None]
    ) & wanted[None, :]
    arrived = jnp.dot(
        selector.astype(jnp.bfloat16), segment, preferred_element_type=jnp.float32
    ).astype(jnp.bfloat16)
    text_block = lax.all_gather(text_rows, "tp", axis=0, tiled=True)
    visual_block = tp_exchange(arrived, tp_ways, True, 5).reshape(-1, model_width)
    landed = dest_table == seq_index
    local_starts = jnp.sum(jnp.where(landed, start_table - seq_index * rows_per_block, 0), 0)
    live_groups = jnp.sum(
        jnp.where(landed, patch_counts.reshape(seq_ways, picture_total) // 4, 0), 0
    )
    slot_index = jnp.arange(merged_total, dtype=jnp.int32)
    targets = (local_starts[:, None] + slot_index[None, :]).reshape(-1)
    in_use = (slot_index[None, :] < live_groups[:, None]).reshape(-1)
    placement = (jnp.arange(rows_per_block, dtype=jnp.int32)[:, None] == targets[None, :]) & in_use[
        None, :
    ]
    covered = jnp.any(placement, 1)
    placed = jnp.dot(
        placement.astype(jnp.bfloat16), visual_block, preferred_element_type=jnp.float32
    ).astype(jnp.bfloat16)
    embedded = jnp.where(covered[:, None], placed, text_block)
    text_normed = rms_normed(embedded, text_gain).astype(jnp.bfloat16)
    text_heads = jnp.dot(
        text_normed,
        text_project.reshape(model_width, 3 * local_width),
        preferred_element_type=jnp.float32,
    )
    positions = seq_index * rows_per_block + jnp.arange(rows_per_block, dtype=jnp.int32)
    query_rows = rotary(
        text_heads[:, :local_width].reshape(rows_per_block, head_count, HEAD), positions
    ).astype(jnp.bfloat16)
    key_rows = rotary(
        text_heads[:, local_width : 2 * local_width].reshape(rows_per_block, head_count, HEAD),
        positions,
    ).astype(jnp.bfloat16)
    value_rows = text_heads[:, 2 * local_width :].astype(jnp.bfloat16)
    key_flat = key_rows.reshape(rows_per_block, local_width)
    kv_operand = jnp.concatenate([jnp.transpose(key_flat), jnp.transpose(value_rows)], 0)
    kv_operand, late_output = lax.optimization_barrier((kv_operand, text_output))
    full_output = tp_exchange(late_output, tp_ways, True, 8).reshape(-1, model_width)
    key_value_all = lax.all_gather(
        kv_operand,
        "seq",
        axis=0,
        tiled=True,
    )
    attended_rows = causal_attention(
        query_rows.reshape(rows_per_block, local_width),
        key_value_all,
        seq_index,
        block_lengths,
        rows_per_block,
    )
    own_rows = text_rows.shape[0]

    head_pieces = tp_exchange(
        attended_rows.reshape(tp_ways, own_rows, local_width), tp_ways, False, 4
    )
    mixed_rows = jnp.transpose(head_pieces, (1, 0, 2)).reshape(own_rows, tp_ways * local_width)
    text_sum = jnp.dot(mixed_rows, full_output, preferred_element_type=jnp.float32)
    residual = lax.dynamic_slice_in_dim(embedded, tp_index * own_rows, own_rows, 0)
    hidden = (residual.astype(jnp.float32) + text_sum).astype(jnp.bfloat16)
    return (hidden, key_flat, value_rows)


def solution(mesh):
    placed = (
        P("seq", "tp", None),
        P(("seq", "tp"), None),
        P(),
        P(),
        P(),
        P(),
        P(None, None, "tp"),
        P("tp", None),
        P(),
        P("tp", None),
        P(),
        P(None, None, "tp"),
        P("tp", None),
    )
    return jax.shard_map(
        shards,
        mesh=mesh,
        in_specs=placed,
        out_specs=(P(("seq", "tp"), None), P("seq", "tp"), P("seq", "tp")),
        check_vma=False,
    )
```

```python
import functools
import math

import jax
import jax.numpy as jnp
from jax import lax
from jax.experimental import pallas as pl
from jax.experimental.pallas import tpu as pltpu
from jax.sharding import PartitionSpec as P

HEAD = 104


LN_EPS = 1e-05
RMS_EPS = 1e-06
MASKED_SCORE = -1e30
KEY_SPAN = 512


def layer_normed(row_values, gain_vector):
    floats = row_values.astype(jnp.float32)
    centre = floats - jnp.mean(floats, -1, keepdims=True)
    spread = jnp.mean(centre * centre, -1, keepdims=True)
    return centre * lax.rsqrt(spread + LN_EPS) * gain_vector


def rms_normed(row_values, gain_vector):
    floats = row_values.astype(jnp.float32)
    return floats * lax.rsqrt(jnp.mean(floats * floats, -1, keepdims=True) + RMS_EPS) * gain_vector


def rotary(heads_in, positions):
    halfway = heads_in.shape[-1] // 2
    rates = 10000.0 ** (-2.0 * jnp.arange(halfway, dtype=jnp.float32) / heads_in.shape[-1])
    angles = positions.astype(jnp.float32)[:, None] * rates[None, :]
    cosine_table = jnp.cos(angles)[:, None, :]
    sine_table = jnp.sin(angles)[:, None, :]
    leading = heads_in[..., :halfway]
    trailing = heads_in[..., halfway:]
    return jnp.concatenate(
        [
            leading * cosine_table - trailing * sine_table,
            trailing * cosine_table + leading * sine_table,
        ],
        -1,
    )


MESH_IDS = pl.DeviceIdType.MESH


def exchange_kernel(axis, ways, stride, gather, x_ref, y_ref, send_sem, recv_sem, local_sem):
    position = lax.axis_index(axis)
    me = lax.rem(lax.div(position, stride), ways)
    base = position - me * stride
    other = lax.axis_index("seq" if axis == "tp" else "tp")

    def device(member):
        index = base + member * stride
        return (other, index) if axis == "tp" else (index, other)

    barrier = pltpu.get_barrier_semaphore()
    for shift in range(1, ways):
        peer = lax.rem(me + shift, ways)
        pl.semaphore_signal(barrier, inc=1, device_id=device(peer), device_id_type=MESH_IDS)
    pl.semaphore_wait(barrier, ways - 1)
    sends = []
    for shift in range(1, ways):
        peer = lax.rem(me + shift, ways)
        copy = pltpu.make_async_remote_copy(
            src_ref=x_ref if gather else x_ref.at[peer],
            dst_ref=y_ref.at[me],
            send_sem=send_sem.at[shift],
            recv_sem=recv_sem.at[shift],
            device_id=device(peer),
            device_id_type=MESH_IDS,
        )
        copy.start()
        sends.append(copy)
    local = pltpu.make_async_copy(x_ref if gather else x_ref.at[me], y_ref.at[me], local_sem)
    local.start()
    for copy in sends:
        copy.wait_send()
    for shift in range(1, ways):
        source = lax.rem(me + ways - shift, ways)
        arriving = pltpu.make_async_remote_copy(
            src_ref=x_ref if gather else x_ref.at[source],
            dst_ref=y_ref.at[source],
            send_sem=send_sem.at[shift],
            recv_sem=recv_sem.at[shift],
            device_id=device(source),
            device_id_type=MESH_IDS,
        )
        arriving.wait_recv()
    local.wait()


def tp_exchange(x, ways, gather, collective_id, axis="tp", stride=1):
    piece = x.shape if gather else x.shape[1:]
    return pl.pallas_call(
        functools.partial(exchange_kernel, axis, ways, stride, gather),
        out_shape=jax.ShapeDtypeStruct((ways,) + tuple(piece), x.dtype),
        in_specs=[pl.BlockSpec(memory_space=pl.ANY)],
        out_specs=pl.BlockSpec(memory_space=pl.ANY),
        scratch_shapes=[
            pltpu.SemaphoreType.DMA((ways,)),
            pltpu.SemaphoreType.DMA((ways,)),
            pltpu.SemaphoreType.DMA(()),
        ],
        compiler_params=pltpu.CompilerParams(collective_id=collective_id, has_side_effects=True),
    )(x)


def seq_gathered(piece, seq_ways, collective_ids):
    inner = math.gcd(seq_ways, 8)
    if seq_ways == inner:
        return tp_exchange(piece, inner, True, collective_ids[0], "seq", 1)
    far = tp_exchange(piece, seq_ways // inner, True, collective_ids[1], "seq", inner)
    near = tp_exchange(far, inner, True, collective_ids[0], "seq", 1)
    return jnp.swapaxes(near, 0, 1).reshape((seq_ways,) + piece.shape)


def summed_rows(term_task, own_rows, collective_id):
    ways = lax.axis_size("tp")
    partial = term_task(jnp.int32(0), own_rows * ways)
    pieces = partial.reshape((ways, own_rows) + partial.shape[1:]).astype(jnp.bfloat16)
    arrived = tp_exchange(pieces, ways, False, collective_id)
    return jnp.sum(arrived.astype(jnp.float32), 0)


def gathered_patches(piece, collective_id):
    ways = lax.axis_size("tp")
    whole = tp_exchange(piece, ways, True, collective_id)
    return jnp.transpose(whole, (1, 0, 2, 3)).reshape(
        (piece.shape[0], ways * piece.shape[1]) + piece.shape[2:]
    )


def attention_kernel(meta_ref, lengths_ref, qt_ref, k_ref, v_ref, o_ref, m_sc, l_sc, acc_sc):
    step = pl.program_id(0)
    seq = meta_ref[0]
    width, rows = qt_ref.shape
    span = k_ref.shape[1]
    heads = width // HEAD
    score_scale = 1.0 / math.sqrt(HEAD)

    @pl.when(step == 0)
    def _():
        m_sc[...] = jnp.full(m_sc.shape, MASKED_SCORE, jnp.float32)
        l_sc[...] = jnp.zeros(l_sc.shape, jnp.float32)
        acc_sc[...] = jnp.zeros(acc_sc.shape, jnp.float32)

    def update(diagonal):
        qt = qt_ref[...]
        k = k_ref[...]
        v = v_ref[...]
        feature = lax.broadcasted_iota(jnp.int32, (width, rows), 0)
        key_index = lax.broadcasted_iota(jnp.int32, (span, 1), 0)
        bias = jnp.where(key_index < lengths_ref[step], 0.0, MASKED_SCORE).astype(jnp.float32)
        if diagonal:
            causal = lax.broadcasted_iota(jnp.int32, (span, rows), 0) <= lax.broadcasted_iota(
                jnp.int32, (span, rows), 1
            )
        for h in range(heads):
            in_head = (feature >= h * HEAD) & (feature < (h + 1) * HEAD)
            qt_head = jnp.where(in_head, qt, jnp.zeros_like(qt))
            scores = (
                lax.dot_general(
                    k, qt_head, (((0,), (0,)), ((), ())), preferred_element_type=jnp.float32
                )
                * score_scale
                + bias
            )
            if diagonal:
                scores = jnp.where(causal, scores, MASKED_SCORE)
            m_prev = m_sc[h]
            m_new = jnp.maximum(m_prev, jnp.max(scores, axis=0, keepdims=True))
            weights = jnp.exp(scores - m_new)
            alpha = jnp.exp(m_prev - m_new)
            l_sc[h] = alpha * l_sc[h] + jnp.sum(weights, axis=0, keepdims=True)
            mixed = jnp.dot(v, weights.astype(jnp.bfloat16), preferred_element_type=jnp.float32)
            acc_sc[h] = acc_sc[h] * alpha + mixed
            m_sc[h] = m_new

    @pl.when(step < seq)
    def _():
        update(False)

    @pl.when(step == seq)
    def _():
        update(True)

    @pl.when(step == pl.num_programs(0) - 1)
    def _():
        feature = lax.broadcasted_iota(jnp.int32, (width, rows), 0)
        result = jnp.zeros((width, rows), jnp.float32)
        for h in range(heads):
            in_head = (feature >= h * HEAD) & (feature < (h + 1) * HEAD)
            result = jnp.where(in_head, acc_sc[h] / l_sc[h], result)
        o_ref[...] = result


def causal_attention(query_flat, key_value_all, seq_index, block_lengths, rows_per_block):
    rows, width = query_flat.shape
    span = rows_per_block
    steps = key_value_all.shape[0] // (2 * width)
    heads = width // HEAD
    meta = jnp.reshape(seq_index, (1,)).astype(jnp.int32)
    grid_spec = pltpu.PrefetchScalarGridSpec(
        num_scalar_prefetch=2,
        grid=(steps,),
        in_specs=[
            pl.BlockSpec((width, rows), lambda i, m, n: (0, 0)),
            pl.BlockSpec((width, span), lambda i, m, n: (2 * jnp.minimum(i, m[0]), 0)),
            pl.BlockSpec((width, span), lambda i, m, n: (2 * jnp.minimum(i, m[0]) + 1, 0)),
        ],
        out_specs=pl.BlockSpec((width, rows), lambda i, m, n: (0, 0)),
        scratch_shapes=[
            pltpu.VMEM((heads, 1, rows), jnp.float32),
            pltpu.VMEM((heads, 1, rows), jnp.float32),
            pltpu.VMEM((heads, width, rows), jnp.float32),
        ],
    )
    keys_total = steps * span
    result = pl.pallas_call(
        attention_kernel,
        grid_spec=grid_spec,
        out_shape=jax.ShapeDtypeStruct((width, rows), jnp.float32),
        compiler_params=pltpu.CompilerParams(dimension_semantics=("arbitrary",)),
        cost_estimate=pl.CostEstimate(
            flops=4 * heads * rows * keys_total * width,
            transcendentals=heads * rows * keys_total,
            bytes_accessed=key_value_all.size * 2 + 3 * query_flat.size * 2,
        ),
    )(meta, block_lengths, jnp.transpose(query_flat), key_value_all, key_value_all)
    return jnp.transpose(result).astype(jnp.bfloat16)


def shards(
    pixels,
    text_rows,
    patch_counts,
    picture_starts,
    block_lengths,
    vision_gain,
    vision_project,
    vision_output,
    merge_gain,
    merge_weight,
    text_gain,
    text_project,
    text_output,
):
    seq_ways = lax.axis_size("seq")
    tp_ways = lax.axis_size("tp")
    seq_index = lax.axis_index("seq")
    tp_index = lax.axis_index("tp")
    picture_total, local_patches, model_width = pixels.shape
    patch_total = local_patches * tp_ways
    local_width = vision_project.shape[2]
    head_count = local_width // HEAD
    patch_normed = layer_normed(pixels, vision_gain).astype(jnp.bfloat16)
    packed_project = vision_project.reshape(model_width, 3 * local_width)
    patch_rows = gathered_patches(patch_normed, 0)
    later_text, patch_rows = lax.optimization_barrier((text_rows, patch_rows))
    projected = jnp.einsum(
        "npd,de->npe",
        patch_rows,
        packed_project,
        preferred_element_type=jnp.float32,
    ).astype(jnp.bfloat16)
    queries = projected[..., :local_width].reshape(picture_total, patch_total, head_count, HEAD)
    key_heads = projected[..., local_width : 2 * local_width].reshape(
        picture_total, patch_total, head_count, HEAD
    )
    value_heads = projected[..., 2 * local_width :].reshape(
        picture_total, patch_total, head_count, HEAD
    )
    live_counts = lax.dynamic_slice_in_dim(
        patch_counts, seq_index * picture_total, picture_total, 0
    )
    score_scale = 1.0 / math.sqrt(HEAD)
    scores = (
        jnp.einsum("nqhd,nkhd->nhqk", queries, key_heads, preferred_element_type=jnp.float32)
        * score_scale
    )
    allowed = (jnp.arange(patch_total, dtype=jnp.int32)[None, :] < live_counts[:, None])[
        :, None, None, :
    ]
    scores = jnp.where(allowed, scores, MASKED_SCORE)
    highest = jnp.max(scores, -1, keepdims=True)
    weights = jnp.where(allowed, jnp.exp(scores - highest), 0.0)
    mixture = jnp.einsum(
        "nhqk,nkhd->nqhd",
        weights.astype(jnp.bfloat16),
        value_heads,
        preferred_element_type=jnp.float32,
    )
    mixture = mixture / jnp.transpose(jnp.sum(weights, -1), (0, 2, 1))[..., None]
    attended = mixture.astype(jnp.bfloat16).reshape(picture_total, patch_total, local_width)
    patch_major = jnp.transpose(attended, (1, 0, 2)).reshape(
        patch_total * picture_total, local_width
    )

    def vision_term(offset, row_count):
        return jnp.dot(patch_major, vision_output, preferred_element_type=jnp.float32)

    vision_sum = summed_rows(vision_term, local_patches * picture_total, 2)
    vision_sum = jnp.transpose(
        vision_sum.reshape(local_patches, picture_total, model_width), (1, 0, 2)
    )
    vision_rows = (pixels.astype(jnp.float32) + vision_sum).astype(jnp.bfloat16)
    merge_input = layer_normed(vision_rows, merge_gain).astype(jnp.bfloat16)
    merged_total = patch_total // 4
    input_share = merge_weight.shape[0]
    groups = input_share * tp_ways // model_width
    halves = tp_ways // groups
    outgoing = merge_input.reshape(
        picture_total, local_patches // groups, groups, halves, input_share
    )
    outgoing = jnp.transpose(outgoing, (2, 3, 0, 1, 4)).reshape(
        tp_ways, picture_total, local_patches // groups, input_share
    )
    incoming = tp_exchange(outgoing, tp_ways, False, 1)
    owned_inputs = jnp.transpose(incoming, (1, 0, 2, 3)).reshape(
        picture_total * merged_total, input_share
    )

    def merge_term(offset, row_count):
        return jnp.dot(owned_inputs, merge_weight, preferred_element_type=jnp.float32)

    part_rows = picture_total * merged_total // tp_ways
    visual_part = summed_rows(merge_term, part_rows, 3).astype(jnp.bfloat16)
    rows_per_block = text_rows.shape[0] * tp_ways
    start_table = picture_starts.reshape(seq_ways, picture_total)
    dest_table = start_table // rows_per_block
    picture_rank = tp_index * part_rows // merged_total
    rank_dest = jnp.sum(
        jnp.where(
            jnp.arange(picture_total, dtype=jnp.int32)[None, :] == picture_rank, dest_table, 0
        ),
        1,
    )
    senders = rank_dest == seq_index
    segment = seq_gathered(visual_part, seq_ways, (6, 7)).reshape(-1, model_width)
    row_count = segment.shape[0]
    sources = jnp.arange(row_count, dtype=jnp.int32) // part_rows
    wanted = jnp.any(
        (sources[:, None] == jnp.arange(seq_ways, dtype=jnp.int32)[None, :]) & senders[None, :], 1
    )
    selector = (
        (jnp.arange(row_count, dtype=jnp.int32) % part_rows)[None, :]
        == jnp.arange(part_rows, dtype=jnp.int32)[:, None]
    ) & wanted[None, :]
    arrived = jnp.dot(
        selector.astype(jnp.bfloat16), segment, preferred_element_type=jnp.float32
    ).astype(jnp.bfloat16)
    text_block = lax.all_gather(later_text, "tp", axis=0, tiled=True)
    visual_block = tp_exchange(arrived, tp_ways, True, 5).reshape(-1, model_width)
    landed = dest_table == seq_index
    local_starts = jnp.sum(jnp.where(landed, start_table - seq_index * rows_per_block, 0), 0)
    live_groups = jnp.sum(
        jnp.where(landed, patch_counts.reshape(seq_ways, picture_total) // 4, 0), 0
    )
    slot_index = jnp.arange(merged_total, dtype=jnp.int32)
    targets = (local_starts[:, None] + slot_index[None, :]).reshape(-1)
    in_use = (slot_index[None, :] < live_groups[:, None]).reshape(-1)
    placement = (jnp.arange(rows_per_block, dtype=jnp.int32)[:, None] == targets[None, :]) & in_use[
        None, :
    ]
    covered = jnp.any(placement, 1)
    placed = jnp.dot(
        placement.astype(jnp.bfloat16), visual_block, preferred_element_type=jnp.float32
    ).astype(jnp.bfloat16)
    embedded = jnp.where(covered[:, None], placed, text_block)
    text_normed = rms_normed(embedded, text_gain).astype(jnp.bfloat16)
    text_heads = jnp.dot(
        text_normed,
        text_project.reshape(model_width, 3 * local_width),
        preferred_element_type=jnp.float32,
    )
    positions = seq_index * rows_per_block + jnp.arange(rows_per_block, dtype=jnp.int32)
    query_rows = rotary(
        text_heads[:, :local_width].reshape(rows_per_block, head_count, HEAD), positions
    ).astype(jnp.bfloat16)
    key_rows = rotary(
        text_heads[:, local_width : 2 * local_width].reshape(rows_per_block, head_count, HEAD),
        positions,
    ).astype(jnp.bfloat16)
    value_rows = text_heads[:, 2 * local_width :].astype(jnp.bfloat16)
    key_flat = key_rows.reshape(rows_per_block, local_width)
    key_value_all = lax.all_gather(
        jnp.concatenate([jnp.transpose(key_flat), jnp.transpose(value_rows)], 0),
        "seq",
        axis=0,
        tiled=True,
    )
    attended_rows = causal_attention(
        query_rows.reshape(rows_per_block, local_width),
        key_value_all,
        seq_index,
        block_lengths,
        rows_per_block,
    )
    own_rows = text_rows.shape[0]

    full_output = lax.all_gather(text_output, "tp", axis=0, tiled=True)
    head_pieces = tp_exchange(
        attended_rows.reshape(tp_ways, own_rows, local_width), tp_ways, False, 4
    )
    mixed_rows = jnp.transpose(head_pieces, (1, 0, 2)).reshape(own_rows, tp_ways * local_width)
    text_sum = jnp.dot(mixed_rows, full_output, preferred_element_type=jnp.float32)
    residual = lax.dynamic_slice_in_dim(embedded, tp_index * own_rows, own_rows, 0)
    hidden = (residual.astype(jnp.float32) + text_sum).astype(jnp.bfloat16)
    return (hidden, key_flat, value_rows)


def solution(mesh):
    placed = (
        P("seq", "tp", None),
        P(("seq", "tp"), None),
        P(),
        P(),
        P(),
        P(),
        P(None, None, "tp"),
        P("tp", None),
        P(),
        P("tp", None),
        P(),
        P(None, None, "tp"),
        P("tp", None),
    )
    return jax.shard_map(
        shards,
        mesh=mesh,
        in_specs=placed,
        out_specs=(P(("seq", "tp"), None), P("seq", "tp"), P("seq", "tp")),
        check_vma=False,
    )
```

```python
import functools
import math

import jax
import jax.numpy as jnp
from jax import lax
from jax.experimental import pallas as pl
from jax.experimental.pallas import tpu as pltpu
from jax.sharding import PartitionSpec as P

HEAD = 104


LN_EPS = 1e-05
RMS_EPS = 1e-06
MASKED_SCORE = -1e30
KEY_SPAN = 512


def layer_normed(row_values, gain_vector):
    floats = row_values.astype(jnp.float32)
    centre = floats - jnp.mean(floats, -1, keepdims=True)
    spread = jnp.mean(centre * centre, -1, keepdims=True)
    return centre * lax.rsqrt(spread + LN_EPS) * gain_vector


def rms_normed(row_values, gain_vector):
    floats = row_values.astype(jnp.float32)
    return floats * lax.rsqrt(jnp.mean(floats * floats, -1, keepdims=True) + RMS_EPS) * gain_vector


def rotary(heads_in, positions):
    halfway = heads_in.shape[-1] // 2
    rates = 10000.0 ** (-2.0 * jnp.arange(halfway, dtype=jnp.float32) / heads_in.shape[-1])
    angles = positions.astype(jnp.float32)[:, None] * rates[None, :]
    cosine_table = jnp.cos(angles)[:, None, :]
    sine_table = jnp.sin(angles)[:, None, :]
    leading = heads_in[..., :halfway]
    trailing = heads_in[..., halfway:]
    return jnp.concatenate(
        [
            leading * cosine_table - trailing * sine_table,
            trailing * cosine_table + leading * sine_table,
        ],
        -1,
    )


MESH_IDS = pl.DeviceIdType.MESH


def exchange_kernel(axis, ways, stride, gather, x_ref, y_ref, send_sem, recv_sem, local_sem):
    position = lax.axis_index(axis)
    me = lax.rem(lax.div(position, stride), ways)
    base = position - me * stride
    other = lax.axis_index("seq" if axis == "tp" else "tp")

    def device(member):
        index = base + member * stride
        return (other, index) if axis == "tp" else (index, other)

    barrier = pltpu.get_barrier_semaphore()
    for shift in range(1, ways):
        peer = lax.rem(me + shift, ways)
        pl.semaphore_signal(barrier, inc=1, device_id=device(peer), device_id_type=MESH_IDS)
    pl.semaphore_wait(barrier, ways - 1)
    sends = []
    for shift in range(1, ways):
        peer = lax.rem(me + shift, ways)
        copy = pltpu.make_async_remote_copy(
            src_ref=x_ref if gather else x_ref.at[peer],
            dst_ref=y_ref.at[me],
            send_sem=send_sem.at[shift],
            recv_sem=recv_sem.at[shift],
            device_id=device(peer),
            device_id_type=MESH_IDS,
        )
        copy.start()
        sends.append(copy)
    local = pltpu.make_async_copy(x_ref if gather else x_ref.at[me], y_ref.at[me], local_sem)
    local.start()
    for copy in sends:
        copy.wait_send()
    for shift in range(1, ways):
        source = lax.rem(me + ways - shift, ways)
        arriving = pltpu.make_async_remote_copy(
            src_ref=x_ref if gather else x_ref.at[source],
            dst_ref=y_ref.at[source],
            send_sem=send_sem.at[shift],
            recv_sem=recv_sem.at[shift],
            device_id=device(source),
            device_id_type=MESH_IDS,
        )
        arriving.wait_recv()
    local.wait()


def tp_exchange(x, ways, gather, collective_id, axis="tp", stride=1):
    piece = x.shape if gather else x.shape[1:]
    return pl.pallas_call(
        functools.partial(exchange_kernel, axis, ways, stride, gather),
        out_shape=jax.ShapeDtypeStruct((ways,) + tuple(piece), x.dtype),
        in_specs=[pl.BlockSpec(memory_space=pl.ANY)],
        out_specs=pl.BlockSpec(memory_space=pl.ANY),
        scratch_shapes=[
            pltpu.SemaphoreType.DMA((ways,)),
            pltpu.SemaphoreType.DMA((ways,)),
            pltpu.SemaphoreType.DMA(()),
        ],
        compiler_params=pltpu.CompilerParams(collective_id=collective_id, has_side_effects=True),
    )(x)


def seq_gathered(piece, seq_ways, collective_ids):
    inner = math.gcd(seq_ways, 8)
    if seq_ways == inner:
        return tp_exchange(piece, inner, True, collective_ids[0], "seq", 1)
    far = tp_exchange(piece, seq_ways // inner, True, collective_ids[1], "seq", inner)
    near = tp_exchange(far, inner, True, collective_ids[0], "seq", 1)
    return jnp.swapaxes(near, 0, 1).reshape((seq_ways,) + piece.shape)


def summed_rows(term_task, own_rows, collective_id):
    ways = lax.axis_size("tp")
    partial = term_task(jnp.int32(0), own_rows * ways)
    pieces = partial.reshape((ways, own_rows) + partial.shape[1:]).astype(jnp.bfloat16)
    arrived = tp_exchange(pieces, ways, False, collective_id)
    return jnp.sum(arrived.astype(jnp.float32), 0)


def gathered_patches(piece, collective_id):
    ways = lax.axis_size("tp")
    whole = tp_exchange(piece, ways, True, collective_id)
    return jnp.transpose(whole, (1, 0, 2, 3)).reshape(
        (piece.shape[0], ways * piece.shape[1]) + piece.shape[2:]
    )


def attention_kernel(meta_ref, lengths_ref, qt_ref, k_ref, v_ref, o_ref, m_sc, l_sc, acc_sc):
    step = pl.program_id(0)
    seq = meta_ref[0]
    width, rows = qt_ref.shape
    span = k_ref.shape[1]
    heads = width // HEAD
    score_scale = 1.0 / math.sqrt(HEAD)

    @pl.when(step == 0)
    def _():
        m_sc[...] = jnp.full(m_sc.shape, MASKED_SCORE, jnp.float32)
        l_sc[...] = jnp.zeros(l_sc.shape, jnp.float32)
        acc_sc[...] = jnp.zeros(acc_sc.shape, jnp.float32)

    def update(diagonal):
        qt = qt_ref[...]
        k = k_ref[...]
        v = v_ref[...]
        feature = lax.broadcasted_iota(jnp.int32, (width, rows), 0)
        key_index = lax.broadcasted_iota(jnp.int32, (span, 1), 0)
        bias = jnp.where(key_index < lengths_ref[step], 0.0, MASKED_SCORE).astype(jnp.float32)
        if diagonal:
            causal = lax.broadcasted_iota(jnp.int32, (span, rows), 0) <= lax.broadcasted_iota(
                jnp.int32, (span, rows), 1
            )
        for h in range(heads):
            in_head = (feature >= h * HEAD) & (feature < (h + 1) * HEAD)
            qt_head = jnp.where(in_head, qt, jnp.zeros_like(qt))
            scores = (
                lax.dot_general(
                    k, qt_head, (((0,), (0,)), ((), ())), preferred_element_type=jnp.float32
                )
                * score_scale
                + bias
            )
            if diagonal:
                scores = jnp.where(causal, scores, MASKED_SCORE)
            m_prev = m_sc[h]
            m_new = jnp.maximum(m_prev, jnp.max(scores, axis=0, keepdims=True))
            weights = jnp.exp(scores - m_new)
            alpha = jnp.exp(m_prev - m_new)
            l_sc[h] = alpha * l_sc[h] + jnp.sum(weights, axis=0, keepdims=True)
            mixed = jnp.dot(v, weights.astype(jnp.bfloat16), preferred_element_type=jnp.float32)
            acc_sc[h] = acc_sc[h] * alpha + mixed
            m_sc[h] = m_new

    @pl.when(step < seq)
    def _():
        update(False)

    @pl.when(step == seq)
    def _():
        update(True)

    @pl.when(step == pl.num_programs(0) - 1)
    def _():
        feature = lax.broadcasted_iota(jnp.int32, (width, rows), 0)
        result = jnp.zeros((width, rows), jnp.float32)
        for h in range(heads):
            in_head = (feature >= h * HEAD) & (feature < (h + 1) * HEAD)
            result = jnp.where(in_head, acc_sc[h] / l_sc[h], result)
        o_ref[...] = result


def causal_attention(query_flat, key_value_all, seq_index, block_lengths, rows_per_block):
    rows, width = query_flat.shape
    span = rows_per_block
    steps = key_value_all.shape[0] // (2 * width)
    heads = width // HEAD
    meta = jnp.reshape(seq_index, (1,)).astype(jnp.int32)
    grid_spec = pltpu.PrefetchScalarGridSpec(
        num_scalar_prefetch=2,
        grid=(steps,),
        in_specs=[
            pl.BlockSpec((width, rows), lambda i, m, n: (0, 0)),
            pl.BlockSpec((width, span), lambda i, m, n: (2 * jnp.minimum(i, m[0]), 0)),
            pl.BlockSpec((width, span), lambda i, m, n: (2 * jnp.minimum(i, m[0]) + 1, 0)),
        ],
        out_specs=pl.BlockSpec((width, rows), lambda i, m, n: (0, 0)),
        scratch_shapes=[
            pltpu.VMEM((heads, 1, rows), jnp.float32),
            pltpu.VMEM((heads, 1, rows), jnp.float32),
            pltpu.VMEM((heads, width, rows), jnp.float32),
        ],
    )
    keys_total = steps * span
    result = pl.pallas_call(
        attention_kernel,
        grid_spec=grid_spec,
        out_shape=jax.ShapeDtypeStruct((width, rows), jnp.float32),
        compiler_params=pltpu.CompilerParams(dimension_semantics=("arbitrary",)),
        cost_estimate=pl.CostEstimate(
            flops=4 * heads * rows * keys_total * width,
            transcendentals=heads * rows * keys_total,
            bytes_accessed=key_value_all.size * 2 + 3 * query_flat.size * 2,
        ),
    )(meta, block_lengths, jnp.transpose(query_flat), key_value_all, key_value_all)
    return jnp.transpose(result).astype(jnp.bfloat16)


def shards(
    pixels,
    text_rows,
    patch_counts,
    picture_starts,
    block_lengths,
    vision_gain,
    vision_project,
    vision_output,
    merge_gain,
    merge_weight,
    text_gain,
    text_project,
    text_output,
):
    seq_ways = lax.axis_size("seq")
    tp_ways = lax.axis_size("tp")
    seq_index = lax.axis_index("seq")
    tp_index = lax.axis_index("tp")
    picture_total, local_patches, model_width = pixels.shape
    patch_total = local_patches * tp_ways
    local_width = vision_project.shape[2]
    head_count = local_width // HEAD
    patch_normed = layer_normed(pixels, vision_gain).astype(jnp.bfloat16)
    packed_project = vision_project.reshape(model_width, 3 * local_width)
    projected = jnp.einsum(
        "tnid,de->ntie",
        tp_exchange(patch_normed, tp_ways, True, 0),
        packed_project,
        preferred_element_type=jnp.float32,
    ).astype(jnp.bfloat16).reshape(picture_total, patch_total, 3 * local_width)
    queries = projected[..., :local_width].reshape(picture_total, patch_total, head_count, HEAD)
    key_heads = projected[..., local_width : 2 * local_width].reshape(
        picture_total, patch_total, head_count, HEAD
    )
    value_heads = projected[..., 2 * local_width :].reshape(
        picture_total, patch_total, head_count, HEAD
    )
    live_counts = lax.dynamic_slice_in_dim(
        patch_counts, seq_index * picture_total, picture_total, 0
    )
    score_scale = 1.0 / math.sqrt(HEAD)
    scores = (
        jnp.einsum("nqhd,nkhd->nhqk", queries, key_heads, preferred_element_type=jnp.float32)
        * score_scale
    )
    allowed = (jnp.arange(patch_total, dtype=jnp.int32)[None, :] < live_counts[:, None])[
        :, None, None, :
    ]
    scores = jnp.where(allowed, scores, MASKED_SCORE)
    highest = jnp.max(scores, -1, keepdims=True)
    weights = jnp.where(allowed, jnp.exp(scores - highest), 0.0)
    mixture = jnp.einsum(
        "nhqk,nkhd->nqhd",
        weights.astype(jnp.bfloat16),
        value_heads,
        preferred_element_type=jnp.float32,
    )
    mixture = mixture / jnp.transpose(jnp.sum(weights, -1), (0, 2, 1))[..., None]
    attended = mixture.astype(jnp.bfloat16).reshape(picture_total, patch_total, local_width)
    patch_major = jnp.transpose(attended, (1, 0, 2)).reshape(
        patch_total * picture_total, local_width
    )

    def vision_term(offset, row_count):
        return jnp.dot(patch_major, vision_output, preferred_element_type=jnp.float32)

    vision_sum = summed_rows(vision_term, local_patches * picture_total, 2)
    vision_sum = jnp.transpose(
        vision_sum.reshape(local_patches, picture_total, model_width), (1, 0, 2)
    )
    vision_rows = (pixels.astype(jnp.float32) + vision_sum).astype(jnp.bfloat16)
    merge_input = layer_normed(vision_rows, merge_gain).astype(jnp.bfloat16)
    merged_total = patch_total // 4
    input_share = merge_weight.shape[0]
    groups = input_share * tp_ways // model_width
    halves = tp_ways // groups
    outgoing = merge_input.reshape(
        picture_total, local_patches // groups, groups, halves, input_share
    )
    outgoing = jnp.transpose(outgoing, (2, 3, 0, 1, 4)).reshape(
        tp_ways, picture_total, local_patches // groups, input_share
    )
    incoming = tp_exchange(outgoing, tp_ways, False, 1)
    owned_inputs = jnp.transpose(incoming, (1, 0, 2, 3)).reshape(
        picture_total * merged_total, input_share
    )

    def merge_term(offset, row_count):
        return jnp.dot(owned_inputs, merge_weight, preferred_element_type=jnp.float32)

    part_rows = picture_total * merged_total // tp_ways
    visual_part = summed_rows(merge_term, part_rows, 3).astype(jnp.bfloat16)
    rows_per_block = text_rows.shape[0] * tp_ways
    start_table = picture_starts.reshape(seq_ways, picture_total)
    dest_table = start_table // rows_per_block
    picture_rank = tp_index * part_rows // merged_total
    rank_dest = jnp.sum(
        jnp.where(
            jnp.arange(picture_total, dtype=jnp.int32)[None, :] == picture_rank, dest_table, 0
        ),
        1,
    )
    senders = rank_dest == seq_index
    segment = seq_gathered(visual_part, seq_ways, (6, 7)).reshape(-1, model_width)
    row_count = segment.shape[0]
    sources = jnp.arange(row_count, dtype=jnp.int32) // part_rows
    wanted = jnp.any(
        (sources[:, None] == jnp.arange(seq_ways, dtype=jnp.int32)[None, :]) & senders[None, :], 1
    )
    selector = (
        (jnp.arange(row_count, dtype=jnp.int32) % part_rows)[None, :]
        == jnp.arange(part_rows, dtype=jnp.int32)[:, None]
    ) & wanted[None, :]
    arrived = jnp.dot(
        selector.astype(jnp.bfloat16), segment, preferred_element_type=jnp.float32
    ).astype(jnp.bfloat16)
    text_block = lax.all_gather(text_rows, "tp", axis=0, tiled=True)
    visual_block = tp_exchange(arrived, tp_ways, True, 5).reshape(-1, model_width)
    landed = dest_table == seq_index
    local_starts = jnp.sum(jnp.where(landed, start_table - seq_index * rows_per_block, 0), 0)
    live_groups = jnp.sum(
        jnp.where(landed, patch_counts.reshape(seq_ways, picture_total) // 4, 0), 0
    )
    slot_index = jnp.arange(merged_total, dtype=jnp.int32)
    targets = (local_starts[:, None] + slot_index[None, :]).reshape(-1)
    in_use = (slot_index[None, :] < live_groups[:, None]).reshape(-1)
    placement = (jnp.arange(rows_per_block, dtype=jnp.int32)[:, None] == targets[None, :]) & in_use[
        None, :
    ]
    covered = jnp.any(placement, 1)
    placed = jnp.dot(
        placement.astype(jnp.bfloat16), visual_block, preferred_element_type=jnp.float32
    ).astype(jnp.bfloat16)
    embedded = jnp.where(covered[:, None], placed, text_block)
    text_normed = rms_normed(embedded, text_gain).astype(jnp.bfloat16)
    text_heads = jnp.dot(
        text_normed,
        text_project.reshape(model_width, 3 * local_width),
        preferred_element_type=jnp.float32,
    )
    positions = seq_index * rows_per_block + jnp.arange(rows_per_block, dtype=jnp.int32)
    query_rows = rotary(
        text_heads[:, :local_width].reshape(rows_per_block, head_count, HEAD), positions
    ).astype(jnp.bfloat16)
    key_rows = rotary(
        text_heads[:, local_width : 2 * local_width].reshape(rows_per_block, head_count, HEAD),
        positions,
    ).astype(jnp.bfloat16)
    value_rows = text_heads[:, 2 * local_width :].astype(jnp.bfloat16)
    key_flat = key_rows.reshape(rows_per_block, local_width)
    key_value_all = lax.all_gather(
        jnp.concatenate([jnp.transpose(key_flat), jnp.transpose(value_rows)], 0),
        "seq",
        axis=0,
        tiled=True,
    )
    attended_rows = causal_attention(
        query_rows.reshape(rows_per_block, local_width),
        key_value_all,
        seq_index,
        block_lengths,
        rows_per_block,
    )
    own_rows = text_rows.shape[0]

    full_output = lax.all_gather(text_output, "tp", axis=0, tiled=True)
    head_pieces = tp_exchange(
        attended_rows.reshape(tp_ways, own_rows, local_width), tp_ways, False, 4
    )
    mixed_rows = jnp.transpose(head_pieces, (1, 0, 2)).reshape(own_rows, tp_ways * local_width)
    text_sum = jnp.dot(mixed_rows, full_output, preferred_element_type=jnp.float32)
    residual = lax.dynamic_slice_in_dim(embedded, tp_index * own_rows, own_rows, 0)
    hidden = (residual.astype(jnp.float32) + text_sum).astype(jnp.bfloat16)
    return (hidden, key_flat, value_rows)


def solution(mesh):
    placed = (
        P("seq", "tp", None),
        P(("seq", "tp"), None),
        P(),
        P(),
        P(),
        P(),
        P(None, None, "tp"),
        P("tp", None),
        P(),
        P("tp", None),
        P(),
        P(None, None, "tp"),
        P("tp", None),
    )
    return jax.shard_map(
        shards,
        mesh=mesh,
        in_specs=placed,
        out_specs=(P(("seq", "tp"), None), P("seq", "tp"), P("seq", "tp")),
        check_vma=False,
    )
```

```python
import functools
import math

import jax
import jax.numpy as jnp
from jax import lax
from jax.experimental import pallas as pl
from jax.experimental.pallas import tpu as pltpu
from jax.sharding import PartitionSpec as P

HEAD = 104


LN_EPS = 1e-05
RMS_EPS = 1e-06
MASKED_SCORE = -1e30
KEY_SPAN = 512


def layer_normed(row_values, gain_vector):
    floats = row_values.astype(jnp.float32)
    centre = floats - jnp.mean(floats, -1, keepdims=True)
    spread = jnp.mean(centre * centre, -1, keepdims=True)
    return centre * lax.rsqrt(spread + LN_EPS) * gain_vector


def rms_normed(row_values, gain_vector):
    floats = row_values.astype(jnp.float32)
    return floats * lax.rsqrt(jnp.mean(floats * floats, -1, keepdims=True) + RMS_EPS) * gain_vector


def rotary(heads_in, positions):
    halfway = heads_in.shape[-1] // 2
    rates = 10000.0 ** (-2.0 * jnp.arange(halfway, dtype=jnp.float32) / heads_in.shape[-1])
    angles = positions.astype(jnp.float32)[:, None] * rates[None, :]
    cosine_table = jnp.cos(angles)[:, None, :]
    sine_table = jnp.sin(angles)[:, None, :]
    leading = heads_in[..., :halfway]
    trailing = heads_in[..., halfway:]
    return jnp.concatenate(
        [
            leading * cosine_table - trailing * sine_table,
            trailing * cosine_table + leading * sine_table,
        ],
        -1,
    )


MESH_IDS = pl.DeviceIdType.MESH


def exchange_kernel(axis, ways, stride, gather, x_ref, y_ref, send_sem, recv_sem, local_sem):
    position = lax.axis_index(axis)
    me = lax.rem(lax.div(position, stride), ways)
    base = position - me * stride
    other = lax.axis_index("seq" if axis == "tp" else "tp")

    def device(member):
        index = base + member * stride
        return (other, index) if axis == "tp" else (index, other)

    barrier = pltpu.get_barrier_semaphore()
    for shift in range(1, ways):
        peer = lax.rem(me + shift, ways)
        pl.semaphore_signal(barrier, inc=1, device_id=device(peer), device_id_type=MESH_IDS)
    pl.semaphore_wait(barrier, ways - 1)
    sends = []
    for shift in range(1, ways):
        peer = lax.rem(me + shift, ways)
        copy = pltpu.make_async_remote_copy(
            src_ref=x_ref if gather else x_ref.at[peer],
            dst_ref=y_ref.at[me],
            send_sem=send_sem.at[shift],
            recv_sem=recv_sem.at[shift],
            device_id=device(peer),
            device_id_type=MESH_IDS,
        )
        copy.start()
        sends.append(copy)
    local = pltpu.make_async_copy(x_ref if gather else x_ref.at[me], y_ref.at[me], local_sem)
    local.start()
    for copy in sends:
        copy.wait_send()
    for shift in range(1, ways):
        source = lax.rem(me + ways - shift, ways)
        arriving = pltpu.make_async_remote_copy(
            src_ref=x_ref if gather else x_ref.at[source],
            dst_ref=y_ref.at[source],
            send_sem=send_sem.at[shift],
            recv_sem=recv_sem.at[shift],
            device_id=device(source),
            device_id_type=MESH_IDS,
        )
        arriving.wait_recv()
    local.wait()


def tp_exchange(x, ways, gather, collective_id, axis="tp", stride=1):
    piece = x.shape if gather else x.shape[1:]
    return pl.pallas_call(
        functools.partial(exchange_kernel, axis, ways, stride, gather),
        out_shape=jax.ShapeDtypeStruct((ways,) + tuple(piece), x.dtype),
        in_specs=[pl.BlockSpec(memory_space=pl.ANY)],
        out_specs=pl.BlockSpec(memory_space=pl.ANY),
        scratch_shapes=[
            pltpu.SemaphoreType.DMA((ways,)),
            pltpu.SemaphoreType.DMA((ways,)),
            pltpu.SemaphoreType.DMA(()),
        ],
        compiler_params=pltpu.CompilerParams(collective_id=collective_id, has_side_effects=True),
    )(x)


def seq_gathered(piece, seq_ways, collective_ids):
    inner = math.gcd(seq_ways, 8)
    if seq_ways == inner:
        return tp_exchange(piece, inner, True, collective_ids[0], "seq", 1)
    far = tp_exchange(piece, seq_ways // inner, True, collective_ids[1], "seq", inner)
    near = tp_exchange(far, inner, True, collective_ids[0], "seq", 1)
    return jnp.swapaxes(near, 0, 1).reshape((seq_ways,) + piece.shape)


def summed_rows(term_task, own_rows, collective_id):
    ways = lax.axis_size("tp")
    partial = term_task(jnp.int32(0), own_rows * ways)
    pieces = partial.reshape((ways, own_rows) + partial.shape[1:]).astype(jnp.bfloat16)
    arrived = tp_exchange(pieces, ways, False, collective_id)
    return jnp.sum(arrived.astype(jnp.float32), 0)


def gathered_patches(piece, collective_id):
    ways = lax.axis_size("tp")
    whole = tp_exchange(piece, ways, True, collective_id)
    return jnp.transpose(whole, (1, 0, 2, 3)).reshape(
        (piece.shape[0], ways * piece.shape[1]) + piece.shape[2:]
    )


def attention_kernel(meta_ref, lengths_ref, qt_ref, k_ref, v_ref, o_ref, m_sc, l_sc, acc_sc):
    step = pl.program_id(0)
    seq = meta_ref[0]
    width, rows = qt_ref.shape
    span = k_ref.shape[1]
    heads = width // HEAD
    score_scale = 1.0 / math.sqrt(HEAD)

    @pl.when(step == 0)
    def _():
        m_sc[...] = jnp.full(m_sc.shape, MASKED_SCORE, jnp.float32)
        l_sc[...] = jnp.zeros(l_sc.shape, jnp.float32)
        acc_sc[...] = jnp.zeros(acc_sc.shape, jnp.float32)

    def update(diagonal):
        qt = qt_ref[...]
        k = k_ref[...]
        v = v_ref[...]
        feature = lax.broadcasted_iota(jnp.int32, (width, rows), 0)
        key_index = lax.broadcasted_iota(jnp.int32, (span, 1), 0)
        bias = jnp.where(key_index < lengths_ref[step], 0.0, MASKED_SCORE).astype(jnp.float32)
        if diagonal:
            causal = lax.broadcasted_iota(jnp.int32, (span, rows), 0) <= lax.broadcasted_iota(
                jnp.int32, (span, rows), 1
            )
        for h in range(heads):
            in_head = (feature >= h * HEAD) & (feature < (h + 1) * HEAD)
            qt_head = jnp.where(in_head, qt, jnp.zeros_like(qt))
            scores = (
                lax.dot_general(
                    k, qt_head, (((0,), (0,)), ((), ())), preferred_element_type=jnp.float32
                )
                * score_scale
                + bias
            )
            if diagonal:
                scores = jnp.where(causal, scores, MASKED_SCORE)
            m_prev = m_sc[h]
            m_new = jnp.maximum(m_prev, jnp.max(scores, axis=0, keepdims=True))
            weights = jnp.exp(scores - m_new)
            alpha = jnp.exp(m_prev - m_new)
            l_sc[h] = alpha * l_sc[h] + jnp.sum(weights, axis=0, keepdims=True)
            mixed = jnp.dot(v, weights.astype(jnp.bfloat16), preferred_element_type=jnp.float32)
            acc_sc[h] = acc_sc[h] * alpha + mixed
            m_sc[h] = m_new

    @pl.when(step < seq)
    def _():
        update(False)

    @pl.when(step == seq)
    def _():
        update(True)

    @pl.when(step == pl.num_programs(0) - 1)
    def _():
        feature = lax.broadcasted_iota(jnp.int32, (width, rows), 0)
        result = jnp.zeros((width, rows), jnp.float32)
        for h in range(heads):
            in_head = (feature >= h * HEAD) & (feature < (h + 1) * HEAD)
            result = jnp.where(in_head, acc_sc[h] / l_sc[h], result)
        o_ref[...] = result.astype(o_ref.dtype)


def causal_attention(query_flat, key_value_all, seq_index, block_lengths, rows_per_block):
    rows, width = query_flat.shape
    span = rows_per_block
    steps = key_value_all.shape[0] // (2 * width)
    heads = width // HEAD
    meta = jnp.reshape(seq_index, (1,)).astype(jnp.int32)
    grid_spec = pltpu.PrefetchScalarGridSpec(
        num_scalar_prefetch=2,
        grid=(steps,),
        in_specs=[
            pl.BlockSpec((width, rows), lambda i, m, n: (0, 0)),
            pl.BlockSpec((width, span), lambda i, m, n: (2 * jnp.minimum(i, m[0]), 0)),
            pl.BlockSpec((width, span), lambda i, m, n: (2 * jnp.minimum(i, m[0]) + 1, 0)),
        ],
        out_specs=pl.BlockSpec((width, rows), lambda i, m, n: (0, 0)),
        scratch_shapes=[
            pltpu.VMEM((heads, 1, rows), jnp.float32),
            pltpu.VMEM((heads, 1, rows), jnp.float32),
            pltpu.VMEM((heads, width, rows), jnp.float32),
        ],
    )
    keys_total = steps * span
    result = pl.pallas_call(
        attention_kernel,
        grid_spec=grid_spec,
        out_shape=jax.ShapeDtypeStruct((width, rows), jnp.bfloat16),
        compiler_params=pltpu.CompilerParams(dimension_semantics=("arbitrary",)),
        cost_estimate=pl.CostEstimate(
            flops=4 * heads * rows * keys_total * width,
            transcendentals=heads * rows * keys_total,
            bytes_accessed=key_value_all.size * 2 + 3 * query_flat.size * 2,
        ),
    )(meta, block_lengths, jnp.transpose(query_flat), key_value_all, key_value_all)
    return jnp.transpose(result)


def shards(
    pixels,
    text_rows,
    patch_counts,
    picture_starts,
    block_lengths,
    vision_gain,
    vision_project,
    vision_output,
    merge_gain,
    merge_weight,
    text_gain,
    text_project,
    text_output,
):
    seq_ways = lax.axis_size("seq")
    tp_ways = lax.axis_size("tp")
    seq_index = lax.axis_index("seq")
    tp_index = lax.axis_index("tp")
    picture_total, local_patches, model_width = pixels.shape
    patch_total = local_patches * tp_ways
    local_width = vision_project.shape[2]
    head_count = local_width // HEAD
    patch_normed = layer_normed(pixels, vision_gain).astype(jnp.bfloat16)
    packed_project = vision_project.reshape(model_width, 3 * local_width)
    projected = jnp.einsum(
        "npd,de->npe",
        gathered_patches(patch_normed, 0),
        packed_project,
        preferred_element_type=jnp.float32,
    ).astype(jnp.bfloat16)
    queries = projected[..., :local_width].reshape(picture_total, patch_total, head_count, HEAD)
    key_heads = projected[..., local_width : 2 * local_width].reshape(
        picture_total, patch_total, head_count, HEAD
    )
    value_heads = projected[..., 2 * local_width :].reshape(
        picture_total, patch_total, head_count, HEAD
    )
    live_counts = lax.dynamic_slice_in_dim(
        patch_counts, seq_index * picture_total, picture_total, 0
    )
    score_scale = 1.0 / math.sqrt(HEAD)
    scores = (
        jnp.einsum("nqhd,nkhd->nhqk", queries, key_heads, preferred_element_type=jnp.float32)
        * score_scale
    )
    allowed = (jnp.arange(patch_total, dtype=jnp.int32)[None, :] < live_counts[:, None])[
        :, None, None, :
    ]
    scores = jnp.where(allowed, scores, MASKED_SCORE)
    highest = jnp.max(scores, -1, keepdims=True)
    weights = jnp.where(allowed, jnp.exp(scores - highest), 0.0)
    mixture = jnp.einsum(
        "nhqk,nkhd->nqhd",
        weights.astype(jnp.bfloat16),
        value_heads,
        preferred_element_type=jnp.float32,
    )
    mixture = mixture / jnp.transpose(jnp.sum(weights, -1), (0, 2, 1))[..., None]
    attended = mixture.astype(jnp.bfloat16).reshape(picture_total, patch_total, local_width)
    patch_major = jnp.transpose(attended, (1, 0, 2)).reshape(
        patch_total * picture_total, local_width
    )

    def vision_term(offset, row_count):
        return jnp.dot(patch_major, vision_output, preferred_element_type=jnp.float32)

    vision_sum = summed_rows(vision_term, local_patches * picture_total, 2)
    vision_sum = jnp.transpose(
        vision_sum.reshape(local_patches, picture_total, model_width), (1, 0, 2)
    )
    vision_rows = (pixels.astype(jnp.float32) + vision_sum).astype(jnp.bfloat16)
    merge_input = layer_normed(vision_rows, merge_gain).astype(jnp.bfloat16)
    merged_total = patch_total // 4
    input_share = merge_weight.shape[0]
    groups = input_share * tp_ways // model_width
    halves = tp_ways // groups
    outgoing = merge_input.reshape(
        picture_total, local_patches // groups, groups, halves, input_share
    )
    outgoing = jnp.transpose(outgoing, (2, 3, 0, 1, 4)).reshape(
        tp_ways, picture_total, local_patches // groups, input_share
    )
    incoming = tp_exchange(outgoing, tp_ways, False, 1)
    owned_inputs = jnp.transpose(incoming, (1, 0, 2, 3)).reshape(
        picture_total * merged_total, input_share
    )

    def merge_term(offset, row_count):
        return jnp.dot(owned_inputs, merge_weight, preferred_element_type=jnp.float32)

    part_rows = picture_total * merged_total // tp_ways
    visual_part = summed_rows(merge_term, part_rows, 3).astype(jnp.bfloat16)
    rows_per_block = text_rows.shape[0] * tp_ways
    start_table = picture_starts.reshape(seq_ways, picture_total)
    dest_table = start_table // rows_per_block
    picture_rank = tp_index * part_rows // merged_total
    rank_dest = jnp.sum(
        jnp.where(
            jnp.arange(picture_total, dtype=jnp.int32)[None, :] == picture_rank, dest_table, 0
        ),
        1,
    )
    senders = rank_dest == seq_index
    segment = seq_gathered(visual_part, seq_ways, (6, 7)).reshape(-1, model_width)
    row_count = segment.shape[0]
    sources = jnp.arange(row_count, dtype=jnp.int32) // part_rows
    wanted = jnp.any(
        (sources[:, None] == jnp.arange(seq_ways, dtype=jnp.int32)[None, :]) & senders[None, :], 1
    )
    selector = (
        (jnp.arange(row_count, dtype=jnp.int32) % part_rows)[None, :]
        == jnp.arange(part_rows, dtype=jnp.int32)[:, None]
    ) & wanted[None, :]
    arrived = jnp.dot(
        selector.astype(jnp.bfloat16), segment, preferred_element_type=jnp.float32
    ).astype(jnp.bfloat16)
    text_block = lax.all_gather(text_rows, "tp", axis=0, tiled=True)
    visual_block = tp_exchange(arrived, tp_ways, True, 5).reshape(-1, model_width)
    landed = dest_table == seq_index
    local_starts = jnp.sum(jnp.where(landed, start_table - seq_index * rows_per_block, 0), 0)
    live_groups = jnp.sum(
        jnp.where(landed, patch_counts.reshape(seq_ways, picture_total) // 4, 0), 0
    )
    slot_index = jnp.arange(merged_total, dtype=jnp.int32)
    targets = (local_starts[:, None] + slot_index[None, :]).reshape(-1)
    in_use = (slot_index[None, :] < live_groups[:, None]).reshape(-1)
    placement = (jnp.arange(rows_per_block, dtype=jnp.int32)[:, None] == targets[None, :]) & in_use[
        None, :
    ]
    covered = jnp.any(placement, 1)
    placed = jnp.dot(
        placement.astype(jnp.bfloat16), visual_block, preferred_element_type=jnp.float32
    ).astype(jnp.bfloat16)
    embedded = jnp.where(covered[:, None], placed, text_block)
    text_normed = rms_normed(embedded, text_gain).astype(jnp.bfloat16)
    text_heads = jnp.dot(
        text_normed,
        text_project.reshape(model_width, 3 * local_width),
        preferred_element_type=jnp.float32,
    )
    positions = seq_index * rows_per_block + jnp.arange(rows_per_block, dtype=jnp.int32)
    query_rows = rotary(
        text_heads[:, :local_width].reshape(rows_per_block, head_count, HEAD), positions
    ).astype(jnp.bfloat16)
    key_rows = rotary(
        text_heads[:, local_width : 2 * local_width].reshape(rows_per_block, head_count, HEAD),
        positions,
    ).astype(jnp.bfloat16)
    value_rows = text_heads[:, 2 * local_width :].astype(jnp.bfloat16)
    key_flat = key_rows.reshape(rows_per_block, local_width)
    key_value_all = lax.all_gather(
        jnp.concatenate([jnp.transpose(key_flat), jnp.transpose(value_rows)], 0),
        "seq",
        axis=0,
        tiled=True,
    )
    attended_rows = causal_attention(
        query_rows.reshape(rows_per_block, local_width),
        key_value_all,
        seq_index,
        block_lengths,
        rows_per_block,
    )
    own_rows = text_rows.shape[0]

    full_output = lax.all_gather(text_output, "tp", axis=0, tiled=True)
    head_pieces = tp_exchange(
        attended_rows.reshape(tp_ways, own_rows, local_width), tp_ways, False, 4
    )
    mixed_rows = jnp.transpose(head_pieces, (1, 0, 2)).reshape(own_rows, tp_ways * local_width)
    text_sum = jnp.dot(mixed_rows, full_output, preferred_element_type=jnp.float32)
    residual = lax.dynamic_slice_in_dim(embedded, tp_index * own_rows, own_rows, 0)
    hidden = (residual.astype(jnp.float32) + text_sum).astype(jnp.bfloat16)
    return (hidden, key_flat, value_rows)


def solution(mesh):
    placed = (
        P("seq", "tp", None),
        P(("seq", "tp"), None),
        P(),
        P(),
        P(),
        P(),
        P(None, None, "tp"),
        P("tp", None),
        P(),
        P("tp", None),
        P(),
        P(None, None, "tp"),
        P("tp", None),
    )
    return jax.shard_map(
        shards,
        mesh=mesh,
        in_specs=placed,
        out_specs=(P(("seq", "tp"), None), P("seq", "tp"), P("seq", "tp")),
        check_vma=False,
    )
```
